256 devices in a mesh: head: 16 (over z, core), tail: 16 (over y, x).
Axes of the slice: x: 4, y: 4, z: 8, core: 2. Of those that a mesh axis runs over, the one named last changes fastest.
Arguments:
- head_emb: bfloat16 [131072, 800], P(('head', 'tail')), may hold values from -48 to 48
- head_state: float32 [131072], P(('head', 'tail')), may hold values from 0.01 to 1
- tail_emb: bfloat16 [64, 128, 800], P('tail'), may hold values from -1.5 to 1.5
- tail_state: float32 [64, 128], P('tail'), may hold values from 0.01 to 1
- relation_emb: bfloat16 [1024, 800], replicated, may hold values from -3.5 to 3.5
- head_rows: int32 [1024, 256], P(('head', 'tail')), may hold values from 0 to 511
- relations: int32 [1024, 256], P(('head', 'tail')), may hold values from 0 to 1023
- tail_offsets: int32 [1024, 256], P(('head', 'tail')), may hold values from 0 to 127
- tail_owner: int32 [1024, 1], P(('head', 'tail')), may hold values from 0 to 15; in each aligned block of 4 rows (0 to 3, 4 to 7, ...) at most 2 rows name the same one
- tail_local: int32 [1024], P(('head', 'tail')), may hold values from 0 to 3
- block_count: int32 [256], P(('head', 'tail')), may hold values from 1 to 4, as said below
- neg_blocks: int32 [8], replicated, may hold values from 0 to 63, as said below
Outputs:
- head_new: bfloat16 [131072, 800], P(('head', 'tail'))
- head_state_new: float32 [131072], P(('head', 'tail'))
- tail_new: bfloat16 [64, 128, 800], P('tail')
- tail_state_new: float32 [64, 128], P('tail')
The draws below stay inside these ranges and needn't reach their ends.
Inputs may be any that keep to these rules, and one draw needn't show every extreme that they name: `tail_owner`: no tail index owns the tail blocks of more than 2 edge block slots of one device, and in some devices one owns exactly 2. `block_count`: some device has all 4 slots live. `neg_blocks`: distinct tail blocks; the last tail block is always among them.
All inputs are finite; a program needn't handle non-finite values.
Results may differ from the reference program's by a relative error of at most 0.0012.
The reference program's roundings to bfloat16 on the way (of `negatives`, `query`, `neg_grad` and `block_grad`) count: a program that leaves them out, or rounds other values in their place, can miss the bound.
Values may be sent and summed in bfloat16 or wider, within the bound.
A program may use at most 128 MiB of HBM per device.

```python
import math
import jax
import jax.numpy as jnp
import numpy as np
from jax import lax

EDGES = 256
TBS = 128
NEGB = 8
RELS = 1024
HROWS = 512
TB_DEV = 4
EB_DEV = 4
WIDTH = 800
NEG = 1024
DEVS = 256
CAP = 2
HEADS = 131072
TBLOCKS = 64
EBLOCKS = 1024
N_HEAD = 16
N_TAIL = 16


def draw_head_emb(key, part):
    values_drawn = jnp.clip(jax.random.normal(key, (HEADS, WIDTH), jnp.float32), -6.0, 6.0) * 0.25
    row_ids = jnp.arange(HEADS, dtype=jnp.int32)
    spiked_start = N_HEAD // 2 * N_TAIL * HROWS
    in_spike = (row_ids >= spiked_start) & (row_ids < spiked_start + N_TAIL * HROWS)
    values_drawn = values_drawn * jnp.where(in_spike, 32.0, 1.0)[:, None]
    values_drawn = jnp.clip(values_drawn, -48.0, 48.0)
    return values_drawn.astype(jnp.bfloat16)


def draw_block_count(key, part):
    halvings = jax.random.randint(key, (DEVS,), 0, 4)
    counts = jnp.maximum(EB_DEV // jnp.left_shift(jnp.ones((DEVS,), jnp.int32), halvings), 1)
    return counts.at[0].set(EB_DEV).astype(jnp.int32)


def draw_neg_blocks(key, part):
    others = jax.random.permutation(key, TBLOCKS - 1)[:NEGB - 1].astype(jnp.int32)
    chosen = jnp.concatenate([others, jnp.full((1,), TBLOCKS - 1, jnp.int32)])
    turn = jax.random.randint(jax.random.fold_in(key, 3), (), 0, NEGB)
    return jnp.roll(chosen, turn).astype(jnp.int32)


def with_ends(result, stream_key, low, top_value):
    longest = result.shape.index(max(result.shape))
    spots = []
    for shift in (0, 1):
        where = [jax.random.randint(jax.random.fold_in(stream_key, axis), (), 0, length) for axis, length in enumerate(result.shape)]
        where[longest] = (where[longest] + shift) % result.shape[longest]
        spots.append(tuple(where))
    return result.at[spots[0]].set(low).at[spots[1]].set(top_value)


def shard_levels(rng, dims, shards, low, high):
    def one(axis_at, parts):
        draws = jax.random.uniform(jax.random.fold_in(jax.random.fold_in(rng, 6), axis_at), (parts,), jnp.float32, low / len(shards), high / len(shards))
        return jnp.repeat(jnp.exp(draws), dims[axis_at] // parts).reshape((-1,) + (1,) * (len(dims) - axis_at - 1))

    factor_of = one(*shards[0])
    for cut in shards[1:]:
        factor_of = factor_of * one(*cut)
    return factor_of


def cumulative_ranks(number_of, skew):
    weights = [(1 << 20) // math.isqrt(rank ** skew) + 1 for rank in range(1, number_of + 1)]
    spread = 1 + sum(weights) // (1 << 30)
    return np.cumsum(np.array([max(1, weight // spread) for weight in weights]))


def skewed_ids(key, extent, amount, slope):
    grid = cumulative_ranks(amount, slope)
    lot = jax.random.randint(jax.random.fold_in(key, 1), extent, 0, int(grid[amount - 1]))
    standing = jnp.searchsorted(jnp.asarray(grid, jnp.int32), lot, side="right")
    return jax.random.permutation(jax.random.fold_in(key, 2), amount)[standing].astype(jnp.int32)


def deal_out(rng, own, number, rows, number_of, top, limit, skew):
    ranking = jax.random.permutation(rng, number_of)
    crowded, ordinary = portions_of(number_of, rows * top, limit, skew, True), portions_of(number_of, rows * top, limit, skew, False)
    places = jnp.arange(number_of)

    def named(lengths, rotation):
        used = int((lengths > 0).sum())
        fixed = max(1, used // 4)
        moved = fixed + (places - fixed + rotation * (used - fixed)) % max(1, number_of - fixed)
        return jnp.zeros((number_of,), jnp.int32).at[ranking[jnp.where(places < fixed, places, moved)]].set(jnp.asarray(lengths, jnp.int32))

    lengths = jnp.where(number % 4 == 0, named(crowded, number // 4), named(ordinary, number - number // 4 - 1))
    mixed = jax.random.permutation(jax.random.fold_in(own, 3), number_of)
    source_of, taker = mixed[0:number_of // 2 * 2:2], mixed[1:number_of // 2 * 2:2]
    room = jnp.minimum(lengths[source_of] - 1, limit - lengths[taker]) // 2
    room = jnp.where((source_of == ranking[0]) | (taker == ranking[0]) | (lengths[taker] == 0), 0, jnp.maximum(room, 0))
    moved = jax.random.randint(jax.random.fold_in(own, 4), (number_of // 2,), 0, 1 << 20) % (room + 1)
    lengths = lengths.at[source_of].add(-moved).at[taker].add(moved)
    members = jnp.searchsorted(jnp.cumsum(lengths), jnp.arange(rows * top), side="right").astype(jnp.int32)
    grid = members.reshape(top, rows).T
    grid = grid[jax.random.permutation(jax.random.fold_in(own, 1), rows)]
    rotation = jax.random.randint(jax.random.fold_in(own, 2), (rows, 1), 0, top)
    return jnp.take_along_axis(grid, (jnp.arange(top)[None, :] + rotation) % top, axis=1)


def portions_of(amount, total, limit, lean, full):
    weights = [(1 << 20) // math.isqrt(standing ** lean) + 1 for standing in range(1, amount + 1)]
    largest = limit if full else min(limit, max(-(-total // amount), total * weights[0] // sum(weights)))
    least = 1 if total - largest >= amount - 1 else 0
    holding, surplus = [largest] + [least] * (amount - 1), total - largest - least * (amount - 1)
    while surplus > 0:
        free = [i for i in range(1, amount) if holding[i] < largest] or [i for i in range(1, amount) if holding[i] < limit]
        whole, left = sum([weights[i] for i in free]), surplus
        for i in free:
            extra = min(limit - holding[i], max(1, left * weights[i] // whole), surplus)
            holding[i] = holding[i] + extra
            surplus = surplus - extra
    return np.array(holding)


def gaussian(key, shape, scale, limit, pieces=(), held_as=jnp.bfloat16):
    array = jax.random.normal(key, shape, jnp.float32) * scale
    if len(pieces) > 0:
        array = shard_levels(key, shape, pieces, -0.22, 0.18) * array
    return jnp.clip(array, min=-limit, max=limit).astype(held_as)


def setup_inputs(seed: int = 0) -> dict:
    key_list = jax.random.split(jax.random.key(seed), 13)
    head_emb = draw_head_emb(jax.random.fold_in(key_list[12], 71), 0)
    head_state = jnp.clip(jnp.exp(math.log(1.0) - 4.6051702 * jax.random.uniform(key_list[1], (HEADS,), jnp.float32) ** shard_levels(key_list[1], (HEADS,), ((0, 256),), -0.2, 0.2)), 0.01, 1.0)
    tail_emb = gaussian(key_list[2], (TBLOCKS, TBS, WIDTH), 0.25, 1.5, ((0, 16),))
    tail_state = jnp.clip(jnp.exp(math.log(1.0) - 4.6051702 * jax.random.uniform(key_list[3], (TBLOCKS, TBS), jnp.float32) ** shard_levels(key_list[3], (TBLOCKS, TBS), ((0, 16),), -0.2, 0.2)), 0.01, 1.0)
    relation_emb = gaussian(key_list[4], (RELS, WIDTH), 0.7, 3.5)
    head_rows = with_ends(jax.random.randint(key_list[5], (EBLOCKS, EDGES), 0, HROWS), jax.random.fold_in(key_list[5], 1), 0, HROWS - 1).astype(jnp.int32)
    relations = with_ends(skewed_ids(key_list[6], (EBLOCKS, EDGES), RELS, 2), jax.random.fold_in(key_list[6], 3), 0, RELS - 1).astype(jnp.int32)
    tail_offsets = with_ends(jax.random.randint(key_list[7], (EBLOCKS, EDGES), 0, TBS), jax.random.fold_in(key_list[7], 1), 0, TBS - 1).astype(jnp.int32)
    tail_owner_keys = jax.random.split(jax.random.fold_in(key_list[8], 1), EBLOCKS // EB_DEV)
    tail_owner_turns = jax.random.permutation(jax.random.fold_in(key_list[8], 3), EBLOCKS // EB_DEV)
    tail_owner = jax.vmap(lambda own, number: deal_out(jax.random.fold_in(key_list[8], 2), own, number, EB_DEV, N_TAIL, 1, CAP, 2))(tail_owner_keys, tail_owner_turns).reshape((EBLOCKS, 1))
    tail_local = with_ends(jax.random.randint(key_list[9], (EBLOCKS,), 0, TB_DEV), jax.random.fold_in(key_list[9], 1), 0, TB_DEV - 1).astype(jnp.int32)
    block_count = draw_block_count(jax.random.fold_in(key_list[12], 71), 0)
    neg_blocks = draw_neg_blocks(jax.random.fold_in(key_list[12], 71), 0)
    return {"head_emb": head_emb, "head_state": head_state, "tail_emb": tail_emb, "tail_state": tail_state, "relation_emb": relation_emb, "head_rows": head_rows, "relations": relations, "tail_offsets": tail_offsets, "tail_owner": tail_owner, "tail_local": tail_local, "block_count": block_count, "neg_blocks": neg_blocks}


LEARN_RATE = 0.3

def complex_product(left, right):
    half_width = left.shape[-1] // 2
    left_re, left_im = (left[..., :half_width], left[..., half_width:])
    right_re, right_im = (right[..., :half_width], right[..., half_width:])
    return jnp.concatenate([left_re * right_re - left_im * right_im, left_re * right_im + left_im * right_re], axis=-1)

def conj_product(left, right):
    half_width = left.shape[-1] // 2
    left_re, left_im = (left[..., :half_width], left[..., half_width:])
    right_re, right_im = (right[..., :half_width], right[..., half_width:])
    return jnp.concatenate([left_re * right_re + left_im * right_im, left_im * right_re - left_re * right_im], axis=-1)

def row_adagrad(embedding, adagrad_state, gradient):
    state_next = adagrad_state + lax.optimization_barrier(jnp.mean(gradient * gradient, axis=-1))
    updated = embedding.astype(jnp.float32) - LEARN_RATE * gradient / jnp.sqrt(state_next)[..., None]
    return (updated.astype(jnp.bfloat16), state_next)

def reference(head_emb, head_state, tail_emb, tail_state, relation_emb, head_rows, relations, tail_offsets, tail_owner, tail_local, block_count, neg_blocks):
    negatives = tail_emb[neg_blocks].reshape(NEG, WIDTH).astype(jnp.float32)
    global_block = (tail_owner[:, 0] * TB_DEV + tail_local).astype(jnp.int32).reshape(DEVS, EB_DEV)
    per_device = (head_emb.reshape(DEVS, HROWS, WIDTH), head_state.reshape(DEVS, HROWS), head_rows.reshape(DEVS, EB_DEV, EDGES), relations.reshape(DEVS, EB_DEV, EDGES), tail_offsets.reshape(DEVS, EB_DEV, EDGES), global_block, block_count)

    def one_device(totals, device_item):
        grad_table, neg_total = totals
        embedding, adagrad_state, row_ids, relation_ids, offset_ids, block_ids, live_count = device_item
        live_mask = jnp.repeat((jnp.arange(EB_DEV, dtype=jnp.int32) < live_count).astype(jnp.float32), EDGES)
        chosen = tail_emb[block_ids].reshape(EB_DEV * TBS, WIDTH)
        tail_index = (jnp.arange(EB_DEV, dtype=jnp.int32)[:, None] * TBS + offset_ids).reshape(-1).astype(jnp.int32)
        flat_rows = row_ids.reshape(-1).astype(jnp.int32)
        tail_vectors = chosen[tail_index].astype(jnp.float32)
        head_vectors = embedding[flat_rows].astype(jnp.float32)
        relation_vectors = relation_emb[relation_ids.reshape(-1)].astype(jnp.float32)
        query = complex_product(head_vectors, relation_vectors).astype(jnp.bfloat16)
        query = lax.optimization_barrier(query).astype(jnp.float32)
        positive = lax.optimization_barrier(jnp.sum(query * tail_vectors, axis=1))
        negative = jnp.dot(query, negatives.T, preferred_element_type=jnp.float32)
        largest = jnp.maximum(positive, lax.optimization_barrier(jnp.max(negative, axis=1)))
        pos_exp = jnp.exp(positive - largest)
        neg_exp = jnp.exp(negative - largest[:, None])
        denominator = pos_exp + lax.optimization_barrier(jnp.sum(neg_exp, axis=1))
        pos_grad = (pos_exp / denominator - 1.0) * live_mask
        neg_grad = (neg_exp / denominator[:, None] * live_mask[:, None]).astype(jnp.bfloat16)
        neg_grad = lax.optimization_barrier(neg_grad).astype(jnp.float32)
        query_grad = pos_grad[:, None] * tail_vectors + jnp.dot(neg_grad, negatives, preferred_element_type=jnp.float32)
        tail_part = pos_grad[:, None] * query
        neg_part = jnp.dot(neg_grad.T, query, preferred_element_type=jnp.float32)
        head_grad = jnp.zeros((HROWS, WIDTH), jnp.float32).at[flat_rows].add(conj_product(query_grad, relation_vectors))
        block_grad = jnp.zeros((EB_DEV * TBS, WIDTH), jnp.float32).at[tail_index].add(tail_part).astype(jnp.bfloat16)
        block_grad = lax.optimization_barrier(block_grad).astype(jnp.float32)
        grad_table = grad_table.at[block_ids].add(block_grad.reshape(EB_DEV, TBS, WIDTH))
        head_updated, state_updated = row_adagrad(embedding, adagrad_state, head_grad)
        return ((grad_table, neg_total + neg_part), (head_updated, state_updated))
    initial = (jnp.zeros((TBLOCKS, TBS, WIDTH), jnp.float32), jnp.zeros((NEG, WIDTH), jnp.float32))
    (grad_table, neg_total), (head_updated, state_updated) = lax.scan(one_device, initial, per_device)
    grad_table = grad_table.at[neg_blocks].add(neg_total.reshape(NEGB, TBS, WIDTH))
    tail_updated, tail_state_updated = row_adagrad(tail_emb, tail_state, grad_table)
    return (head_updated.reshape(HEADS, WIDTH), state_updated.reshape(HEADS), tail_updated, tail_state_updated)
```

```python
import jax
import jax.numpy as jnp
from jax import lax
from jax.experimental import pallas as pl
from jax.experimental.pallas import tpu as pltpu
from jax.sharding import PartitionSpec as P

LEARN_RATE = 0.3
MESH = pl.DeviceIdType.MESH
F32 = jnp.float32
BF16 = jnp.bfloat16
SIDE = 4
DEPTH = 8
HEAD = 16
TAIL = 16


def greet(targets):
    barrier = pltpu.get_barrier_semaphore()
    for target in targets:
        pl.semaphore_signal(barrier, inc=1, device_id=target, device_id_type=MESH)
    pl.semaphore_wait(barrier, len(targets))


def table_gather(own, table, send1, recv1, send2, recv2, send3, recv3, local):
    head, tail = lax.axis_index("head"), lax.axis_index("tail")
    core, col, row = lax.rem(head, 2), lax.rem(tail, SIDE), lax.div(tail, SIDE)
    sibling = (head + 1 - 2 * core, tail)
    half = own.shape[1] // 2
    everything = (0, own.shape[1])
    first, second = (0, half), (half, half)

    def place(which, along, across):
        dx, dy = (along, across) if which == 0 else (across, along)
        return lax.rem(row + dy + SIDE, SIDE) * SIDE + lax.rem(col + dx + SIDE, SIDE)

    greet(
        [sibling]
        + [(head, place(0, 1, 0)), (head, place(0, -1, 0))]
        + [(head, place(1, 1, 0)), (head, place(1, -1, 0))]
    )

    def copy(which, origin, part, sems, spot, target):
        block = 2 * core + which
        start, size = part
        here = table.at[place(which, *origin), block, pl.ds(start, size)]
        source = own.at[block, pl.ds(start, size)] if origin == (0, 0) else here
        return pltpu.make_async_remote_copy(
            src_ref=source,
            dst_ref=here,
            send_sem=sems[0].at[which, spot],
            recv_sem=sems[1].at[which, spot],
            device_id=target,
            device_id_type=MESH,
        )

    def landing(which, origin, part, sems, spot):
        block = 2 * core + which
        start, size = part
        here = table.at[place(which, *origin), block, pl.ds(start, size)]
        return pltpu.make_async_remote_copy(
            src_ref=here,
            dst_ref=here,
            send_sem=sems[0].at[which, spot],
            recv_sem=sems[1].at[which, spot],
            device_id=sibling,
            device_id_type=MESH,
        )

    stage1, stage2, stage3 = (send1, recv1), (send2, recv2), (send3, recv3)
    sent = []

    def send(*description):
        transfer = copy(*description)
        transfer.start()
        sent.append(transfer)

    def spread(which, origin):
        spot = (origin[0] % SIDE) * 4
        send(which, origin, everything, stage2, spot, (head, place(which, 0, 1)))
        send(which, origin, everything, stage2, spot + 1, (head, place(which, 0, -1)))

    def share(which, origin):
        spot = (origin[0] % SIDE) * 4 + origin[1] % SIDE
        send(which, origin, everything, stage3, spot, sibling)

    for which in (0, 1):
        send(which, (0, 0), everything, stage1, 0, (head, place(which, 1, 0)))
        send(which, (0, 0), everything, stage1, 1, (head, place(which, -1, 0)))
    keep = pltpu.make_async_copy(own, table.at[tail], local)
    keep.start()
    for which in (0, 1):
        spread(which, (0, 0))
    for which in (0, 1):
        landing(which, (-1, 0), everything, stage1, 0).wait_recv()
        send(which, (-1, 0), first, stage1, 2, (head, place(which, 1, 0)))
        spread(which, (-1, 0))
        share(which, (-1, 0))
        landing(which, (1, 0), everything, stage1, 1).wait_recv()
        send(which, (1, 0), second, stage1, 3, (head, place(which, -1, 0)))
        spread(which, (1, 0))
        share(which, (1, 0))
    for which in (0, 1):
        landing(which, (2, 0), first, stage1, 2).wait_recv()
        landing(which, (2, 0), second, stage1, 3).wait_recv()
        spread(which, (2, 0))
        share(which, (2, 0))
    for along in (0, -1, 1, 2):
        spot = (along % SIDE) * 4
        for which in (0, 1):
            landing(which, (along, -1), everything, stage2, spot).wait_recv()
            send(which, (along, -1), first, stage2, spot + 2, (head, place(which, 0, 1)))
            share(which, (along, -1))
            landing(which, (along, 1), everything, stage2, spot + 1).wait_recv()
            send(which, (along, 1), second, stage2, spot + 3, (head, place(which, 0, -1)))
            share(which, (along, 1))
    for along in (0, -1, 1, 2):
        spot = (along % SIDE) * 4
        for which in (0, 1):
            landing(which, (along, 2), first, stage2, spot + 2).wait_recv()
            landing(which, (along, 2), second, stage2, spot + 3).wait_recv()
            share(which, (along, 2))
    for which in (0, 1):
        for along in range(SIDE):
            for across in range(SIDE):
                if (along, across) != (0, 0):
                    block = 2 * (1 - core) + which
                    here = table.at[place(which, along, across), block]
                    pltpu.make_async_remote_copy(
                        src_ref=here,
                        dst_ref=here,
                        send_sem=send3.at[which, along * 4 + across],
                        recv_sem=recv3.at[which, along * 4 + across],
                        device_id=sibling,
                        device_id_type=MESH,
                    ).wait_recv()
    keep.wait()
    for transfer in sent:
        transfer.wait_send()


def gather_table(tail_emb):
    shape = (TAIL,) + tail_emb.shape
    sems = pltpu.SemaphoreType.DMA
    return pl.pallas_call(
        table_gather,
        out_shape=jax.ShapeDtypeStruct(shape, tail_emb.dtype),
        in_specs=[pl.BlockSpec(memory_space=pl.ANY)],
        out_specs=pl.BlockSpec(memory_space=pl.ANY),
        scratch_shapes=[
            sems((2, 4)),
            sems((2, 4)),
            sems((2, 16)),
            sems((2, 16)),
            sems((2, 16)),
            sems((2, 16)),
            sems(()),
        ],
        compiler_params=pltpu.CompilerParams(collective_id=0, has_side_effects=True),
    )(tail_emb)


TN = (((0,), (0,)), ((), ()))
NT = (((1,), (1,)), ((), ()))


def mm(left, right, dims=(((1,), (0,)), ((), ()))):
    return lax.dot_general(left, right, dims, preferred_element_type=F32)


def one_hot(count, index_row):
    spots = lax.broadcasted_iota(jnp.int32, (count, index_row.shape[1]), 0)
    return jnp.where(spots == index_row, 1.0, 0.0).astype(BF16)


def edge_work(
    block_ids,
    neg_ids,
    live_count,
    table,
    head_emb,
    head_state,
    relation_emb,
    head_rows,
    relations,
    offsets,
    head_new,
    state_new,
    block_out,
    neg_out,
    chosen,
    negs,
    head_t,
    rel_t,
    neg_t,
    query_all,
    prob_all,
    grad_hi,
    grad_lo,
    sems,
):
    blocks, edges = head_rows.shape
    rows, width = head_emb.shape
    half = width // 2
    span = chosen.shape[1]
    neg_count = negs.shape[0]

    fetches = []
    for k in range(neg_count):
        fetches.append(pltpu.make_async_copy(table.at[neg_ids[k]], negs.at[k], sems.at[k]))
    for b in range(blocks):
        fetches.append(
            pltpu.make_async_copy(table.at[block_ids[b]], chosen.at[b], sems.at[neg_count + b])
        )
    for fetch in fetches:
        fetch.start()
    head_t[...] = head_emb[...].T
    rel_t[...] = relation_emb[...].T
    for fetch in fetches:
        fetch.wait()
    for k in range(neg_count):
        neg_t[:, k * span : (k + 1) * span] = negs[k].T

    def one_block(b, carry):
        lanes = pl.ds(pl.multiple_of(b * edges, edges), edges)
        live = jnp.where(b < live_count[0], 1.0, 0.0).astype(F32)
        pick = one_hot(span, offsets[pl.ds(b, 1), :])
        head_vec = mm(head_t[...], one_hot(rows, head_rows[pl.ds(b, 1), :]))
        rel_vec = mm(rel_t[...], one_hot(rel_t.shape[1], relations[pl.ds(b, 1), :]))
        tail_vec = mm(chosen[b], pick, TN)
        hr, hi = head_vec[:half], head_vec[half:]
        rr, ri = rel_vec[:half], rel_vec[half:]
        query = jnp.concatenate([hr * rr - hi * ri, hr * ri + hi * rr], axis=0).astype(BF16)
        query_all[:, lanes] = query
        query = query.astype(F32)
        positive = jnp.sum(query * tail_vec, axis=0, keepdims=True)
        score = mm(negs[...].reshape(neg_count * span, width), query_all[:, lanes])
        largest = jnp.maximum(positive, jnp.max(score, axis=0, keepdims=True))
        pos_exp = jnp.exp(positive - largest)
        neg_exp = jnp.exp(score - largest)
        denominator = pos_exp + jnp.sum(neg_exp, axis=0, keepdims=True)
        pos_grad = (pos_exp / denominator - 1.0) * live
        prob_all[:, lanes] = (neg_exp * (live / denominator)).astype(BF16)
        query_grad = pos_grad * tail_vec + mm(neg_t[...], prob_all[:, lanes])
        part = pos_grad * query
        part_a = part.astype(BF16)
        rest = part - part_a.astype(F32)
        part_b = rest.astype(BF16)
        part_c = (rest - part_b.astype(F32)).astype(BF16)
        block_grad = mm(pick, part_a, NT) + (mm(pick, part_b, NT) + mm(pick, part_c, NT))
        for i in range(HEAD):
            block_out[i, b] = block_grad[i * 8 : (i + 1) * 8].astype(BF16)
        qr, qi = query_grad[:half], query_grad[half:]
        change = jnp.concatenate([qr * rr + qi * ri, qi * rr - qr * ri], axis=0)
        change_hi = change.astype(BF16)
        grad_hi[:, lanes] = change_hi
        grad_lo[:, lanes] = (change - change_hi.astype(F32)).astype(BF16)
        return carry

    lax.fori_loop(0, blocks, one_block, 0)

    def neg_rows(k, carry):
        span_rows = pl.ds(pl.multiple_of(k * 256, 256), 256)
        neg_out[span_rows, :] = mm(prob_all[span_rows, :], query_all[...], NT)
        return carry

    lax.fori_loop(0, neg_count * span // 256, neg_rows, 0)

    diagonal = lax.broadcasted_iota(jnp.int32, (128, 128), 0) == lax.broadcasted_iota(
        jnp.int32, (128, 128), 1
    )
    for part in range(rows // 128):
        span_rows = pl.ds(part * 128, 128)
        spots = lax.broadcasted_iota(jnp.int32, (128, edges), 0) + part * 128
        gradient = jnp.zeros((128, width), F32)
        for b in range(blocks):
            hot = jnp.where(spots == head_rows[b : b + 1, :], 1.0, 0.0).astype(BF16)
            lanes = pl.ds(b * edges, edges)
            gradient += mm(hot, grad_hi[:, lanes], NT) + mm(hot, grad_lo[:, lanes], NT)
        state_row = head_state[:, span_rows]
        state_column = jnp.sum(jnp.where(diagonal, state_row, 0.0), axis=1, keepdims=True)
        state_next = state_column + jnp.sum(gradient * gradient, axis=1, keepdims=True) / width
        head_new[span_rows, :] = (
            head_emb[span_rows, :].astype(F32) - gradient * (LEARN_RATE / jnp.sqrt(state_next))
        ).astype(BF16)
        state_new[:, span_rows] = jnp.sum(
            jnp.where(diagonal, state_next, 0.0), axis=0, keepdims=True
        )


def run_edges(
    block_ids,
    neg_ids,
    live_count,
    table,
    head_emb,
    head_state,
    relation_emb,
    head_rows,
    relations,
    offsets,
):
    blocks, edges = head_rows.shape
    rows, width = head_emb.shape
    span = table.shape[1]
    negs = neg_ids.shape[0]
    total = blocks * edges
    smem = pl.BlockSpec(memory_space=pltpu.SMEM)
    vmem = pl.BlockSpec(memory_space=pltpu.VMEM)
    rels = relation_emb.shape[0]
    return pl.pallas_call(
        edge_work,
        out_shape=(
            jax.ShapeDtypeStruct((rows, width), BF16),
            jax.ShapeDtypeStruct((1, rows), F32),
            jax.ShapeDtypeStruct((HEAD, blocks, span // HEAD, width), BF16),
            jax.ShapeDtypeStruct((negs * span, width), F32),
        ),
        in_specs=[smem, smem, smem, pl.BlockSpec(memory_space=pl.ANY)] + [vmem] * 6,
        out_specs=(vmem, vmem, vmem, vmem),
        scratch_shapes=[
            pltpu.VMEM((blocks, span, width), BF16),
            pltpu.VMEM((negs, span, width), BF16),
            pltpu.VMEM((width, rows), BF16),
            pltpu.VMEM((width, rels), BF16),
            pltpu.VMEM((width, negs * span), BF16),
            pltpu.VMEM((width, total), BF16),
            pltpu.VMEM((negs * span, total), BF16),
            pltpu.VMEM((width, total), BF16),
            pltpu.VMEM((width, total), BF16),
            pltpu.SemaphoreType.DMA((blocks + negs,)),
        ],
        compiler_params=pltpu.CompilerParams(vmem_limit_bytes=56 << 20),
    )(
        block_ids,
        neg_ids,
        live_count,
        table,
        head_emb,
        head_state,
        relation_emb,
        head_rows,
        relations,
        offsets,
    )


def exchange(
    neg_ids,
    block_part,
    places,
    neg_part,
    own_rows,
    own_state,
    out,
    state_out,
    slots,
    seats,
    theirs,
    mine,
    planes,
    deep,
    deep_in,
    neg_total,
    slot_rows,
    dense,
    dense_in,
    rows_now,
    update,
    state_next,
    sem_bs,
    sem_br,
    sem_is,
    sem_ir,
    sem_cs,
    sem_cr,
    sem_cl,
    sem_ps,
    sem_pr,
    sem_zs,
    sem_zr,
    sem_ds,
    sem_dr,
    sem_ns,
    sem_nr,
    sem_us,
    sem_ur,
    sem_ws,
    sem_wr,
    sem_fs,
    sem_fr,
    sem_gs,
    sem_gr,
    sem_local,
):
    head, tail = lax.axis_index("head"), lax.axis_index("tail")
    core, depth = lax.rem(head, 2), lax.div(head, 2)
    other = head + 1 - 2 * core
    owned = own_rows.shape[0]
    quarter = DEPTH // 2
    width = own_rows.shape[-1]

    def around(index, step, count):
        return lax.rem(index + step, count)

    def remote(source, target, send_sem, recv_sem, device):
        return pltpu.make_async_remote_copy(
            src_ref=source,
            dst_ref=target,
            send_sem=send_sem,
            recv_sem=recv_sem,
            device_id=device,
            device_id_type=MESH,
        )

    barrier = pltpu.get_barrier_semaphore()

    @pl.loop(1, HEAD)
    def _(step):
        pl.semaphore_signal(
            barrier, inc=1, device_id=(around(head, step, HEAD), tail), device_id_type=MESH
        )
        pl.semaphore_signal(
            barrier, inc=1, device_id=(head, around(tail, step, TAIL)), device_id_type=MESH
        )

    pl.semaphore_wait(barrier, HEAD + TAIL - 2)

    def chunk(peer, side):
        return neg_part.at[lax.div(peer, 2), pl.ds(lax.rem(peer, 2) * quarter, quarter), side]

    def pair_copy(step):
        peer = around(tail, step, TAIL)
        return remote(
            chunk(peer, 1 - core), theirs.at[peer], sem_cs.at[step], sem_cr.at[step], (other, tail)
        )

    def pair_local(step):
        peer = around(tail, step, TAIL)
        return pltpu.make_async_copy(chunk(peer, core), mine.at[peer], sem_cl.at[step])

    @pl.loop(0, TAIL)
    def _(step):
        pair_copy(step).start()
        pair_local(step).start()

    def block_copy(step):
        return remote(
            block_part.at[around(head, step, HEAD)],
            slots.at[head],
            sem_bs.at[step],
            sem_br.at[step],
            (around(head, step, HEAD), tail),
        )

    def seat_copy(step):
        return remote(
            places,
            seats.at[head],
            sem_is.at[step],
            sem_ir.at[step],
            (around(head, step, HEAD), tail),
        )

    @pl.loop(1, HEAD)
    def _(step):
        block_copy(step).start()
        seat_copy(step).start()

    keep_block = pltpu.make_async_copy(block_part.at[head], slots.at[head], sem_local.at[0])
    keep_block.start()
    keep_rows = pltpu.make_async_copy(own_rows.at[:, head], rows_now, sem_local.at[1])
    keep_rows.start()
    seats[head] = places[...]

    def plane_copy(step):
        peer = around(tail, step, TAIL)
        return remote(
            mine.at[peer], planes.at[tail], sem_ps.at[step], sem_pr.at[step], (head, peer)
        )

    @pl.loop(1, TAIL)
    def _(step):
        peer = around(tail, step, TAIL)
        pair_copy(step).wait_recv()
        pair_local(step).wait()
        mine[peer] = mine[peer] + theirs[peer]
        plane_copy(step).start()

    pair_copy(0).wait_recv()
    pair_local(0).wait()
    planes[tail] = mine[tail] + theirs[tail]

    @pl.loop(1, HEAD)
    def _(step):
        block_copy(step).wait_recv()
        seat_copy(step).wait_recv()

    keep_block.wait()

    @pl.loop(0, HEAD)
    def _(source):
        for b in range(owned):
            slot_rows[pl.ds(pl.multiple_of(source * owned * 8 + b * 8, 8), 8), :] = slots[
                source, b
            ].astype(F32)

    seat_row = jnp.concatenate(
        [
            seats[4 * q, 0:1] + seats[4 * q + 1, 0:1] + seats[4 * q + 2, 0:1] + seats[4 * q + 3, 0:1]
            for q in range(HEAD // 4)
        ],
        axis=1,
    )
    hot = one_hot(TAIL * owned * 8, seat_row)
    dense[...] = mm(hot, slot_rows[...].astype(BF16)).reshape(dense.shape)

    @pl.loop(1, TAIL)
    def _(step):
        plane_copy(step).wait_recv()

    deep[...] = jnp.zeros_like(deep)

    @pl.loop(0, TAIL)
    def _(source):
        deep[...] += planes[source]

    zone = lax.rem(tail, 2)
    takes = lax.div(depth, quarter) == zone

    def deep_copy(step):
        level = zone * quarter + step
        return remote(
            deep.at[step],
            deep_in.at[depth],
            sem_zs.at[step],
            sem_zr.at[depth],
            (level * 2 + core, tail),
        )

    def deep_landing(source):
        return remote(
            deep.at[0], deep_in.at[source], sem_zs.at[0], sem_zr.at[source], (other, tail)
        )

    @pl.loop(0, quarter)
    def _(step):
        @pl.when(zone * quarter + step != depth)
        def _():
            deep_copy(step).start()

    @pl.when(takes)
    def _():
        deep_in[depth] = deep[depth - zone * quarter]

    def dense_copy(step):
        peer = around(tail, step, TAIL)
        return remote(
            dense.at[peer], dense_in.at[tail], sem_ds.at[step], sem_dr.at[step], (head, peer)
        )

    @pl.loop(1, TAIL)
    def _(step):
        dense_copy(step).start()

    dense_in[tail] = dense[tail]
    mine_k = lax.div(tail, 2)

    def total_copy(step):
        return remote(
            neg_total.at[mine_k],
            neg_total.at[mine_k],
            sem_ns.at[step],
            sem_nr.at[mine_k],
            (head, around(tail, step, TAIL)),
        )

    def total_landing(k):
        return remote(
            neg_total.at[k], neg_total.at[k], sem_ns.at[1], sem_nr.at[k], (other, tail)
        )

    @pl.when(takes)
    def _():
        @pl.loop(0, DEPTH)
        def _(source):
            @pl.when(source != depth)
            def _():
                deep_landing(source).wait_recv()

        total = deep_in[0]
        for source in range(1, DEPTH):
            total = total + deep_in[source]
        neg_total[mine_k] = total

        @pl.loop(1, TAIL)
        def _(step):
            total_copy(step).start()

    @pl.loop(1, TAIL)
    def _(step):
        dense_copy(step).wait_recv()

    @pl.loop(0, neg_total.shape[0])
    def _(k):
        @pl.when(2 * k + lax.div(depth, quarter) != tail)
        def _():
            total_landing(k).wait_recv()

    keep_rows.wait()
    for b in range(owned):
        gradient = dense_in[0, b * 8 : (b + 1) * 8]
        for source in range(1, TAIL):
            gradient = gradient + dense_in[source, b * 8 : (b + 1) * 8]
        for k in range(neg_total.shape[0]):
            weight = jnp.where(neg_ids[k] == tail * owned + b, 1.0, 0.0).astype(F32)
            gradient = gradient + weight * neg_total[k]
        fresh = (
            own_state[b * 8 : (b + 1) * 8, 0:1]
            + jnp.sum(gradient * gradient, axis=1, keepdims=True) / width
        )
        state_next[b * 8 : (b + 1) * 8, :] = jnp.broadcast_to(fresh, (8, state_next.shape[1]))
        update[b] = (
            rows_now[b].astype(F32) - gradient * (LEARN_RATE / jnp.sqrt(fresh))
        ).astype(BF16)

    def rows_copy(step):
        return remote(
            update,
            out.at[:, head],
            sem_us.at[step],
            sem_ur.at[step],
            (around(depth, step, DEPTH) * 2 + core, tail),
        )

    def state_copy(step):
        return remote(
            state_next,
            state_out.at[head],
            sem_ws.at[step],
            sem_wr.at[step],
            (around(depth, step, DEPTH) * 2 + core, tail),
        )

    def source_of(step):
        return around(depth, DEPTH - step, DEPTH) * 2 + core

    @pl.loop(1, DEPTH)
    def _(step):
        rows_copy(step).start()
        state_copy(step).start()

    out_own = pltpu.make_async_copy(update, out.at[:, head], sem_local.at[2])
    out_own.start()
    state_own = pltpu.make_async_copy(state_next, state_out.at[head], sem_local.at[3])
    state_own.start()
    first_rows = remote(update, out.at[:, head], sem_fs.at[0], sem_fr.at[0], (other, tail))
    first_state = remote(state_next, state_out.at[head], sem_gs.at[0], sem_gr.at[0], (other, tail))
    first_rows.start()
    first_state.start()

    def pass_rows(step):
        place = source_of(step)
        return remote(
            out.at[:, place], out.at[:, place], sem_fs.at[step], sem_fr.at[step], (other, tail)
        )

    def pass_state(step):
        place = source_of(step)
        return remote(
            state_out.at[place],
            state_out.at[place],
            sem_gs.at[step],
            sem_gr.at[step],
            (other, tail),
        )

    @pl.loop(1, DEPTH)
    def _(step):
        rows_copy(step).wait_recv()
        pass_rows(step).start()
        state_copy(step).wait_recv()
        pass_state(step).start()

    out_own.wait()
    state_own.wait()
    first_rows.wait()
    first_state.wait()

    @pl.loop(1, DEPTH)
    def _(step):
        pass_rows(step).wait()
        pass_state(step).wait()
        rows_copy(step).wait_send()
        state_copy(step).wait_send()

    pair_copy(0).wait_send()

    @pl.loop(1, TAIL)
    def _(step):
        block_copy(step).wait_send()
        seat_copy(step).wait_send()
        pair_copy(step).wait_send()
        plane_copy(step).wait_send()
        dense_copy(step).wait_send()

    @pl.loop(0, quarter)
    def _(step):
        @pl.when(zone * quarter + step != depth)
        def _():
            deep_copy(step).wait_send()

    @pl.when(takes)
    def _():
        @pl.loop(1, TAIL)
        def _(step):
            total_copy(step).wait_send()


def run_exchange(neg_ids, block_part, places, neg_part, own_rows, own_state):
    owned, _, group, width = own_rows.shape
    negs = neg_ids.shape[0]
    quarter = DEPTH // 2
    sems = pltpu.SemaphoreType.DMA
    anywhere = pl.BlockSpec(memory_space=pl.ANY)
    vmem = pl.BlockSpec(memory_space=pltpu.VMEM)
    rows = owned * group
    return pl.pallas_call(
        exchange,
        out_shape=(
            jax.ShapeDtypeStruct(own_rows.shape, BF16),
            jax.ShapeDtypeStruct((HEAD, rows, 128), F32),
        ),
        in_specs=[
            pl.BlockSpec(memory_space=pltpu.SMEM),
            anywhere,
            vmem,
            anywhere,
            anywhere,
            vmem,
        ],
        out_specs=(anywhere, anywhere),
        scratch_shapes=[
            pltpu.VMEM((HEAD, owned, group, width), BF16),
            pltpu.VMEM((HEAD, 8, 128), jnp.int32),
            pltpu.VMEM((TAIL, quarter, group, width), F32),
            pltpu.VMEM((TAIL, quarter, group, width), F32),
            pltpu.VMEM((TAIL, quarter, group, width), F32),
            pltpu.VMEM((quarter, group, width), F32),
            pltpu.VMEM((DEPTH, group, width), F32),
            pltpu.VMEM((negs, group, width), F32),
            pltpu.VMEM((HEAD * rows, width), F32),
            pltpu.VMEM((TAIL, rows, width), F32),
            pltpu.VMEM((TAIL, rows, width), F32),
            pltpu.VMEM((owned, group, width), BF16),
            pltpu.VMEM((owned, group, width), BF16),
            pltpu.VMEM((rows, 128), F32),
            sems((HEAD,)),
            sems((HEAD,)),
            sems((HEAD,)),
            sems((HEAD,)),
            sems((TAIL,)),
            sems((TAIL,)),
            sems((TAIL,)),
            sems((TAIL,)),
            sems((TAIL,)),
            sems((quarter,)),
            sems((DEPTH,)),
            sems((TAIL,)),
            sems((TAIL,)),
            sems((TAIL,)),
            sems((negs,)),
            sems((DEPTH,)),
            sems((DEPTH,)),
            sems((DEPTH,)),
            sems((DEPTH,)),
            sems((DEPTH,)),
            sems((DEPTH,)),
            sems((DEPTH,)),
            sems((DEPTH,)),
            sems((4,)),
        ],
        compiler_params=pltpu.CompilerParams(
            collective_id=1, has_side_effects=True, vmem_limit_bytes=40 << 20
        ),
    )(neg_ids, block_part, places, neg_part, own_rows, own_state)


def per_device(
    head_emb,
    head_state,
    tail_emb,
    tail_state,
    relation_emb,
    head_rows,
    relations,
    tail_offsets,
    tail_owner,
    tail_local,
    block_count,
    neg_blocks,
):
    owned, span, width = tail_emb.shape
    blocks = tail_local.shape[0]
    head = lax.axis_index("head")
    group = span // HEAD
    block_ids = tail_owner[:, 0] * owned + tail_local
    lane = jnp.arange(128, dtype=jnp.int32)
    base = (head % 4) * blocks * group
    inside = (lane >= base) & (lane < base + blocks * group)
    spot = jnp.clip(lane - base, 0, blocks * group - 1)
    hits = (spot[:, None] // group) == jnp.arange(blocks, dtype=jnp.int32)[None, :]
    block_of = jnp.sum(jnp.where(hits, block_ids[None, :], 0), axis=1)
    places = jnp.where(inside, block_of * group + spot % group, 0)
    places = jnp.broadcast_to(places[None, :], (8, 128)).astype(jnp.int32)
    own_state = lax.dynamic_index_in_dim(
        tail_state.reshape(owned, HEAD, group), head, axis=1, keepdims=False
    )
    own_state = jnp.broadcast_to(own_state.reshape(owned * group, 1), (owned * group, 128))

    table = gather_table(tail_emb)
    head_new, head_state_new, block_part, neg_part = run_edges(
        block_ids,
        neg_blocks,
        block_count,
        table.reshape(TAIL * owned, span, width),
        head_emb,
        head_state[None, :],
        relation_emb,
        head_rows,
        relations,
        tail_offsets,
    )
    tail_new, tail_state_new = run_exchange(
        neg_blocks,
        block_part,
        places,
        neg_part.reshape(neg_blocks.shape[0], DEPTH, 2, group, width),
        tail_emb.reshape(owned, HEAD, group, width),
        own_state,
    )
    tail_state_new = tail_state_new[:, :, 0].reshape(HEAD, owned, group)
    tail_state_new = tail_state_new.transpose(1, 0, 2).reshape(owned, span)
    return (head_new, head_state_new[0], tail_new.reshape(owned, span, width), tail_state_new)


def solution(mesh):
    placed = (
        P(("head", "tail"), None),
        P(("head", "tail")),
        P("tail", None, None),
        P("tail", None),
        P(),
        P(("head", "tail"), None),
        P(("head", "tail"), None),
        P(("head", "tail"), None),
        P(("head", "tail"), None),
        P(("head", "tail")),
        P(("head", "tail")),
        P(),
    )
    return jax.shard_map(
        per_device,
        mesh=mesh,
        in_specs=placed,
        out_specs=(
            P(("head", "tail"), None),
            P(("head", "tail")),
            P("tail", None, None),
            P("tail", None),
        ),
        check_vma=False,
    )
```

```python
import jax
import jax.numpy as jnp
from jax import lax
from jax.experimental import pallas as pl
from jax.experimental.pallas import tpu as pltpu
from jax.sharding import PartitionSpec as P

LEARN_RATE = 0.3
MESH = pl.DeviceIdType.MESH
F32 = jnp.float32
BF16 = jnp.bfloat16
SIDE = 4
DEPTH = 8
HEAD = 16
TAIL = 16
LANES = 896


def greet(targets):
    barrier = pltpu.get_barrier_semaphore()
    for target in targets:
        pl.semaphore_signal(barrier, inc=1, device_id=target, device_id_type=MESH)
    pl.semaphore_wait(barrier, len(targets))


TN = (((0,), (0,)), ((), ()))
NT = (((1,), (1,)), ((), ()))


def mm(left, right, dims=(((1,), (0,)), ((), ()))):
    return lax.dot_general(left, right, dims, preferred_element_type=F32)


def one_hot(count, index_row):
    spots = lax.broadcasted_iota(jnp.int32, (count, index_row.shape[1]), 0)
    return jnp.where(spots == index_row, 1.0, 0.0).astype(BF16)


def table_gather(
    own,
    head_hbm,
    rel_hbm,
    head_rows,
    relations,
    table,
    query_out,
    rel_out,
    head_t,
    rel_t,
    query,
    rel_vec,
    send1,
    recv1,
    send2,
    recv2,
    send3,
    recv3,
    local,
):
    head, tail = lax.axis_index("head"), lax.axis_index("tail")
    core, col, row = lax.rem(head, 2), lax.rem(tail, SIDE), lax.div(tail, SIDE)
    sibling = (head + 1 - 2 * core, tail)
    size = own.shape[1]
    everything = (0, size)
    first, second = (0, size // 2), (size // 2, size // 2)
    blocks = query.shape[0]

    loads = [
        pltpu.make_async_copy(head_hbm, head_t, local.at[0]),
        pltpu.make_async_copy(rel_hbm, rel_t, local.at[1]),
        pltpu.make_async_copy(own, table.at[tail], local.at[2]),
    ]
    for load in loads:
        load.start()

    def place(which, along, across):
        dx, dy = (along, across) if which == 0 else (across, along)
        return lax.rem(row + dy + SIDE, SIDE) * SIDE + lax.rem(col + dx + SIDE, SIDE)

    greet(
        [sibling]
        + [(head, place(0, 1, 0)), (head, place(0, -1, 0))]
        + [(head, place(1, 1, 0)), (head, place(1, -1, 0))]
    )

    def copy(which, origin, part, sems, spot, target):
        block = 2 * core + which
        start, count = part
        here = table.at[place(which, *origin), block, pl.ds(start, count)]
        source = own.at[block, pl.ds(start, count)] if origin == (0, 0) else here
        return pltpu.make_async_remote_copy(
            src_ref=source,
            dst_ref=here,
            send_sem=sems[0].at[which, spot],
            recv_sem=sems[1].at[which, spot],
            device_id=target,
            device_id_type=MESH,
        )

    def landing(which, origin, part, sems, spot, block=None):
        block = 2 * core + which if block is None else block
        start, count = part
        here = table.at[place(which, *origin), block, pl.ds(start, count)]
        return pltpu.make_async_remote_copy(
            src_ref=here,
            dst_ref=here,
            send_sem=sems[0].at[which, spot],
            recv_sem=sems[1].at[which, spot],
            device_id=sibling,
            device_id_type=MESH,
        )

    stage1, stage2, stage3 = (send1, recv1), (send2, recv2), (send3, recv3)
    sent = []

    def send(*description):
        transfer = copy(*description)
        transfer.start()
        sent.append(transfer)

    def spread(which, origin):
        spot = (origin[0] % SIDE) * 4
        send(which, origin, everything, stage2, spot, (head, place(which, 0, 1)))
        send(which, origin, everything, stage2, spot + 1, (head, place(which, 0, -1)))

    def share(which, origin):
        spot = (origin[0] % SIDE) * 4 + origin[1] % SIDE
        send(which, origin, everything, stage3, spot, sibling)

    stores = []

    def make_query(b):
        half = size // 2
        vec = mm(head_t[...], one_hot(head_t.shape[1], head_rows[b : b + 1, :]))
        rel = mm(rel_t[...], one_hot(rel_t.shape[1], relations[b : b + 1, :]))
        rel_vec[b] = rel.astype(BF16)
        query[b, :half] = (vec[:half] * rel[:half] - vec[half:] * rel[half:]).astype(BF16)
        query[b, half:] = (vec[:half] * rel[half:] + vec[half:] * rel[:half]).astype(BF16)
        for value, target, spot in ((query, query_out, 3), (rel_vec, rel_out, 3 + blocks)):
            store = pltpu.make_async_copy(value.at[b], target.at[b], local.at[spot + b])
            store.start()
            stores.append(store)

    for which in (0, 1):
        send(which, (0, 0), everything, stage1, 0, (head, place(which, 1, 0)))
        send(which, (0, 0), everything, stage1, 1, (head, place(which, -1, 0)))
    for which in (0, 1):
        spread(which, (0, 0))
    loads[0].wait()
    loads[1].wait()
    make_query(0)
    for which in (0, 1):
        landing(which, (-1, 0), everything, stage1, 0).wait_recv()
        send(which, (-1, 0), first, stage1, 2, (head, place(which, 1, 0)))
        spread(which, (-1, 0))
        share(which, (-1, 0))
        landing(which, (1, 0), everything, stage1, 1).wait_recv()
        send(which, (1, 0), second, stage1, 3, (head, place(which, -1, 0)))
        spread(which, (1, 0))
        share(which, (1, 0))
    for b in range(1, blocks - 1):
        make_query(b)
    for which in (0, 1):
        landing(which, (2, 0), first, stage1, 2).wait_recv()
        landing(which, (2, 0), second, stage1, 3).wait_recv()
        spread(which, (2, 0))
        share(which, (2, 0))
    for along in (0, -1, 1, 2):
        spot = (along % SIDE) * 4
        for which in (0, 1):
            landing(which, (along, -1), everything, stage2, spot).wait_recv()
            send(which, (along, -1), first, stage2, spot + 2, (head, place(which, 0, 1)))
            share(which, (along, -1))
            landing(which, (along, 1), everything, stage2, spot + 1).wait_recv()
            send(which, (along, 1), second, stage2, spot + 3, (head, place(which, 0, -1)))
            share(which, (along, 1))
        if along == 0:
            make_query(blocks - 1)
    for along in (0, -1, 1, 2):
        spot = (along % SIDE) * 4
        for which in (0, 1):
            landing(which, (along, 2), first, stage2, spot + 2).wait_recv()
            landing(which, (along, 2), second, stage2, spot + 3).wait_recv()
            share(which, (along, 2))
    for which in (0, 1):
        for along in range(SIDE):
            for across in range(SIDE):
                if (along, across) != (0, 0):
                    block = 2 * (1 - core) + which
                    spot = along * 4 + across
                    landing(which, (along, across), everything, stage3, spot, block).wait_recv()
    loads[2].wait()
    for store in stores:
        store.wait()
    for transfer in sent:
        transfer.wait_send()


def gather_table(tail_t, head_t, rel_t, head_rows, relations):
    blocks, edges = head_rows.shape
    width = head_t.shape[0]
    sems = pltpu.SemaphoreType.DMA
    anywhere = pl.BlockSpec(memory_space=pl.ANY)
    vmem = pl.BlockSpec(memory_space=pltpu.VMEM)
    return pl.pallas_call(
        table_gather,
        out_shape=(
            jax.ShapeDtypeStruct((TAIL,) + tail_t.shape, BF16),
            jax.ShapeDtypeStruct((blocks, width, edges), BF16),
            jax.ShapeDtypeStruct((blocks, width, edges), BF16),
        ),
        in_specs=[anywhere, anywhere, anywhere, vmem, vmem],
        out_specs=(anywhere, anywhere, anywhere),
        scratch_shapes=[
            pltpu.VMEM(head_t.shape, BF16),
            pltpu.VMEM(rel_t.shape, BF16),
            pltpu.VMEM((blocks, width, edges), BF16),
            pltpu.VMEM((blocks, width, edges), BF16),
            sems((2, 4)),
            sems((2, 4)),
            sems((2, 16)),
            sems((2, 16)),
            sems((2, 16)),
            sems((2, 16)),
            sems((3 + 2 * blocks,)),
        ],
        compiler_params=pltpu.CompilerParams(
            collective_id=0, has_side_effects=True, vmem_limit_bytes=40 << 20
        ),
    )(tail_t, head_t, rel_t, head_rows, relations)


def edge_work(
    owners,
    locals_,
    neg_ids,
    live_count,
    table,
    query_hbm,
    rel_hbm,
    head_emb,
    head_state,
    head_rows,
    offsets,
    head_new,
    state_new,
    block_out,
    neg_out,
    chosen,
    neg_t,
    negs,
    query_all,
    rel_all,
    prob_all,
    grad_hi,
    grad_lo,
    hot_all,
    head_grad,
    sems,
):
    blocks, edges = head_rows.shape
    width, rows = head_emb.shape
    half = width // 2
    owned = table.shape[0] // TAIL
    span = chosen.shape[2]
    neg_count = neg_ids.shape[0]
    piece = 160

    fetches = []
    for k in range(neg_count):
        lanes = pl.ds(k * span, span)
        fetches.append(pltpu.make_async_copy(table.at[neg_ids[k]], neg_t.at[:, lanes], sems.at[k]))
    for b in range(blocks):
        block = owners[b] * owned + locals_[b]
        lanes = pl.ds(b * edges, edges)
        spot = neg_count + 3 * b
        fetches.append(
            pltpu.make_async_copy(query_hbm.at[b], query_all.at[:, lanes], sems.at[spot])
        )
        fetches.append(pltpu.make_async_copy(table.at[block], chosen.at[b], sems.at[spot + 1]))
        fetches.append(pltpu.make_async_copy(rel_hbm.at[b], rel_all.at[b], sems.at[spot + 2]))
    for fetch in fetches:
        fetch.start()
    for b in range(blocks):
        hot_all[:, b * edges : (b + 1) * edges] = one_hot(rows, head_rows[b : b + 1, :])
    for fetch in fetches:
        fetch.wait()
    for k in range(neg_count):
        negs[k * span : (k + 1) * span, :] = neg_t[:, k * span : (k + 1) * span].T

    def one_block(b, carry):
        lanes = pl.ds(pl.multiple_of(b * edges, edges), edges)
        live = jnp.where(b < live_count[0], 1.0, 0.0).astype(F32)
        pick = one_hot(span, offsets[pl.ds(b, 1), :])
        tail_vec = mm(chosen[b], pick)
        query = query_all[:, lanes].astype(F32)
        positive = jnp.sum(query * tail_vec, axis=0, keepdims=True)
        score = mm(negs[...], query_all[:, lanes])
        largest = jnp.maximum(positive, jnp.max(score, axis=0, keepdims=True))
        pos_exp = jnp.exp(positive - largest)
        neg_exp = jnp.exp(score - largest)
        denominator = pos_exp + jnp.sum(neg_exp, axis=0, keepdims=True)
        pos_grad = (pos_exp / denominator - 1.0) * live
        prob_all[:, lanes] = (neg_exp * (live / denominator)).astype(BF16)
        query_grad = pos_grad * tail_vec + mm(neg_t[...], prob_all[:, lanes])
        part = pos_grad * query
        part_a = part.astype(BF16)
        rest = part - part_a.astype(F32)
        part_b = rest.astype(BF16)
        part_c = (rest - part_b.astype(F32)).astype(BF16)
        block_grad = mm(pick, part_a, NT) + (mm(pick, part_b, NT) + mm(pick, part_c, NT))
        number = (owners[b] * owned + locals_[b]).astype(F32)
        group = span // HEAD
        for i in range(HEAD):
            block_out[i, b, :, :width] = block_grad[i * group : (i + 1) * group].astype(BF16)
            block_out[i, b, :, width:] = jnp.full((group, LANES - width), number, BF16)
        rel = rel_all[b].astype(F32)
        rr, ri = rel[:half], rel[half:]
        qr, qi = query_grad[:half], query_grad[half:]
        for start, change in ((0, qr * rr + qi * ri), (half, qi * rr - qr * ri)):
            change_hi = change.astype(BF16)
            grad_hi[start : start + half, lanes] = change_hi
            grad_lo[start : start + half, lanes] = (change - change_hi.astype(F32)).astype(BF16)
        return carry

    lax.fori_loop(0, blocks, one_block, 0)

    def neg_rows(k, carry):
        span_rows = pl.ds(pl.multiple_of(k * 256, 256), 256)
        neg_out[span_rows, :] = mm(prob_all[span_rows, :], query_all[...], NT)
        return carry

    lax.fori_loop(0, neg_count * span // 256, neg_rows, 0)

    def head_piece(p, squares):
        spots = pl.ds(pl.multiple_of(p * piece, piece), piece)
        gradient = mm(grad_hi[spots, :], hot_all[...], NT) + mm(grad_lo[spots, :], hot_all[...], NT)
        head_grad[spots, :] = gradient
        return squares + jnp.sum(gradient * gradient, axis=0, keepdims=True)

    squares = lax.fori_loop(0, width // piece, head_piece, jnp.zeros((1, rows), F32))
    state_next = head_state[...] + squares / width
    state_new[...] = state_next
    rate = LEARN_RATE / jnp.sqrt(state_next)

    def head_update(p, carry):
        spots = pl.ds(pl.multiple_of(p * piece, piece), piece)
        head_new[spots, :] = (head_emb[spots, :].astype(F32) - head_grad[spots, :] * rate).astype(
            BF16
        )
        return carry

    lax.fori_loop(0, width // piece, head_update, 0)


def run_edges(
    owners, locals_, neg_ids, live_count, table, query, rel_vec, head_t, head_state, head_rows, offsets
):
    blocks, edges = head_rows.shape
    width, rows = head_t.shape
    span = table.shape[2]
    negs = neg_ids.shape[0]
    total = blocks * edges
    smem = pl.BlockSpec(memory_space=pltpu.SMEM)
    vmem = pl.BlockSpec(memory_space=pltpu.VMEM)
    anywhere = pl.BlockSpec(memory_space=pl.ANY)
    return pl.pallas_call(
        edge_work,
        out_shape=(
            jax.ShapeDtypeStruct((width, rows), BF16),
            jax.ShapeDtypeStruct((1, rows), F32),
            jax.ShapeDtypeStruct((HEAD, blocks, span // HEAD, LANES), BF16),
            jax.ShapeDtypeStruct((negs * span, width), F32),
        ),
        in_specs=[smem, smem, smem, smem, anywhere, anywhere, anywhere] + [vmem] * 4,
        out_specs=(vmem, vmem, vmem, vmem),
        scratch_shapes=[
            pltpu.VMEM((blocks, width, span), BF16),
            pltpu.VMEM((width, negs * span), BF16),
            pltpu.VMEM((negs * span, width), BF16),
            pltpu.VMEM((width, total), BF16),
            pltpu.VMEM((blocks, width, edges), BF16),
            pltpu.VMEM((negs * span, total), BF16),
            pltpu.VMEM((width, total), BF16),
            pltpu.VMEM((width, total), BF16),
            pltpu.VMEM((rows, total), BF16),
            pltpu.VMEM((width, rows), F32),
            pltpu.SemaphoreType.DMA((3 * blocks + negs,)),
        ],
        compiler_params=pltpu.CompilerParams(vmem_limit_bytes=48 << 20),
    )(owners, locals_, neg_ids, live_count, table, query, rel_vec, head_t, head_state, head_rows, offsets)


def remote(source, target, send_sem, recv_sem, device):
    return pltpu.make_async_remote_copy(
        src_ref=source,
        dst_ref=target,
        send_sem=send_sem,
        recv_sem=recv_sem,
        device_id=device,
        device_id_type=MESH,
    )


class PlaneSum:
    def __init__(self, spread, in_x, in_y, mid_x, mid_y, end_x, end_y, sems):
        self.refs = (spread, in_x, in_y, mid_x, mid_y, end_x, end_y)
        self.sems = sems
        self.head, tail = lax.axis_index("head"), lax.axis_index("tail")
        self.col, self.row = lax.rem(tail, SIDE), lax.div(tail, SIDE)

    def steps(self):
        for step in range(1, SIDE):
            col = lax.rem(self.col + step, SIDE)
            row = lax.rem(self.row + step, SIDE)
            yield step - 1, col, row, (self.head, self.row * SIDE + col), (
                self.head,
                row * SIDE + self.col,
            )

    def first(self):
        spread, in_x, in_y = self.refs[:3]
        send, recv = self.sems
        copies = []
        for n, col, row, over_x, over_y in self.steps():
            copies.append(
                remote(spread.at[:, col, pl.ds(0, 2)], in_x.at[n], send.at[n], recv.at[n], over_x)
            )
            copies.append(
                remote(
                    spread.at[row, :, pl.ds(2, 2)], in_y.at[n], send.at[3 + n], recv.at[3 + n], over_y
                )
            )
        return copies

    def second(self):
        mid_x, mid_y, end_x, end_y = self.refs[3:]
        send, recv = self.sems
        copies = []
        for n, col, row, over_x, over_y in self.steps():
            copies.append(remote(mid_x.at[row], end_x.at[n], send.at[6 + n], recv.at[6 + n], over_y))
            copies.append(remote(mid_y.at[col], end_y.at[n], send.at[9 + n], recv.at[9 + n], over_x))
        return copies

    def start_first(self):
        for copy in self.first():
            copy.start()

    def start_second(self):
        spread, in_x, in_y, mid_x, mid_y = self.refs[:5]
        for copy in self.first():
            copy.wait_recv()
        for place in range(SIDE):
            for part in range(2):
                total = spread[place, self.col, part]
                other = spread[self.row, place, 2 + part]
                for n in range(SIDE - 1):
                    total = total + in_x[n, place, part]
                    other = other + in_y[n, place, part]
                mid_x[place, part] = total
                mid_y[place, part] = other
        for copy in self.second():
            copy.start()

    def result(self):
        mid_x, mid_y, end_x, end_y = self.refs[3:]
        for copy in self.second():
            copy.wait_recv()
        parts = []
        for part in range(2):
            total = mid_x[self.row, part]
            for n in range(SIDE - 1):
                total = total + end_x[n, part]
            parts.append(total)
        for part in range(2):
            total = mid_y[self.col, part]
            for n in range(SIDE - 1):
                total = total + end_y[n, part]
            parts.append(total)
        return parts

    def finish(self):
        for copy in self.first() + self.second():
            copy.wait_send()


def exchange(
    neg_ids,
    block_part,
    neg_part,
    own_t,
    own_state,
    out,
    slots,
    theirs,
    mine,
    neg_in_x,
    neg_in_y,
    neg_mid_x,
    neg_mid_y,
    neg_end_x,
    neg_end_y,
    deep,
    deep_in,
    neg_total,
    slot_rows,
    dense,
    in_x,
    in_y,
    mid_x,
    mid_y,
    end_x,
    end_y,
    update,
    sem_bs,
    sem_br,
    sem_cs,
    sem_cr,
    sem_ps,
    sem_pr,
    sem_zs,
    sem_zr,
    sem_ds,
    sem_dr,
    sem_us,
    sem_ur,
    sem_fs,
    sem_fr,
    sem_local,
):
    head, tail = lax.axis_index("head"), lax.axis_index("tail")
    core, depth = lax.rem(head, 2), lax.div(head, 2)
    other = head + 1 - 2 * core
    owned = own_t.shape[0]
    width = own_t.shape[1]
    group = slots.shape[2]
    quarter = DEPTH // 2

    def around(index, step, count):
        return lax.rem(index + step, count)

    keep_block = pltpu.make_async_copy(block_part.at[head], slots.at[head], sem_local.at[0])
    keep_neg = pltpu.make_async_copy(neg_part.at[:, :, :, core], mine, sem_local.at[1])
    keep_neg.start()
    keep_block.start()

    barrier = pltpu.get_barrier_semaphore()

    @pl.loop(1, HEAD)
    def _(step):
        pl.semaphore_signal(
            barrier, inc=1, device_id=(around(head, step, HEAD), tail), device_id_type=MESH
        )
        pl.semaphore_signal(
            barrier, inc=1, device_id=(head, around(tail, step, TAIL)), device_id_type=MESH
        )

    pl.semaphore_wait(barrier, HEAD + TAIL - 2)

    def pair_copy(part):
        return remote(
            neg_part.at[part, :, :, 1 - core],
            theirs.at[part],
            sem_cs.at[part],
            sem_cr.at[part],
            (other, tail),
        )

    for part in range(SIDE):
        pair_copy(part).start()

    def block_copy(step):
        peer = around(head, step, HEAD)
        return remote(
            block_part.at[peer], slots.at[head], sem_bs.at[step], sem_br.at[step], (peer, tail)
        )

    @pl.loop(1, HEAD)
    def _(step):
        block_copy(step).start()

    keep_neg.wait()
    for part in range(SIDE):
        pair_copy(part).wait_recv()
        for place in range(SIDE):
            mine[part, place] = mine[part, place] + theirs[part, place]
    plane = PlaneSum(
        mine, neg_in_x, neg_in_y, neg_mid_x, neg_mid_y, neg_end_x, neg_end_y, (sem_ps, sem_pr)
    )
    plane.start_first()
    plane.start_second()
    for place, total in enumerate(plane.result()):
        deep[place] = total

    zone = lax.rem(tail, 2)
    takes = lax.div(depth, quarter) == zone

    def deep_copy(step):
        level = zone * quarter + step
        return remote(
            deep.at[step],
            deep_in.at[depth],
            sem_zs.at[step],
            sem_zr.at[depth],
            (level * 2 + core, tail),
        )

    def deep_landing(source):
        return remote(
            deep.at[0], deep_in.at[source], sem_zs.at[0], sem_zr.at[source], (other, tail)
        )

    @pl.loop(0, quarter)
    def _(step):
        @pl.when(zone * quarter + step != depth)
        def _():
            deep_copy(step).start()

    neg_total[...] = jnp.zeros_like(neg_total)

    keep_block.wait()

    @pl.loop(1, HEAD)
    def _(step):
        block_copy(step).wait_recv()

    @pl.loop(0, HEAD)
    def _(source):
        for b in range(owned):
            spot = pl.multiple_of((source * owned + b) * group, group)
            slot_rows[pl.ds(spot, group), :] = slots[source, b].astype(F32)

    count = HEAD * owned * group
    number = slot_rows[:, width : width + 1]
    inner = lax.broadcasted_iota(jnp.int32, (count, 1), 0) % group
    goal = number * group + inner.astype(F32)
    spots = lax.broadcasted_iota(jnp.int32, (count, count), 1).astype(F32)
    hot = jnp.where(spots == goal, 1.0, 0.0).astype(BF16)
    sums = mm(hot, slot_rows[:, :width].astype(BF16), TN)

    @pl.when(takes)
    def _():
        deep_in[depth] = deep[depth - zone * quarter]

        @pl.loop(0, DEPTH)
        def _(source):
            @pl.when(source != depth)
            def _():
                deep_landing(source).wait_recv()

        total = deep_in[0]
        for source in range(1, DEPTH):
            total = total + deep_in[source]
        neg_total[...] = total

    target = neg_ids[lax.div(tail, 2)]
    total = neg_total[...]
    for block in range(TAIL * owned):
        y, x, part = block // owned // SIDE, block // owned % SIDE, block % owned
        weight = jnp.where(target == block, 1.0, 0.0).astype(F32)
        dense[y, x, part] = sums[block * group : (block + 1) * group] + weight * total

    table = PlaneSum(dense, in_x, in_y, mid_x, mid_y, end_x, end_y, (sem_ds, sem_dr))
    table.start_first()
    lane = lax.broadcasted_iota(jnp.int32, (group, own_t.shape[2]), 1)
    mark = lane == head * group + lax.broadcasted_iota(jnp.int32, (group, own_t.shape[2]), 0)
    rows_now = [
        mm(jnp.where(mark, 1.0, 0.0).astype(BF16), own_t[b], NT) for b in range(owned)
    ]
    states_now = [
        jnp.sum(jnp.where(mark, own_state[b : b + 1, :], 0.0), axis=1, keepdims=True)
        for b in range(owned)
    ]
    table.start_second()

    for b, gradient in enumerate(table.result()):
        fresh = states_now[b] + jnp.sum(gradient * gradient, axis=1, keepdims=True) / width
        update[b, :, :width] = (
            rows_now[b] - gradient * (LEARN_RATE / jnp.sqrt(fresh))
        ).astype(BF16)
        spot = lax.broadcasted_iota(jnp.int32, (group, LANES - width), 1)
        fresh_a = fresh.astype(BF16).astype(F32)
        fresh_b = (fresh - fresh_a).astype(BF16).astype(F32)
        fresh_c = fresh - fresh_a - fresh_b
        pieces = jnp.where(spot == 0, fresh_a, jnp.where(spot == 1, fresh_b, fresh_c))
        update[b, :, width:] = pieces.astype(BF16)

    def rows_copy(step):
        peer = around(depth, step, DEPTH) * 2 + core
        return remote(update, out.at[:, head], sem_us.at[step], sem_ur.at[step], (peer, tail))

    @pl.loop(1, DEPTH)
    def _(step):
        rows_copy(step).start()

    out_own = pltpu.make_async_copy(update, out.at[:, head], sem_local.at[2])
    out_own.start()
    first_rows = remote(update, out.at[:, head], sem_fs.at[0], sem_fr.at[0], (other, tail))
    first_rows.start()

    def pass_rows(step):
        place = around(depth, DEPTH - step, DEPTH) * 2 + core
        return remote(
            out.at[:, place], out.at[:, place], sem_fs.at[step], sem_fr.at[step], (other, tail)
        )

    @pl.loop(1, DEPTH)
    def _(step):
        rows_copy(step).wait_recv()
        pass_rows(step).start()

    plane.finish()
    table.finish()
    for part in range(SIDE):
        pair_copy(part).wait_send()

    @pl.loop(1, HEAD)
    def _(step):
        block_copy(step).wait_send()

    @pl.loop(0, quarter)
    def _(step):
        @pl.when(zone * quarter + step != depth)
        def _():
            deep_copy(step).wait_send()

    out_own.wait()
    first_rows.wait()

    @pl.loop(1, DEPTH)
    def _(step):
        pass_rows(step).wait()
        rows_copy(step).wait_send()


def run_exchange(neg_ids, block_part, neg_part, own_t, own_state):
    owned, width, span = own_t.shape
    group = span // HEAD
    quarter = DEPTH // 2
    sems = pltpu.SemaphoreType.DMA
    anywhere = pl.BlockSpec(memory_space=pl.ANY)
    vmem = pl.BlockSpec(memory_space=pltpu.VMEM)
    whole = pltpu.VMEM((SIDE, SIDE, 4, group, width), F32)
    plane_sum = (
        [pltpu.VMEM((SIDE - 1, SIDE, 2, group, width), F32)] * 2
        + [pltpu.VMEM((SIDE, 2, group, width), F32)] * 2
        + [pltpu.VMEM((SIDE - 1, 2, group, width), F32)] * 2
    )
    return pl.pallas_call(
        exchange,
        out_shape=jax.ShapeDtypeStruct((owned, HEAD, group, LANES), BF16),
        in_specs=[pl.BlockSpec(memory_space=pltpu.SMEM), anywhere, anywhere, vmem, vmem],
        out_specs=anywhere,
        scratch_shapes=[
            pltpu.VMEM((HEAD, owned, group, LANES), BF16),
            whole,
            whole,
            *plane_sum,
            pltpu.VMEM((quarter, group, width), F32),
            pltpu.VMEM((DEPTH, group, width), F32),
            pltpu.VMEM((group, width), F32),
            pltpu.VMEM((HEAD * owned * group, LANES), F32),
            whole,
            *plane_sum,
            pltpu.VMEM((owned, group, LANES), BF16),
            sems((HEAD,)),
            sems((HEAD,)),
            sems((SIDE,)),
            sems((SIDE,)),
            sems((12,)),
            sems((12,)),
            sems((quarter,)),
            sems((DEPTH,)),
            sems((12,)),
            sems((12,)),
            sems((DEPTH,)),
            sems((DEPTH,)),
            sems((DEPTH,)),
            sems((DEPTH,)),
            sems((3,)),
        ],
        compiler_params=pltpu.CompilerParams(
            collective_id=1, has_side_effects=True, vmem_limit_bytes=48 << 20
        ),
    )(neg_ids, block_part, neg_part, own_t, own_state)


def per_device(
    head_emb,
    head_state,
    tail_emb,
    tail_state,
    relation_emb,
    head_rows,
    relations,
    tail_offsets,
    tail_owner,
    tail_local,
    block_count,
    neg_blocks,
):
    owned, span, width = tail_emb.shape
    group = span // HEAD
    head_t, tail_t = head_emb.T, tail_emb.transpose(0, 2, 1)
    table, query, rel_vec = gather_table(tail_t, head_t, relation_emb.T, head_rows, relations)
    head_new, head_state_new, block_part, neg_part = run_edges(
        tail_owner.reshape(-1),
        tail_local,
        neg_blocks,
        block_count,
        table.reshape(TAIL * owned, width, span),
        query,
        rel_vec,
        head_t,
        head_state[None, :],
        head_rows,
        tail_offsets,
    )
    fresh = run_exchange(
        neg_blocks,
        block_part,
        neg_part.reshape(SIDE, SIDE, DEPTH // 2, 2, group, width),
        tail_t,
        tail_state,
    )
    fresh = fresh.reshape(owned, span, LANES)
    pieces = fresh[:, :, width : width + 3].astype(F32)
    tail_state_new = (pieces[..., 0] + pieces[..., 1]) + pieces[..., 2]
    return (head_new.T, head_state_new[0], fresh[:, :, :width], tail_state_new)


def solution(mesh):
    placed = (
        P(("head", "tail"), None),
        P(("head", "tail")),
        P("tail", None, None),
        P("tail", None),
        P(),
        P(("head", "tail"), None),
        P(("head", "tail"), None),
        P(("head", "tail"), None),
        P(("head", "tail"), None),
        P(("head", "tail")),
        P(("head", "tail")),
        P(),
    )
    return jax.shard_map(
        per_device,
        mesh=mesh,
        in_specs=placed,
        out_specs=(
            P(("head", "tail"), None),
            P(("head", "tail")),
            P("tail", None, None),
            P("tail", None),
        ),
        check_vma=False,
    )
```

```python
import jax
import jax.numpy as jnp
from jax import lax
from jax.experimental import pallas as pl
from jax.experimental.pallas import tpu as pltpu
from jax.sharding import PartitionSpec as P

LEARN_RATE = 0.3
MESH = pl.DeviceIdType.MESH
F32 = jnp.float32
BF16 = jnp.bfloat16
SIDE = 4
DEPTH = 8
HEAD = 16
TAIL = 16
LANES = 896
VMEM_BYTES = 64 << 20


def greet(targets):
    barrier = pltpu.get_barrier_semaphore()
    for target in targets:
        pl.semaphore_signal(barrier, inc=1, device_id=target, device_id_type=MESH)
    pl.semaphore_wait(barrier, len(targets))


TN = (((0,), (0,)), ((), ()))
NT = (((1,), (1,)), ((), ()))


def mm(left, right, dims=(((1,), (0,)), ((), ()))):
    return lax.dot_general(left, right, dims, preferred_element_type=F32)


def one_hot(count, index_row):
    spots = lax.broadcasted_iota(jnp.int32, (count, index_row.shape[1]), 0)
    return jnp.where(spots == index_row, 1.0, 0.0).astype(BF16)


def table_gather(
    own,
    head_hbm,
    rel_hbm,
    head_rows_hbm,
    relations_hbm,
    table,
    query_out,
    rel_out,
    head_t,
    rel_t,
    head_rows,
    relations,
    query,
    rel_vec,
    send1,
    recv1,
    send2,
    recv2,
    send3,
    recv3,
    local,
):
    head, tail = lax.axis_index("head"), lax.axis_index("tail")
    core, col, row = lax.rem(head, 2), lax.rem(tail, SIDE), lax.div(tail, SIDE)
    sibling = (head + 1 - 2 * core, tail)
    size = own.shape[1]
    everything = (0, size)
    first, second = (0, size // 2), (size // 2, size // 2)
    blocks = query.shape[0]

    loads = [
        pltpu.make_async_copy(head_hbm, head_t, local.at[0]),
        pltpu.make_async_copy(rel_hbm, rel_t, local.at[1]),
        pltpu.make_async_copy(own, table.at[tail], local.at[2]),
        pltpu.make_async_copy(head_rows_hbm, head_rows, local.at[3 + 2 * blocks]),
        pltpu.make_async_copy(relations_hbm, relations, local.at[4 + 2 * blocks]),
    ]
    for load in loads:
        load.start()

    def place(which, along, across):
        dx, dy = (along, across) if which == 0 else (across, along)
        return lax.rem(row + dy + SIDE, SIDE) * SIDE + lax.rem(col + dx + SIDE, SIDE)

    greet(
        [sibling]
        + [(head, place(0, 1, 0)), (head, place(0, -1, 0))]
        + [(head, place(1, 1, 0)), (head, place(1, -1, 0))]
    )

    def copy(which, origin, part, sems, spot, target):
        block = 2 * core + which
        start, count = part
        here = table.at[place(which, *origin), block, pl.ds(start, count)]
        source = own.at[block, pl.ds(start, count)] if origin == (0, 0) else here
        return pltpu.make_async_remote_copy(
            src_ref=source,
            dst_ref=here,
            send_sem=sems[0].at[which, spot],
            recv_sem=sems[1].at[which, spot],
            device_id=target,
            device_id_type=MESH,
        )

    def landing(which, origin, part, sems, spot, block=None):
        block = 2 * core + which if block is None else block
        start, count = part
        here = table.at[place(which, *origin), block, pl.ds(start, count)]
        return pltpu.make_async_remote_copy(
            src_ref=here,
            dst_ref=here,
            send_sem=sems[0].at[which, spot],
            recv_sem=sems[1].at[which, spot],
            device_id=sibling,
            device_id_type=MESH,
        )

    stage1, stage2, stage3 = (send1, recv1), (send2, recv2), (send3, recv3)
    sent = []

    def send(*description):
        transfer = copy(*description)
        transfer.start()
        sent.append(transfer)

    def spread(which, origin):
        spot = (origin[0] % SIDE) * 4
        send(which, origin, everything, stage2, spot, (head, place(which, 0, 1)))
        send(which, origin, everything, stage2, spot + 1, (head, place(which, 0, -1)))

    def share(which, origin):
        spot = (origin[0] % SIDE) * 4 + origin[1] % SIDE
        send(which, origin, everything, stage3, spot, sibling)

    stores = []

    def make_query(b):
        half = size // 2
        vec = mm(head_t[...], one_hot(head_t.shape[1], head_rows[b : b + 1, :]))
        rel = mm(rel_t[...], one_hot(rel_t.shape[1], relations[b : b + 1, :]))
        rel_vec[b] = rel.astype(BF16)
        query[b, :half] = (vec[:half] * rel[:half] - vec[half:] * rel[half:]).astype(BF16)
        query[b, half:] = (vec[:half] * rel[half:] + vec[half:] * rel[:half]).astype(BF16)
        for value, target, spot in ((query, query_out, 3), (rel_vec, rel_out, 3 + blocks)):
            store = pltpu.make_async_copy(value.at[b], target.at[b], local.at[spot + b])
            store.start()
            stores.append(store)

    for which in (0, 1):
        send(which, (0, 0), everything, stage1, 0, (head, place(which, 1, 0)))
        send(which, (0, 0), everything, stage1, 1, (head, place(which, -1, 0)))
    for which in (0, 1):
        spread(which, (0, 0))
    for n in (0, 1, 3, 4):
        loads[n].wait()
    make_query(0)
    for which in (0, 1):
        landing(which, (-1, 0), everything, stage1, 0).wait_recv()
        send(which, (-1, 0), first, stage1, 2, (head, place(which, 1, 0)))
        spread(which, (-1, 0))
        share(which, (-1, 0))
        landing(which, (1, 0), everything, stage1, 1).wait_recv()
        send(which, (1, 0), second, stage1, 3, (head, place(which, -1, 0)))
        spread(which, (1, 0))
        share(which, (1, 0))
    for b in range(1, blocks - 1):
        make_query(b)
    for which in (0, 1):
        landing(which, (2, 0), first, stage1, 2).wait_recv()
        landing(which, (2, 0), second, stage1, 3).wait_recv()
        spread(which, (2, 0))
        share(which, (2, 0))
    for along in (0, -1, 1, 2):
        spot = (along % SIDE) * 4
        for which in (0, 1):
            landing(which, (along, -1), everything, stage2, spot).wait_recv()
            send(which, (along, -1), first, stage2, spot + 2, (head, place(which, 0, 1)))
            share(which, (along, -1))
            landing(which, (along, 1), everything, stage2, spot + 1).wait_recv()
            send(which, (along, 1), second, stage2, spot + 3, (head, place(which, 0, -1)))
            share(which, (along, 1))
        if along == 0:
            make_query(blocks - 1)
    for along in (0, -1, 1, 2):
        spot = (along % SIDE) * 4
        for which in (0, 1):
            landing(which, (along, 2), first, stage2, spot + 2).wait_recv()
            landing(which, (along, 2), second, stage2, spot + 3).wait_recv()
            share(which, (along, 2))
    for which in (0, 1):
        for along in range(SIDE):
            for across in range(SIDE):
                if (along, across) != (0, 0):
                    block = 2 * (1 - core) + which
                    spot = along * 4 + across
                    landing(which, (along, across), everything, stage3, spot, block).wait_recv()
    loads[2].wait()
    for store in stores:
        store.wait()
    for transfer in sent:
        transfer.wait_send()


def gather_table(tail_t, head_t, rel_t, head_rows, relations):
    blocks, edges = head_rows.shape
    width = head_t.shape[0]
    sems = pltpu.SemaphoreType.DMA
    anywhere = pl.BlockSpec(memory_space=pl.ANY)
    return pl.pallas_call(
        table_gather,
        out_shape=(
            jax.ShapeDtypeStruct((TAIL,) + tail_t.shape, BF16),
            jax.ShapeDtypeStruct((blocks, width, edges), BF16),
            jax.ShapeDtypeStruct((blocks, width, edges), BF16),
        ),
        in_specs=[pl.BlockSpec(memory_space=pltpu.HBM)] * 5,
        out_specs=(anywhere, anywhere, anywhere),
        scratch_shapes=[
            pltpu.VMEM(head_t.shape, BF16),
            pltpu.VMEM(rel_t.shape, BF16),
            pltpu.VMEM(head_rows.shape, jnp.int32),
            pltpu.VMEM(relations.shape, jnp.int32),
            pltpu.VMEM((blocks, width, edges), BF16),
            pltpu.VMEM((blocks, width, edges), BF16),
            sems((2, 4)),
            sems((2, 4)),
            sems((2, 16)),
            sems((2, 16)),
            sems((2, 16)),
            sems((2, 16)),
            sems((5 + 2 * blocks,)),
        ],
        compiler_params=pltpu.CompilerParams(
            collective_id=0, has_side_effects=True, vmem_limit_bytes=VMEM_BYTES
        ),
    )(tail_t, head_t, rel_t, head_rows, relations)


def edge_work(
    owners,
    locals_,
    neg_ids,
    live_count,
    table,
    query_hbm,
    rel_hbm,
    offsets,
    block_out,
    prob_out,
    grad_out,
    chosen,
    neg_t,
    negs,
    query_all,
    rel_all,
    prob,
    grad,
    sems,
):
    blocks, edges = offsets.shape
    width = neg_t.shape[0]
    half = width // 2
    owned = table.shape[0] // TAIL
    span = chosen.shape[2]
    group = span // HEAD
    neg_count = neg_ids.shape[0]

    fetches = []
    for k in range(neg_count):
        lanes = pl.ds(k * span, span)
        fetches.append(pltpu.make_async_copy(table.at[neg_ids[k]], neg_t.at[:, lanes], sems.at[k]))
    for b in range(blocks):
        block = owners[b] * owned + locals_[b]
        spot = neg_count + 3 * b
        fetches.append(pltpu.make_async_copy(query_hbm.at[b], query_all.at[b], sems.at[spot]))
        fetches.append(pltpu.make_async_copy(table.at[block], chosen.at[b], sems.at[spot + 1]))
        fetches.append(pltpu.make_async_copy(rel_hbm.at[b], rel_all.at[b], sems.at[spot + 2]))
    for fetch in fetches:
        fetch.start()
    for k in range(neg_count):
        fetches[k].wait()
        negs[k * span : (k + 1) * span, :] = neg_t[:, k * span : (k + 1) * span].T
    for fetch in fetches[neg_count:]:
        fetch.wait()

    def results(b):
        spot = neg_count + 3 * blocks
        return [
            pltpu.make_async_copy(prob.at[b], prob_out.at[b], sems.at[spot + b]),
            pltpu.make_async_copy(grad.at[b], grad_out.at[b], sems.at[spot + blocks + b]),
        ]

    def one_block(b, carry):
        live = jnp.where(b < live_count[0], 1.0, 0.0).astype(F32)
        pick = one_hot(span, offsets[pl.ds(b, 1), :])
        tail_vec = mm(chosen[b], pick)
        query = query_all[b].astype(F32)
        positive = jnp.sum(query * tail_vec, axis=0, keepdims=True)
        score = mm(negs[...], query_all[b])
        largest = jnp.maximum(positive, jnp.max(score, axis=0, keepdims=True))
        pos_exp = jnp.exp(positive - largest)
        neg_exp = jnp.exp(score - largest)
        denominator = pos_exp + jnp.sum(neg_exp, axis=0, keepdims=True)
        pos_grad = (pos_exp / denominator - 1.0) * live
        prob[b] = (neg_exp * (live / denominator)).astype(BF16)
        query_grad = pos_grad * tail_vec + mm(neg_t[...], prob[b])
        part = pos_grad * query
        part_a = part.astype(BF16)
        rest = part - part_a.astype(F32)
        part_b = rest.astype(BF16)
        part_c = (rest - part_b.astype(F32)).astype(BF16)
        block_grad = mm(pick, part_a, NT) + (mm(pick, part_b, NT) + mm(pick, part_c, NT))
        number = (owners[b] * owned + locals_[b]).astype(F32)
        for i in range(HEAD):
            block_out[i, b, :, :width] = block_grad[i * group : (i + 1) * group].astype(BF16)
            block_out[i, b, :, width:] = jnp.full((group, LANES - width), number, BF16)
        rel = rel_all[b].astype(F32)
        rr, ri = rel[:half], rel[half:]
        qr, qi = query_grad[:half], query_grad[half:]
        for start, change in ((0, qr * rr + qi * ri), (half, qi * rr - qr * ri)):
            change_hi = change.astype(BF16)
            grad[b, 0, start : start + half, :] = change_hi
            grad[b, 1, start : start + half, :] = (change - change_hi.astype(F32)).astype(BF16)
        for result in results(b):
            result.start()
        return carry

    lax.fori_loop(0, blocks, one_block, 0)
    for b in range(blocks):
        for result in results(b):
            result.wait()


def run_edges(owners, locals_, neg_ids, live_count, table, query, rel_vec, offsets):
    blocks, edges = offsets.shape
    width, span = table.shape[1:]
    negs = neg_ids.shape[0]
    smem = pl.BlockSpec(memory_space=pltpu.SMEM)
    vmem = pl.BlockSpec(memory_space=pltpu.VMEM)
    anywhere = pl.BlockSpec(memory_space=pl.ANY)
    return pl.pallas_call(
        edge_work,
        out_shape=(
            jax.ShapeDtypeStruct((HEAD, blocks, span // HEAD, LANES), BF16),
            jax.ShapeDtypeStruct((blocks, negs * span, edges), BF16),
            jax.ShapeDtypeStruct((blocks, 2, width, edges), BF16),
        ),
        in_specs=[smem, smem, smem, smem, anywhere, anywhere, anywhere, vmem],
        out_specs=(vmem, anywhere, anywhere),
        scratch_shapes=[
            pltpu.VMEM((blocks, width, span), BF16),
            pltpu.VMEM((width, negs * span), BF16),
            pltpu.VMEM((negs * span, width), BF16),
            pltpu.VMEM((blocks, width, edges), BF16),
            pltpu.VMEM((blocks, width, edges), BF16),
            pltpu.VMEM((blocks, negs * span, edges), BF16),
            pltpu.VMEM((blocks, 2, width, edges), BF16),
            pltpu.SemaphoreType.DMA((5 * blocks + negs,)),
        ],
        compiler_params=pltpu.CompilerParams(vmem_limit_bytes=VMEM_BYTES),
    )(owners, locals_, neg_ids, live_count, table, query, rel_vec, offsets)


def remote(source, target, send_sem, recv_sem, device):
    return pltpu.make_async_remote_copy(
        src_ref=source,
        dst_ref=target,
        send_sem=send_sem,
        recv_sem=recv_sem,
        device_id=device,
        device_id_type=MESH,
    )


class PlaneSum:
    def __init__(self, spread, in_x, in_y, mid_x, mid_y, end_x, end_y, sems):
        self.refs = (spread, in_x, in_y, mid_x, mid_y, end_x, end_y)
        self.sems = sems
        self.head, tail = lax.axis_index("head"), lax.axis_index("tail")
        self.col, self.row = lax.rem(tail, SIDE), lax.div(tail, SIDE)

    def steps(self):
        for step in range(1, SIDE):
            col = lax.rem(self.col + step, SIDE)
            row = lax.rem(self.row + step, SIDE)
            yield step - 1, col, row, (self.head, self.row * SIDE + col), (
                self.head,
                row * SIDE + self.col,
            )

    def first(self):
        spread, in_x, in_y = self.refs[:3]
        send, recv = self.sems
        copies = []
        for n, col, row, over_x, over_y in self.steps():
            copies.append(
                remote(spread.at[:, col, pl.ds(0, 2)], in_x.at[n], send.at[n], recv.at[n], over_x)
            )
            copies.append(
                remote(
                    spread.at[row, :, pl.ds(2, 2)], in_y.at[n], send.at[3 + n], recv.at[3 + n], over_y
                )
            )
        return copies

    def second(self):
        mid_x, mid_y, end_x, end_y = self.refs[3:]
        send, recv = self.sems
        copies = []
        for n, col, row, over_x, over_y in self.steps():
            copies.append(remote(mid_x.at[row], end_x.at[n], send.at[6 + n], recv.at[6 + n], over_y))
            copies.append(remote(mid_y.at[col], end_y.at[n], send.at[9 + n], recv.at[9 + n], over_x))
        return copies

    def start_first(self):
        for copy in self.first():
            copy.start()

    def start_second(self):
        spread, in_x, in_y, mid_x, mid_y = self.refs[:5]
        for copy in self.first():
            copy.wait_recv()
        for place in range(SIDE):
            for part in range(2):
                total = spread[place, self.col, part]
                other = spread[self.row, place, 2 + part]
                for n in range(SIDE - 1):
                    total = total + in_x[n, place, part]
                    other = other + in_y[n, place, part]
                mid_x[place, part] = total
                mid_y[place, part] = other
        for copy in self.second():
            copy.start()

    def result(self):
        mid_x, mid_y, end_x, end_y = self.refs[3:]
        for copy in self.second():
            copy.wait_recv()
        parts = []
        for part in range(2):
            total = mid_x[self.row, part]
            for n in range(SIDE - 1):
                total = total + end_x[n, part]
            parts.append(total)
        for part in range(2):
            total = mid_y[self.col, part]
            for n in range(SIDE - 1):
                total = total + end_y[n, part]
            parts.append(total)
        return parts

    def finish(self):
        for copy in self.first() + self.second():
            copy.wait_send()


def exchange(
    neg_ids,
    block_part,
    prob_hbm,
    query_hbm,
    grad_hbm,
    head_hbm,
    head_rows,
    head_state,
    own_t,
    own_state,
    out,
    head_new,
    state_new,
    prob,
    query,
    grad,
    head_emb,
    head_grad,
    hot_head,
    neg_part,
    slots,
    theirs,
    mine,
    neg_in_x,
    neg_in_y,
    neg_mid_x,
    neg_mid_y,
    neg_end_x,
    neg_end_y,
    deep,
    deep_in,
    neg_total,
    slot_rows,
    dense,
    in_x,
    in_y,
    mid_x,
    mid_y,
    end_x,
    end_y,
    update,
    sem_bs,
    sem_br,
    sem_cs,
    sem_cr,
    sem_ps,
    sem_pr,
    sem_zs,
    sem_zr,
    sem_ds,
    sem_dr,
    sem_us,
    sem_ur,
    sem_fs,
    sem_fr,
    sem_local,
):
    head, tail = lax.axis_index("head"), lax.axis_index("tail")
    core, depth = lax.rem(head, 2), lax.div(head, 2)
    other = head + 1 - 2 * core
    owned = own_t.shape[0]
    width = own_t.shape[1]
    group = slots.shape[2]
    quarter = DEPTH // 2

    def around(index, step, count):
        return lax.rem(index + step, count)

    keep_block = pltpu.make_async_copy(block_part.at[head], slots.at[head], sem_local.at[0])
    loads = [
        pltpu.make_async_copy(prob_hbm, prob, sem_local.at[1]),
        pltpu.make_async_copy(query_hbm, query, sem_local.at[3]),
        pltpu.make_async_copy(grad_hbm, grad, sem_local.at[4]),
        pltpu.make_async_copy(head_hbm, head_emb, sem_local.at[5]),
    ]
    for load in loads:
        load.start()
    keep_block.start()

    barrier = pltpu.get_barrier_semaphore()

    @pl.loop(1, HEAD)
    def _(step):
        pl.semaphore_signal(
            barrier, inc=1, device_id=(around(head, step, HEAD), tail), device_id_type=MESH
        )
        pl.semaphore_signal(
            barrier, inc=1, device_id=(head, around(tail, step, TAIL)), device_id_type=MESH
        )

    loads[0].wait()
    loads[1].wait()
    blocks = prob.shape[0]
    chunk = prob.shape[1] // SIDE

    @pl.loop(0, SIDE)
    def _(part):
        spots = pl.ds(pl.multiple_of(part * chunk, chunk), chunk)
        total = mm(prob[0, spots, :], query[0], NT)
        for b in range(1, blocks):
            total = total + mm(prob[b, spots, :], query[b], NT)
        neg_part[part] = total.reshape(neg_part.shape[1:])

    pl.semaphore_wait(barrier, HEAD + TAIL - 2)

    def pair_copy(part):
        return remote(
            neg_part.at[part, :, :, 1 - core],
            theirs.at[part],
            sem_cs.at[part],
            sem_cr.at[part],
            (other, tail),
        )

    for part in range(SIDE):
        pair_copy(part).start()

    def block_copy(step):
        peer = around(head, step, HEAD)
        return remote(
            block_part.at[peer], slots.at[head], sem_bs.at[step], sem_br.at[step], (peer, tail)
        )

    @pl.loop(1, HEAD)
    def _(step):
        block_copy(step).start()

    for part in range(SIDE):
        pair_copy(part).wait_recv()
        for place in range(SIDE):
            mine[part, place] = neg_part[part, place, :, core] + theirs[part, place]
    plane = PlaneSum(
        mine, neg_in_x, neg_in_y, neg_mid_x, neg_mid_y, neg_end_x, neg_end_y, (sem_ps, sem_pr)
    )
    plane.start_first()

    loads[2].wait()
    loads[3].wait()
    rows, edges = hot_head.shape[0], head_rows.shape[1]
    piece = 160
    for b in range(blocks):
        hot_head[:, b * edges : (b + 1) * edges] = one_hot(rows, head_rows[b : b + 1, :])

    def head_piece(p, squares):
        spots = pl.ds(pl.multiple_of(p * piece, piece), piece)
        gradient = jnp.zeros((piece, rows), F32)
        for b in range(blocks):
            lanes = slice(b * edges, (b + 1) * edges)
            for n in range(2):
                gradient = gradient + mm(grad[b, n, spots, :], hot_head[:, lanes], NT)
        head_grad[spots, :] = gradient
        return squares + jnp.sum(gradient * gradient, axis=0, keepdims=True)

    squares = lax.fori_loop(0, width // piece, head_piece, jnp.zeros((1, rows), F32))
    plane.start_second()
    head_next = head_state[...] + squares / width
    state_new[...] = head_next
    rate = LEARN_RATE / jnp.sqrt(head_next)

    @pl.loop(0, width // piece)
    def _(p):
        spots = pl.ds(pl.multiple_of(p * piece, piece), piece)
        head_emb[spots, :] = (head_emb[spots, :].astype(F32) - head_grad[spots, :] * rate).astype(
            BF16
        )

    head_store = pltpu.make_async_copy(head_emb, head_new, sem_local.at[6])
    head_store.start()
    for place, total in enumerate(plane.result()):
        deep[place] = total

    zone = lax.rem(tail, 2)
    takes = lax.div(depth, quarter) == zone

    def deep_copy(step):
        level = zone * quarter + step
        return remote(
            deep.at[step],
            deep_in.at[depth],
            sem_zs.at[step],
            sem_zr.at[depth],
            (level * 2 + core, tail),
        )

    def deep_landing(source):
        return remote(
            deep.at[0], deep_in.at[source], sem_zs.at[0], sem_zr.at[source], (other, tail)
        )

    @pl.loop(0, quarter)
    def _(step):
        @pl.when(zone * quarter + step != depth)
        def _():
            deep_copy(step).start()

    neg_total[...] = jnp.zeros_like(neg_total)

    keep_block.wait()

    @pl.loop(1, HEAD)
    def _(step):
        block_copy(step).wait_recv()

    @pl.loop(0, HEAD)
    def _(source):
        for b in range(owned):
            spot = pl.multiple_of((source * owned + b) * group, group)
            slot_rows[pl.ds(spot, group), :] = slots[source, b].astype(F32)

    count = HEAD * owned * group
    number = slot_rows[:, width : width + 1]
    inner = lax.broadcasted_iota(jnp.int32, (count, 1), 0) % group
    goal = number * group + inner.astype(F32)
    spots = lax.broadcasted_iota(jnp.int32, (count, count), 1).astype(F32)
    hot = jnp.where(spots == goal, 1.0, 0.0).astype(BF16)
    sums = mm(hot, slot_rows[:, :width].astype(BF16), TN)

    @pl.when(takes)
    def _():
        deep_in[depth] = deep[depth - zone * quarter]

        @pl.loop(0, DEPTH)
        def _(source):
            @pl.when(source != depth)
            def _():
                deep_landing(source).wait_recv()

        total = deep_in[0]
        for source in range(1, DEPTH):
            total = total + deep_in[source]
        neg_total[...] = total

    target = neg_ids[lax.div(tail, 2)]
    total = neg_total[...]
    for block in range(TAIL * owned):
        y, x, part = block // owned // SIDE, block // owned % SIDE, block % owned
        weight = jnp.where(target == block, 1.0, 0.0).astype(F32)
        dense[y, x, part] = sums[block * group : (block + 1) * group] + weight * total

    table = PlaneSum(dense, in_x, in_y, mid_x, mid_y, end_x, end_y, (sem_ds, sem_dr))
    table.start_first()
    lane = lax.broadcasted_iota(jnp.int32, (group, own_t.shape[2]), 1)
    mark = lane == head * group + lax.broadcasted_iota(jnp.int32, (group, own_t.shape[2]), 0)
    rows_now = [
        mm(jnp.where(mark, 1.0, 0.0).astype(BF16), own_t[b], NT) for b in range(owned)
    ]
    states_now = [
        jnp.sum(jnp.where(mark, own_state[b : b + 1, :], 0.0), axis=1, keepdims=True)
        for b in range(owned)
    ]
    table.start_second()

    for b, gradient in enumerate(table.result()):
        fresh = states_now[b] + jnp.sum(gradient * gradient, axis=1, keepdims=True) / width
        update[b, :, :width] = (
            rows_now[b] - gradient * (LEARN_RATE / jnp.sqrt(fresh))
        ).astype(BF16)
        spot = lax.broadcasted_iota(jnp.int32, (group, LANES - width), 1)
        fresh_a = fresh.astype(BF16).astype(F32)
        fresh_b = (fresh - fresh_a).astype(BF16).astype(F32)
        fresh_c = fresh - fresh_a - fresh_b
        pieces = jnp.where(spot == 0, fresh_a, jnp.where(spot == 1, fresh_b, fresh_c))
        update[b, :, width:] = pieces.astype(BF16)

    def rows_copy(step):
        peer = around(depth, step, DEPTH) * 2 + core
        return remote(update, out.at[:, head], sem_us.at[step], sem_ur.at[step], (peer, tail))

    @pl.loop(1, DEPTH)
    def _(step):
        rows_copy(step).start()

    out_own = pltpu.make_async_copy(update, out.at[:, head], sem_local.at[2])
    out_own.start()
    first_rows = remote(update, out.at[:, head], sem_fs.at[0], sem_fr.at[0], (other, tail))
    first_rows.start()

    def pass_rows(step):
        place = around(depth, DEPTH - step, DEPTH) * 2 + core
        return remote(
            out.at[:, place], out.at[:, place], sem_fs.at[step], sem_fr.at[step], (other, tail)
        )

    @pl.loop(1, DEPTH)
    def _(step):
        rows_copy(step).wait_recv()
        pass_rows(step).start()

    plane.finish()
    table.finish()
    for part in range(SIDE):
        pair_copy(part).wait_send()

    @pl.loop(1, HEAD)
    def _(step):
        block_copy(step).wait_send()

    @pl.loop(0, quarter)
    def _(step):
        @pl.when(zone * quarter + step != depth)
        def _():
            deep_copy(step).wait_send()

    out_own.wait()
    head_store.wait()
    first_rows.wait()

    @pl.loop(1, DEPTH)
    def _(step):
        pass_rows(step).wait()
        rows_copy(step).wait_send()


def run_exchange(
    neg_ids, block_part, prob, query, grad, head_t, head_rows, head_state, own_t, own_state
):
    rows = head_t.shape[1]
    total = head_rows.shape[0] * head_rows.shape[1]
    owned, width, span = own_t.shape
    group = span // HEAD
    quarter = DEPTH // 2
    sems = pltpu.SemaphoreType.DMA
    anywhere = pl.BlockSpec(memory_space=pl.ANY)
    vmem = pl.BlockSpec(memory_space=pltpu.VMEM)
    whole = pltpu.VMEM((SIDE, SIDE, 4, group, width), F32)
    plane_sum = (
        [pltpu.VMEM((SIDE - 1, SIDE, 2, group, width), F32)] * 2
        + [pltpu.VMEM((SIDE, 2, group, width), F32)] * 2
        + [pltpu.VMEM((SIDE - 1, 2, group, width), F32)] * 2
    )
    return pl.pallas_call(
        exchange,
        out_shape=(
            jax.ShapeDtypeStruct((owned, HEAD, group, LANES), BF16),
            jax.ShapeDtypeStruct(head_t.shape, BF16),
            jax.ShapeDtypeStruct((1, rows), F32),
        ),
        in_specs=[pl.BlockSpec(memory_space=pltpu.SMEM)]
        + [anywhere] * 4
        + [pl.BlockSpec(memory_space=pltpu.HBM)]
        + [vmem] * 4,
        out_specs=(anywhere, anywhere, vmem),
        scratch_shapes=[
            pltpu.VMEM(prob.shape, BF16),
            pltpu.VMEM(query.shape, BF16),
            pltpu.VMEM(grad.shape, BF16),
            pltpu.VMEM(head_t.shape, BF16),
            pltpu.VMEM(head_t.shape, F32),
            pltpu.VMEM((rows, total), BF16),
            pltpu.VMEM((SIDE, SIDE, 4, 2, group, width), F32),
            pltpu.VMEM((HEAD, owned, group, LANES), BF16),
            whole,
            whole,
            *plane_sum,
            pltpu.VMEM((quarter, group, width), F32),
            pltpu.VMEM((DEPTH, group, width), F32),
            pltpu.VMEM((group, width), F32),
            pltpu.VMEM((HEAD * owned * group, LANES), F32),
            whole,
            *plane_sum,
            pltpu.VMEM((owned, group, LANES), BF16),
            sems((HEAD,)),
            sems((HEAD,)),
            sems((SIDE,)),
            sems((SIDE,)),
            sems((12,)),
            sems((12,)),
            sems((quarter,)),
            sems((DEPTH,)),
            sems((12,)),
            sems((12,)),
            sems((DEPTH,)),
            sems((DEPTH,)),
            sems((DEPTH,)),
            sems((DEPTH,)),
            sems((7,)),
        ],
        compiler_params=pltpu.CompilerParams(
            collective_id=1, has_side_effects=True, vmem_limit_bytes=VMEM_BYTES
        ),
    )(neg_ids, block_part, prob, query, grad, head_t, head_rows, head_state, own_t, own_state)


def per_device(
    head_emb,
    head_state,
    tail_emb,
    tail_state,
    relation_emb,
    head_rows,
    relations,
    tail_offsets,
    tail_owner,
    tail_local,
    block_count,
    neg_blocks,
):
    owned, span, width = tail_emb.shape
    head_t, tail_t = head_emb.T, tail_emb.transpose(0, 2, 1)
    table, query, rel_vec = gather_table(tail_t, head_t, relation_emb.T, head_rows, relations)
    block_part, prob, grad = run_edges(
        tail_owner.reshape(-1),
        tail_local,
        neg_blocks,
        block_count,
        table.reshape(TAIL * owned, width, span),
        query,
        rel_vec,
        tail_offsets,
    )
    fresh, head_new, head_state_new = run_exchange(
        neg_blocks,
        block_part,
        prob,
        query,
        grad,
        head_t,
        head_rows,
        head_state[None, :],
        tail_t,
        tail_state,
    )
    fresh = fresh.reshape(owned, span, LANES)
    pieces = fresh[:, :, width : width + 3].astype(F32)
    tail_state_new = (pieces[..., 0] + pieces[..., 1]) + pieces[..., 2]
    return (head_new.T, head_state_new[0], fresh[:, :, :width], tail_state_new)


def solution(mesh):
    placed = (
        P(("head", "tail"), None),
        P(("head", "tail")),
        P("tail", None, None),
        P("tail", None),
        P(),
        P(("head", "tail"), None),
        P(("head", "tail"), None),
        P(("head", "tail"), None),
        P(("head", "tail"), None),
        P(("head", "tail")),
        P(("head", "tail")),
        P(),
    )
    return jax.shard_map(
        per_device,
        mesh=mesh,
        in_specs=placed,
        out_specs=(
            P(("head", "tail"), None),
            P(("head", "tail")),
            P("tail", None, None),
            P("tail", None),
        ),
        check_vma=False,
    )
```

```python
import jax
import jax.numpy as jnp
from jax import lax
from jax.experimental import pallas as pl
from jax.experimental.pallas import tpu as pltpu
from jax.sharding import PartitionSpec as P

LEARN_RATE = 0.3
MESH = pl.DeviceIdType.MESH
F32 = jnp.float32
BF16 = jnp.bfloat16
SIDE = 4
DEPTH = 8
HEAD = 16
TAIL = 16
CUT = 512
LANES = 896
VMEM_BYTES = 64 << 20


def greet(targets):
    barrier = pltpu.get_barrier_semaphore()
    for target in targets:
        pl.semaphore_signal(barrier, inc=1, device_id=target, device_id_type=MESH)
    pl.semaphore_wait(barrier, len(targets))


TN = (((0,), (0,)), ((), ()))
NT = (((1,), (1,)), ((), ()))


def mm(left, right, dims=(((1,), (0,)), ((), ()))):
    return lax.dot_general(left, right, dims, preferred_element_type=F32)


def one_hot(count, index_row):
    spots = lax.broadcasted_iota(jnp.int32, (count, index_row.shape[1]), 0)
    return jnp.where(spots == index_row, 1.0, 0.0).astype(BF16)


def table_gather(
    own,
    head_hbm,
    rel_hbm,
    head_rows_hbm,
    relations_hbm,
    table,
    query_out,
    rel_out,
    head_t,
    rel_t,
    head_rows,
    relations,
    query,
    rel_vec,
    send1,
    recv1,
    send2,
    recv2,
    send3,
    recv3,
    local,
):
    head, tail = lax.axis_index("head"), lax.axis_index("tail")
    core, col, row = lax.rem(head, 2), lax.rem(tail, SIDE), lax.div(tail, SIDE)
    sibling = (head + 1 - 2 * core, tail)
    size = own.shape[1]
    everything = (0, size)
    first, second = (0, size // 2), (size // 2, size // 2)
    blocks = query.shape[0]

    loads = [
        pltpu.make_async_copy(head_hbm, head_t, local.at[0]),
        pltpu.make_async_copy(rel_hbm, rel_t, local.at[1]),
        pltpu.make_async_copy(own, table.at[tail], local.at[2]),
        pltpu.make_async_copy(head_rows_hbm, head_rows, local.at[3 + 2 * blocks]),
        pltpu.make_async_copy(relations_hbm, relations, local.at[4 + 2 * blocks]),
    ]
    for load in loads:
        load.start()

    def place(which, along, across):
        dx, dy = (along, across) if which == 0 else (across, along)
        return lax.rem(row + dy + SIDE, SIDE) * SIDE + lax.rem(col + dx + SIDE, SIDE)

    greet(
        [sibling]
        + [(head, place(0, 1, 0)), (head, place(0, -1, 0))]
        + [(head, place(1, 1, 0)), (head, place(1, -1, 0))]
    )

    def copy(which, origin, part, sems, spot, target):
        block = 2 * core + which
        start, count = part
        here = table.at[place(which, *origin), block, pl.ds(start, count)]
        source = own.at[block, pl.ds(start, count)] if origin == (0, 0) else here
        return pltpu.make_async_remote_copy(
            src_ref=source,
            dst_ref=here,
            send_sem=sems[0].at[which, spot],
            recv_sem=sems[1].at[which, spot],
            device_id=target,
            device_id_type=MESH,
        )

    def landing(which, origin, part, sems, spot, block=None):
        block = 2 * core + which if block is None else block
        start, count = part
        here = table.at[place(which, *origin), block, pl.ds(start, count)]
        return pltpu.make_async_remote_copy(
            src_ref=here,
            dst_ref=here,
            send_sem=sems[0].at[which, spot],
            recv_sem=sems[1].at[which, spot],
            device_id=sibling,
            device_id_type=MESH,
        )

    stage1, stage2, stage3 = (send1, recv1), (send2, recv2), (send3, recv3)
    sent = []

    def send(*description):
        transfer = copy(*description)
        transfer.start()
        sent.append(transfer)

    def spread(which, origin):
        spot = (origin[0] % SIDE) * 4
        send(which, origin, everything, stage2, spot, (head, place(which, 0, 1)))
        send(which, origin, everything, stage2, spot + 1, (head, place(which, 0, -1)))

    def share(which, origin):
        spot = (origin[0] % SIDE) * 4 + origin[1] % SIDE
        send(which, origin, everything, stage3, spot, sibling)

    stores = []

    def make_query(b):
        half = size // 2
        vec = mm(head_t[...], one_hot(head_t.shape[1], head_rows[b : b + 1, :]))
        rel = mm(rel_t[...], one_hot(rel_t.shape[1], relations[b : b + 1, :]))
        rel_vec[b] = rel.astype(BF16)
        query[b, :half] = (vec[:half] * rel[:half] - vec[half:] * rel[half:]).astype(BF16)
        query[b, half:] = (vec[:half] * rel[half:] + vec[half:] * rel[:half]).astype(BF16)
        for value, target, spot in ((query, query_out, 3), (rel_vec, rel_out, 3 + blocks)):
            store = pltpu.make_async_copy(value.at[b], target.at[b], local.at[spot + b])
            store.start()
            stores.append(store)

    for which in (0, 1):
        send(which, (0, 0), everything, stage1, 0, (head, place(which, 1, 0)))
        send(which, (0, 0), everything, stage1, 1, (head, place(which, -1, 0)))
    for which in (0, 1):
        spread(which, (0, 0))
    for n in (0, 1, 3, 4):
        loads[n].wait()
    make_query(0)
    for which in (0, 1):
        landing(which, (-1, 0), everything, stage1, 0).wait_recv()
        send(which, (-1, 0), first, stage1, 2, (head, place(which, 1, 0)))
        spread(which, (-1, 0))
        share(which, (-1, 0))
        landing(which, (1, 0), everything, stage1, 1).wait_recv()
        send(which, (1, 0), second, stage1, 3, (head, place(which, -1, 0)))
        spread(which, (1, 0))
        share(which, (1, 0))
    for b in range(1, blocks - 1):
        make_query(b)
    for which in (0, 1):
        landing(which, (2, 0), first, stage1, 2).wait_recv()
        landing(which, (2, 0), second, stage1, 3).wait_recv()
        spread(which, (2, 0))
        share(which, (2, 0))
    for along in (0, -1, 1, 2):
        spot = (along % SIDE) * 4
        for which in (0, 1):
            landing(which, (along, -1), everything, stage2, spot).wait_recv()
            send(which, (along, -1), first, stage2, spot + 2, (head, place(which, 0, 1)))
            share(which, (along, -1))
            landing(which, (along, 1), everything, stage2, spot + 1).wait_recv()
            send(which, (along, 1), second, stage2, spot + 3, (head, place(which, 0, -1)))
            share(which, (along, 1))
        if along == 0:
            make_query(blocks - 1)
    for along in (0, -1, 1, 2):
        spot = (along % SIDE) * 4
        for which in (0, 1):
            landing(which, (along, 2), first, stage2, spot + 2).wait_recv()
            landing(which, (along, 2), second, stage2, spot + 3).wait_recv()
            share(which, (along, 2))
    for which in (0, 1):
        for along in range(SIDE):
            for across in range(SIDE):
                if (along, across) != (0, 0):
                    block = 2 * (1 - core) + which
                    spot = along * 4 + across
                    landing(which, (along, across), everything, stage3, spot, block).wait_recv()
    loads[2].wait()
    for store in stores:
        store.wait()
    for transfer in sent:
        transfer.wait_send()


def gather_table(tail_t, head_t, rel_t, head_rows, relations):
    blocks, edges = head_rows.shape
    width = head_t.shape[0]
    sems = pltpu.SemaphoreType.DMA
    anywhere = pl.BlockSpec(memory_space=pl.ANY)
    return pl.pallas_call(
        table_gather,
        out_shape=(
            jax.ShapeDtypeStruct((TAIL,) + tail_t.shape, BF16),
            jax.ShapeDtypeStruct((blocks, width, edges), BF16),
            jax.ShapeDtypeStruct((blocks, width, edges), BF16),
        ),
        in_specs=[pl.BlockSpec(memory_space=pltpu.HBM)] * 5,
        out_specs=(anywhere, anywhere, anywhere),
        scratch_shapes=[
            pltpu.VMEM(head_t.shape, BF16),
            pltpu.VMEM(rel_t.shape, BF16),
            pltpu.VMEM(head_rows.shape, jnp.int32),
            pltpu.VMEM(relations.shape, jnp.int32),
            pltpu.VMEM((blocks, width, edges), BF16),
            pltpu.VMEM((blocks, width, edges), BF16),
            sems((2, 4)),
            sems((2, 4)),
            sems((2, 16)),
            sems((2, 16)),
            sems((2, 16)),
            sems((2, 16)),
            sems((5 + 2 * blocks,)),
        ],
        compiler_params=pltpu.CompilerParams(
            collective_id=0, has_side_effects=True, vmem_limit_bytes=VMEM_BYTES
        ),
    )(tail_t, head_t, rel_t, head_rows, relations)


def pick_blocks(owners, locals_, neg_ids, table, chosen, neg_t, sems):
    owned = table.shape[0] // TAIL
    span = table.shape[2]
    copies = []
    for k in range(neg_ids.shape[0]):
        lanes = pl.ds(k * span, span)
        copies.append(pltpu.make_async_copy(table.at[neg_ids[k]], neg_t.at[:, lanes], sems.at[k]))
    for b in range(chosen.shape[0]):
        block = owners[b] * owned + locals_[b]
        spot = neg_ids.shape[0] + b
        copies.append(pltpu.make_async_copy(table.at[block], chosen.at[b], sems.at[spot]))
    for copy in copies:
        copy.start()
    for copy in copies:
        copy.wait()


def run_pick(owners, locals_, neg_ids, table):
    blocks, negs = owners.shape[0], neg_ids.shape[0]
    width, span = table.shape[1:]
    smem = pl.BlockSpec(memory_space=pltpu.SMEM)
    anywhere = pl.BlockSpec(memory_space=pl.ANY)
    return pl.pallas_call(
        pick_blocks,
        out_shape=(
            jax.ShapeDtypeStruct((blocks, width, span), BF16),
            jax.ShapeDtypeStruct((width, negs * span), BF16),
        ),
        in_specs=[smem, smem, smem, anywhere],
        out_specs=(anywhere, anywhere),
        scratch_shapes=[pltpu.SemaphoreType.DMA((blocks + negs,))],
        compiler_params=pltpu.CompilerParams(vmem_limit_bytes=VMEM_BYTES),
    )(owners, locals_, neg_ids, table)


def remote(source, target, send_sem, recv_sem, device):
    return pltpu.make_async_remote_copy(
        src_ref=source,
        dst_ref=target,
        send_sem=send_sem,
        recv_sem=recv_sem,
        device_id=device,
        device_id_type=MESH,
    )


class PlaneSum:
    def __init__(self, spread, in_x, in_y, mid_x, mid_y, end_x, end_y, sems):
        self.refs = (spread, in_x, in_y, mid_x, mid_y, end_x, end_y)
        self.sems = sems
        self.head, tail = lax.axis_index("head"), lax.axis_index("tail")
        self.col, self.row = lax.rem(tail, SIDE), lax.div(tail, SIDE)

    def steps(self):
        for step in range(1, SIDE):
            col = lax.rem(self.col + step, SIDE)
            row = lax.rem(self.row + step, SIDE)
            yield step - 1, col, row, (self.head, self.row * SIDE + col), (
                self.head,
                row * SIDE + self.col,
            )

    def first(self):
        spread, in_x, in_y = self.refs[:3]
        send, recv = self.sems
        copies = []
        for n, col, row, over_x, over_y in self.steps():
            copies.append(
                remote(spread.at[:, col, pl.ds(0, 2)], in_x.at[n], send.at[n], recv.at[n], over_x)
            )
            copies.append(
                remote(
                    spread.at[row, :, pl.ds(2, 2)], in_y.at[n], send.at[3 + n], recv.at[3 + n], over_y
                )
            )
        return copies

    def second(self):
        mid_x, mid_y, end_x, end_y = self.refs[3:]
        send, recv = self.sems
        copies = []
        for n, col, row, over_x, over_y in self.steps():
            copies.append(remote(mid_x.at[row], end_x.at[n], send.at[6 + n], recv.at[6 + n], over_y))
            copies.append(remote(mid_y.at[col], end_y.at[n], send.at[9 + n], recv.at[9 + n], over_x))
        return copies

    def start_first(self):
        for copy in self.first():
            copy.start()

    def start_second(self):
        spread, in_x, in_y, mid_x, mid_y = self.refs[:5]
        for copy in self.first():
            copy.wait_recv()
        for place in range(SIDE):
            for part in range(2):
                total = spread[place, self.col, part]
                other = spread[self.row, place, 2 + part]
                for n in range(SIDE - 1):
                    total = total + in_x[n, place, part]
                    other = other + in_y[n, place, part]
                mid_x[place, part] = total
                mid_y[place, part] = other
        for copy in self.second():
            copy.start()

    def result(self):
        mid_x, mid_y, end_x, end_y = self.refs[3:]
        for copy in self.second():
            copy.wait_recv()
        parts = []
        for part in range(2):
            total = mid_x[self.row, part]
            for n in range(SIDE - 1):
                total = total + end_x[n, part]
            parts.append(total)
        for part in range(2):
            total = mid_y[self.col, part]
            for n in range(SIDE - 1):
                total = total + end_y[n, part]
            parts.append(total)
        return parts

    def finish(self):
        for copy in self.first() + self.second():
            copy.wait_send()


def exchange(
    owners,
    locals_,
    live_count,
    neg_ids,
    chosen_hbm,
    neg_hbm,
    query_hbm,
    rel_hbm,
    head_hbm,
    offsets,
    head_rows,
    head_state,
    own_t,
    own_state,
    out,
    head_new,
    state_new,
    chosen,
    neg_t,
    negs,
    query,
    rel_all,
    prob,
    grad,
    block_part,
    head_emb,
    head_grad,
    hot_head,
    neg_part,
    slots,
    theirs,
    mine,
    neg_in_x,
    neg_in_y,
    neg_mid_x,
    neg_mid_y,
    neg_end_x,
    neg_end_y,
    deep,
    deep_in,
    neg_total,
    slot_rows,
    seats,
    lo,
    lo_in_x,
    lo_in_y,
    lo_mid_x,
    lo_mid_y,
    lo_end_x,
    lo_end_y,
    hi,
    hi_in_x,
    hi_in_y,
    hi_mid_x,
    hi_mid_y,
    hi_end_x,
    hi_end_y,
    update,
    sem_bs,
    sem_br,
    sem_cs,
    sem_cr,
    sem_ps,
    sem_pr,
    sem_zs,
    sem_zr,
    sem_ls,
    sem_lr,
    sem_hs,
    sem_hr,
    sem_ns,
    sem_nr,
    sem_us,
    sem_ur,
    sem_fs,
    sem_fr,
    sem_local,
):
    head, tail = lax.axis_index("head"), lax.axis_index("tail")
    core, depth = lax.rem(head, 2), lax.div(head, 2)
    other = head + 1 - 2 * core
    owned, width, span = own_t.shape
    group = slots.shape[2]
    quarter = DEPTH // 2
    blocks, edges = offsets.shape
    half = width // 2

    def around(index, step, count):
        return lax.rem(index + step, count)

    loads = [
        pltpu.make_async_copy(neg_hbm, neg_t, sem_local.at[0]),
        pltpu.make_async_copy(query_hbm, query, sem_local.at[1]),
        pltpu.make_async_copy(chosen_hbm, chosen, sem_local.at[2]),
        pltpu.make_async_copy(rel_hbm, rel_all, sem_local.at[3]),
        pltpu.make_async_copy(head_hbm, head_emb, sem_local.at[4]),
    ]
    for load in loads:
        load.start()

    barrier = pltpu.get_barrier_semaphore()

    @pl.loop(1, HEAD)
    def _(step):
        pl.semaphore_signal(
            barrier, inc=1, device_id=(around(head, step, HEAD), tail), device_id_type=MESH
        )
        pl.semaphore_signal(
            barrier, inc=1, device_id=(head, around(tail, step, TAIL)), device_id_type=MESH
        )

    loads[0].wait()
    for k in range(negs.shape[0] // span):
        negs[k * span : (k + 1) * span, :] = neg_t[:, k * span : (k + 1) * span].T
    for load in loads[1:]:
        load.wait()

    def edge_block(b):
        live = jnp.where(b < live_count[0], 1.0, 0.0).astype(F32)
        pick = one_hot(span, offsets[pl.ds(b, 1), :])
        tail_vec = mm(chosen[b], pick)
        queries = query[b].astype(F32)
        positive = jnp.sum(queries * tail_vec, axis=0, keepdims=True)
        score = mm(negs[...], query[b])
        largest = jnp.maximum(positive, jnp.max(score, axis=0, keepdims=True))
        pos_exp = jnp.exp(positive - largest)
        neg_exp = jnp.exp(score - largest)
        denominator = pos_exp + jnp.sum(neg_exp, axis=0, keepdims=True)
        pos_grad = (pos_exp / denominator - 1.0) * live
        part = pos_grad * queries
        part_a = part.astype(BF16)
        rest = part - part_a.astype(F32)
        part_b = rest.astype(BF16)
        part_c = (rest - part_b.astype(F32)).astype(BF16)
        block_grad = mm(pick, part_a, NT) + (mm(pick, part_b, NT) + mm(pick, part_c, NT))
        number = (owners[b] * owned + locals_[b]).astype(F32)
        for i in range(HEAD):
            block_part[i, b, :, :width] = block_grad[i * group : (i + 1) * group].astype(BF16)
            block_part[i, b, :, width:] = jnp.full((group, LANES - width), number, BF16)
        prob[b] = (neg_exp * (live / denominator)).astype(BF16)
        query_grad = pos_grad * tail_vec + mm(neg_t[...], prob[b])
        rel = rel_all[b].astype(F32)
        rr, ri = rel[:half], rel[half:]
        qr, qi = query_grad[:half], query_grad[half:]
        for start, change in ((0, qr * rr + qi * ri), (half, qi * rr - qr * ri)):
            change_hi = change.astype(BF16)
            grad[b, 0, start : start + half, :] = change_hi
            grad[b, 1, start : start + half, :] = (change - change_hi.astype(F32)).astype(BF16)

    early = blocks // 2
    pieces = (
        (pl.ds(0, early), pl.ds(0, LANES)),
        (pl.ds(early, blocks - early), pl.ds(CUT, LANES - CUT)),
        (pl.ds(early, blocks - early), pl.ds(0, CUT)),
    )

    def block_copy(piece, step):
        which, lanes = pieces[piece]
        peer = around(head, step, HEAD)
        return remote(
            block_part.at[peer, which, :, lanes],
            slots.at[head, which, :, lanes],
            sem_bs.at[piece, step],
            sem_br.at[piece, step],
            (peer, tail),
        )

    @pl.loop(0, early)
    def _(b):
        edge_block(b)

    pl.semaphore_wait(barrier, HEAD + TAIL - 2)

    @pl.loop(1, HEAD)
    def _(step):
        block_copy(0, step).start()

    @pl.loop(early, blocks)
    def _(b):
        edge_block(b)

    for piece in (1, 2):

        @pl.loop(1, HEAD)
        def _(step):
            block_copy(piece, step).start()

    keep_block = pltpu.make_async_copy(block_part.at[head], slots.at[head], sem_local.at[5])
    keep_block.start()

    def pair_copy(part):
        return remote(
            neg_part.at[part, :, :, 1 - core],
            theirs.at[part],
            sem_cs.at[part],
            sem_cr.at[part],
            (other, tail),
        )

    chunk = prob.shape[1] // SIDE

    @pl.loop(0, SIDE)
    def _(part):
        spots = pl.ds(pl.multiple_of(part * chunk, chunk), chunk)
        total = mm(prob[0, spots, :], query[0], NT)
        for b in range(1, blocks):
            total = total + mm(prob[b, spots, :], query[b], NT)
        neg_part[part] = total.reshape(neg_part.shape[1:])
        pair_copy(part).start()

    for part in range(SIDE):
        pair_copy(part).wait_recv()
        for place in range(SIDE):
            mine[part, place] = neg_part[part, place, :, core] + theirs[part, place]
    plane = PlaneSum(
        mine, neg_in_x, neg_in_y, neg_mid_x, neg_mid_y, neg_end_x, neg_end_y, (sem_ps, sem_pr)
    )
    plane.start_first()

    def spread_rows(piece):
        which, lanes = pieces[piece]

        @pl.loop(0, HEAD)
        def _(source):
            for b in range(which.start, which.start + which.size):
                spot = pl.multiple_of((source * owned + b) * group, group)
                slot_rows[pl.ds(spot, group), lanes] = slots[source, b, :, lanes].astype(F32)

    def arrive(piece):
        @pl.loop(1, HEAD)
        def _(step):
            block_copy(piece, step).wait_recv()

        if piece == 0:
            keep_block.wait()
        spread_rows(piece)

    def fill(dense, sums):
        for block in range(TAIL * owned):
            y, x, part = block // owned // SIDE, block // owned % SIDE, block % owned
            dense[y, x, part] = sums[block * group : (block + 1) * group]

    arrive(0)
    arrive(1)
    count = HEAD * owned * group
    number = slot_rows[:, width : width + 1]
    inner = lax.broadcasted_iota(jnp.int32, (count, 1), 0) % group
    goal = number * group + inner.astype(F32)
    places = lax.broadcasted_iota(jnp.int32, (count, count), 1).astype(F32)
    seats[...] = jnp.where(places == goal, 1.0, 0.0).astype(BF16).T
    fill(hi, mm(seats[...], slot_rows[:, CUT:width].astype(BF16)))
    high = PlaneSum(hi, hi_in_x, hi_in_y, hi_mid_x, hi_mid_y, hi_end_x, hi_end_y, (sem_hs, sem_hr))
    high.start_first()

    rows = hot_head.shape[0]
    piece_rows = 160
    for b in range(blocks):
        hot_head[:, b * edges : (b + 1) * edges] = one_hot(rows, head_rows[b : b + 1, :])

    def head_piece(p, squares):
        spots = pl.ds(pl.multiple_of(p * piece_rows, piece_rows), piece_rows)
        gradient = jnp.zeros((piece_rows, rows), F32)
        for b in range(blocks):
            lanes = slice(b * edges, (b + 1) * edges)
            for n in range(2):
                gradient = gradient + mm(grad[b, n, spots, :], hot_head[:, lanes], NT)
        head_grad[spots, :] = gradient
        return squares + jnp.sum(gradient * gradient, axis=0, keepdims=True)

    squares = lax.fori_loop(0, width // piece_rows, head_piece, jnp.zeros((1, rows), F32))

    arrive(2)
    fill(lo, mm(seats[...], slot_rows[:, :CUT].astype(BF16)))
    low = PlaneSum(lo, lo_in_x, lo_in_y, lo_mid_x, lo_mid_y, lo_end_x, lo_end_y, (sem_ls, sem_lr))
    low.start_first()
    plane.start_second()
    high.start_second()

    head_next = head_state[...] + squares / width
    state_new[...] = head_next
    rate = LEARN_RATE / jnp.sqrt(head_next)

    @pl.loop(0, width // piece_rows)
    def _(p):
        spots = pl.ds(pl.multiple_of(p * piece_rows, piece_rows), piece_rows)
        head_emb[spots, :] = (head_emb[spots, :].astype(F32) - head_grad[spots, :] * rate).astype(
            BF16
        )

    head_store = pltpu.make_async_copy(head_emb, head_new, sem_local.at[6])
    head_store.start()

    for place, total in enumerate(plane.result()):
        deep[place] = total

    zone = lax.rem(tail, 2)
    takes = lax.div(depth, quarter) == zone
    mine_k = lax.div(tail, 2)

    def deep_copy(step):
        level = zone * quarter + step
        return remote(
            deep.at[step],
            deep_in.at[depth],
            sem_zs.at[step],
            sem_zr.at[depth],
            (level * 2 + core, tail),
        )

    def deep_landing(source):
        return remote(
            deep.at[0], deep_in.at[source], sem_zs.at[0], sem_zr.at[source], (other, tail)
        )

    def total_copy(step):
        return remote(
            neg_total.at[mine_k],
            neg_total.at[mine_k],
            sem_ns.at[step],
            sem_nr.at[mine_k],
            (head, around(tail, step, TAIL)),
        )

    def total_landing(k):
        return remote(neg_total.at[k], neg_total.at[k], sem_ns.at[1], sem_nr.at[k], (other, tail))

    @pl.loop(0, quarter)
    def _(step):
        @pl.when(zone * quarter + step != depth)
        def _():
            deep_copy(step).start()

    low.start_second()
    lane = lax.broadcasted_iota(jnp.int32, (group, span), 1)
    mark = lane == head * group + lax.broadcasted_iota(jnp.int32, (group, span), 0)
    rows_now = [mm(jnp.where(mark, 1.0, 0.0).astype(BF16), own_t[b], NT) for b in range(owned)]
    states_now = [
        jnp.sum(jnp.where(mark, own_state[b : b + 1, :], 0.0), axis=1, keepdims=True)
        for b in range(owned)
    ]

    @pl.when(takes)
    def _():
        deep_in[depth] = deep[depth - zone * quarter]

        @pl.loop(0, DEPTH)
        def _(source):
            @pl.when(source != depth)
            def _():
                deep_landing(source).wait_recv()

        total = deep_in[0]
        for source in range(1, DEPTH):
            total = total + deep_in[source]
        neg_total[mine_k] = total

        @pl.loop(1, TAIL)
        def _(step):
            total_copy(step).start()

    high_sums, low_sums = high.result(), low.result()

    @pl.loop(0, neg_total.shape[0])
    def _(k):
        @pl.when(2 * k + lax.div(depth, quarter) != tail)
        def _():
            total_landing(k).wait_recv()

    for b in range(owned):
        low_part, high_part = low_sums[b], high_sums[b]
        for k in range(neg_total.shape[0]):
            weight = jnp.where(neg_ids[k] == tail * owned + b, 1.0, 0.0).astype(F32)
            low_part = low_part + weight * neg_total[k, :, :CUT]
            high_part = high_part + weight * neg_total[k, :, CUT:]
        squares = jnp.sum(low_part * low_part, axis=1, keepdims=True) + jnp.sum(
            high_part * high_part, axis=1, keepdims=True
        )
        fresh = states_now[b] + squares / width
        rate = LEARN_RATE / jnp.sqrt(fresh)
        update[b, :, :CUT] = (rows_now[b][:, :CUT] - low_part * rate).astype(BF16)
        update[b, :, CUT:width] = (rows_now[b][:, CUT:] - high_part * rate).astype(BF16)
        spot = lax.broadcasted_iota(jnp.int32, (group, LANES - width), 1)
        fresh_a = fresh.astype(BF16).astype(F32)
        fresh_b = (fresh - fresh_a).astype(BF16).astype(F32)
        fresh_c = fresh - fresh_a - fresh_b
        parts = jnp.where(spot == 0, fresh_a, jnp.where(spot == 1, fresh_b, fresh_c))
        update[b, :, width:] = parts.astype(BF16)

    def rows_copy(step):
        peer = around(depth, step, DEPTH) * 2 + core
        return remote(update, out.at[:, head], sem_us.at[step], sem_ur.at[step], (peer, tail))

    @pl.loop(1, DEPTH)
    def _(step):
        rows_copy(step).start()

    out_own = pltpu.make_async_copy(update, out.at[:, head], sem_local.at[7])
    out_own.start()
    first_rows = remote(update, out.at[:, head], sem_fs.at[0], sem_fr.at[0], (other, tail))
    first_rows.start()

    def pass_rows(step):
        place = around(depth, DEPTH - step, DEPTH) * 2 + core
        return remote(
            out.at[:, place], out.at[:, place], sem_fs.at[step], sem_fr.at[step], (other, tail)
        )

    plane.finish()
    high.finish()
    low.finish()
    for part in range(SIDE):
        pair_copy(part).wait_send()

    for piece in range(3):

        @pl.loop(1, HEAD)
        def _(step):
            block_copy(piece, step).wait_send()

    @pl.loop(0, quarter)
    def _(step):
        @pl.when(zone * quarter + step != depth)
        def _():
            deep_copy(step).wait_send()

    @pl.when(takes)
    def _():
        @pl.loop(1, TAIL)
        def _(step):
            total_copy(step).wait_send()

    head_store.wait()

    @pl.loop(1, DEPTH)
    def _(step):
        rows_copy(step).wait_recv()
        pass_rows(step).start()

    out_own.wait()
    first_rows.wait()

    @pl.loop(1, DEPTH)
    def _(step):
        pass_rows(step).wait()
        rows_copy(step).wait_send()


def run_exchange(
    owners,
    locals_,
    live_count,
    neg_ids,
    chosen,
    neg_t,
    query,
    rel_vec,
    head_t,
    offsets,
    head_rows,
    head_state,
    own_t,
    own_state,
):
    owned, width, span = own_t.shape
    blocks, edges = offsets.shape
    rows = head_t.shape[1]
    group = span // HEAD
    negs = neg_ids.shape[0]
    quarter = DEPTH // 2
    count = HEAD * owned * group
    sems = pltpu.SemaphoreType.DMA
    smem = pl.BlockSpec(memory_space=pltpu.SMEM)
    anywhere = pl.BlockSpec(memory_space=pl.ANY)
    vmem = pl.BlockSpec(memory_space=pltpu.VMEM)

    def plane_sum(columns):
        return [
            pltpu.VMEM((SIDE, SIDE, 4, group, columns), F32),
            *([pltpu.VMEM((SIDE - 1, SIDE, 2, group, columns), F32)] * 2),
            *([pltpu.VMEM((SIDE, 2, group, columns), F32)] * 2),
            *([pltpu.VMEM((SIDE - 1, 2, group, columns), F32)] * 2),
        ]

    return pl.pallas_call(
        exchange,
        out_shape=(
            jax.ShapeDtypeStruct((owned, HEAD, group, LANES), BF16),
            jax.ShapeDtypeStruct(head_t.shape, BF16),
            jax.ShapeDtypeStruct((1, rows), F32),
        ),
        in_specs=[smem] * 4 + [anywhere] * 5 + [vmem] * 5,
        out_specs=(anywhere, anywhere, vmem),
        scratch_shapes=[
            pltpu.VMEM(chosen.shape, BF16),
            pltpu.VMEM(neg_t.shape, BF16),
            pltpu.VMEM((negs * span, width), BF16),
            pltpu.VMEM(query.shape, BF16),
            pltpu.VMEM(rel_vec.shape, BF16),
            pltpu.VMEM((blocks, negs * span, edges), BF16),
            pltpu.VMEM((blocks, 2, width, edges), BF16),
            pltpu.VMEM((HEAD, blocks, group, LANES), BF16),
            pltpu.VMEM(head_t.shape, BF16),
            pltpu.VMEM(head_t.shape, F32),
            pltpu.VMEM((rows, blocks * edges), BF16),
            pltpu.VMEM((SIDE, SIDE, 4, 2, group, width), F32),
            pltpu.VMEM((HEAD, owned, group, LANES), BF16),
            pltpu.VMEM((SIDE, SIDE, 4, group, width), F32),
            *plane_sum(width),
            pltpu.VMEM((quarter, group, width), F32),
            pltpu.VMEM((DEPTH, group, width), F32),
            pltpu.VMEM((negs, group, width), F32),
            pltpu.VMEM((count, LANES), F32),
            pltpu.VMEM((count, count), BF16),
            *plane_sum(CUT),
            *plane_sum(width - CUT),
            pltpu.VMEM((owned, group, LANES), BF16),
            sems((3, HEAD)),
            sems((3, HEAD)),
            sems((SIDE,)),
            sems((SIDE,)),
            sems((12,)),
            sems((12,)),
            sems((quarter,)),
            sems((DEPTH,)),
            sems((12,)),
            sems((12,)),
            sems((12,)),
            sems((12,)),
            sems((TAIL,)),
            sems((negs,)),
            sems((DEPTH,)),
            sems((DEPTH,)),
            sems((DEPTH,)),
            sems((DEPTH,)),
            sems((8,)),
        ],
        compiler_params=pltpu.CompilerParams(
            collective_id=1, has_side_effects=True, vmem_limit_bytes=VMEM_BYTES
        ),
    )(
        owners,
        locals_,
        live_count,
        neg_ids,
        chosen,
        neg_t,
        query,
        rel_vec,
        head_t,
        offsets,
        head_rows,
        head_state,
        own_t,
        own_state,
    )


def per_device(
    head_emb,
    head_state,
    tail_emb,
    tail_state,
    relation_emb,
    head_rows,
    relations,
    tail_offsets,
    tail_owner,
    tail_local,
    block_count,
    neg_blocks,
):
    owned, span, width = tail_emb.shape
    head_t, tail_t = head_emb.T, tail_emb.transpose(0, 2, 1)
    table, query, rel_vec = gather_table(tail_t, head_t, relation_emb.T, head_rows, relations)
    owners = tail_owner.reshape(-1)
    chosen, neg_t = run_pick(
        owners, tail_local, neg_blocks, table.reshape(TAIL * owned, width, span)
    )
    fresh, head_new, head_state_new = run_exchange(
        owners,
        tail_local,
        block_count,
        neg_blocks,
        chosen,
        neg_t,
        query,
        rel_vec,
        head_t,
        tail_offsets,
        head_rows,
        head_state[None, :],
        tail_t,
        tail_state,
    )
    fresh = fresh.reshape(owned, span, LANES)
    pieces = fresh[:, :, width : width + 3].astype(F32)
    tail_state_new = (pieces[..., 0] + pieces[..., 1]) + pieces[..., 2]
    return (head_new.T, head_state_new[0], fresh[:, :, :width], tail_state_new)


def solution(mesh):
    placed = (
        P(("head", "tail"), None),
        P(("head", "tail")),
        P("tail", None, None),
        P("tail", None),
        P(),
        P(("head", "tail"), None),
        P(("head", "tail"), None),
        P(("head", "tail"), None),
        P(("head", "tail"), None),
        P(("head", "tail")),
        P(("head", "tail")),
        P(),
    )
    return jax.shard_map(
        per_device,
        mesh=mesh,
        in_specs=placed,
        out_specs=(
            P(("head", "tail"), None),
            P(("head", "tail")),
            P("tail", None, None),
            P("tail", None),
        ),
        check_vma=False,
    )
```

```python
import jax
import jax.numpy as jnp
from jax import lax
from jax.experimental import pallas as pl
from jax.experimental.pallas import tpu as pltpu
from jax.sharding import PartitionSpec as P

LEARN_RATE = 0.3
MESH = pl.DeviceIdType.MESH
F32 = jnp.float32
BF16 = jnp.bfloat16
SIDE = 4
DEPTH = 8
HEAD = 16
TAIL = 16
CUT = 512
LANES = 896
VMEM_BYTES = 64 << 20


def greet(targets):
    barrier = pltpu.get_barrier_semaphore()
    for target in targets:
        pl.semaphore_signal(barrier, inc=1, device_id=target, device_id_type=MESH)
    pl.semaphore_wait(barrier, len(targets))


TN = (((0,), (0,)), ((), ()))
NT = (((1,), (1,)), ((), ()))


def mm(left, right, dims=(((1,), (0,)), ((), ()))):
    return lax.dot_general(left, right, dims, preferred_element_type=F32)


def one_hot(count, index_row):
    spots = lax.broadcasted_iota(jnp.int32, (count, index_row.shape[1]), 0)
    return jnp.where(spots == index_row, 1.0, 0.0).astype(BF16)


def table_gather(
    own,
    head_hbm,
    rel_hbm,
    head_rows_hbm,
    relations_hbm,
    table,
    query_out,
    rel_out,
    head_t,
    rel_t,
    head_rows,
    relations,
    query,
    rel_vec,
    send1,
    recv1,
    send2,
    recv2,
    send3,
    recv3,
    local,
):
    head, tail = lax.axis_index("head"), lax.axis_index("tail")
    core, col, row = lax.rem(head, 2), lax.rem(tail, SIDE), lax.div(tail, SIDE)
    sibling = (head + 1 - 2 * core, tail)
    size = own.shape[1]
    everything = (0, size)
    first, second = (0, size // 2), (size // 2, size // 2)
    blocks = query.shape[0]

    loads = [
        pltpu.make_async_copy(head_hbm, head_t, local.at[0]),
        pltpu.make_async_copy(rel_hbm, rel_t, local.at[1]),
        pltpu.make_async_copy(own, table.at[tail], local.at[2]),
        pltpu.make_async_copy(head_rows_hbm, head_rows, local.at[3 + 2 * blocks]),
        pltpu.make_async_copy(relations_hbm, relations, local.at[4 + 2 * blocks]),
    ]
    for load in loads:
        load.start()

    def place(which, along, across):
        dx, dy = (along, across) if which == 0 else (across, along)
        return lax.rem(row + dy + SIDE, SIDE) * SIDE + lax.rem(col + dx + SIDE, SIDE)

    greet(
        [sibling]
        + [(head, place(0, 1, 0)), (head, place(0, -1, 0))]
        + [(head, place(1, 1, 0)), (head, place(1, -1, 0))]
    )

    def copy(which, origin, part, sems, spot, target):
        block = 2 * core + which
        start, count = part
        here = table.at[place(which, *origin), block, pl.ds(start, count)]
        source = own.at[block, pl.ds(start, count)] if origin == (0, 0) else here
        return pltpu.make_async_remote_copy(
            src_ref=source,
            dst_ref=here,
            send_sem=sems[0].at[which, spot],
            recv_sem=sems[1].at[which, spot],
            device_id=target,
            device_id_type=MESH,
        )

    def landing(which, origin, part, sems, spot, block=None):
        block = 2 * core + which if block is None else block
        start, count = part
        here = table.at[place(which, *origin), block, pl.ds(start, count)]
        return pltpu.make_async_remote_copy(
            src_ref=here,
            dst_ref=here,
            send_sem=sems[0].at[which, spot],
            recv_sem=sems[1].at[which, spot],
            device_id=sibling,
            device_id_type=MESH,
        )

    stage1, stage2, stage3 = (send1, recv1), (send2, recv2), (send3, recv3)
    sent = []

    def send(*description):
        transfer = copy(*description)
        transfer.start()
        sent.append(transfer)

    def spread(which, origin):
        spot = (origin[0] % SIDE) * 4
        send(which, origin, everything, stage2, spot, (head, place(which, 0, 1)))
        send(which, origin, everything, stage2, spot + 1, (head, place(which, 0, -1)))

    def share(which, origin):
        spot = (origin[0] % SIDE) * 4 + origin[1] % SIDE
        send(which, origin, everything, stage3, spot, sibling)

    stores = []

    def make_query(b):
        half = size // 2
        vec = mm(head_t[...], one_hot(head_t.shape[1], head_rows[b : b + 1, :]))
        rel = mm(rel_t[...], one_hot(rel_t.shape[1], relations[b : b + 1, :]))
        rel_vec[b] = rel.astype(BF16)
        query[b, :half] = (vec[:half] * rel[:half] - vec[half:] * rel[half:]).astype(BF16)
        query[b, half:] = (vec[:half] * rel[half:] + vec[half:] * rel[:half]).astype(BF16)
        for value, target, spot in ((query, query_out, 3), (rel_vec, rel_out, 3 + blocks)):
            store = pltpu.make_async_copy(value.at[b], target.at[b], local.at[spot + b])
            store.start()
            stores.append(store)

    for which in (0, 1):
        send(which, (0, 0), everything, stage1, 0, (head, place(which, 1, 0)))
        send(which, (0, 0), everything, stage1, 1, (head, place(which, -1, 0)))
    for which in (0, 1):
        spread(which, (0, 0))
    for n in (0, 1, 3, 4):
        loads[n].wait()
    make_query(0)
    for which in (0, 1):
        landing(which, (-1, 0), everything, stage1, 0).wait_recv()
        send(which, (-1, 0), first, stage1, 2, (head, place(which, 1, 0)))
        spread(which, (-1, 0))
        share(which, (-1, 0))
        landing(which, (1, 0), everything, stage1, 1).wait_recv()
        send(which, (1, 0), second, stage1, 3, (head, place(which, -1, 0)))
        spread(which, (1, 0))
        share(which, (1, 0))
    for b in range(1, blocks - 1):
        make_query(b)
    for which in (0, 1):
        landing(which, (2, 0), first, stage1, 2).wait_recv()
        landing(which, (2, 0), second, stage1, 3).wait_recv()
        spread(which, (2, 0))
        share(which, (2, 0))
    for along in (0, -1, 1, 2):
        spot = (along % SIDE) * 4
        for which in (0, 1):
            landing(which, (along, -1), everything, stage2, spot).wait_recv()
            send(which, (along, -1), first, stage2, spot + 2, (head, place(which, 0, 1)))
            share(which, (along, -1))
            landing(which, (along, 1), everything, stage2, spot + 1).wait_recv()
            send(which, (along, 1), second, stage2, spot + 3, (head, place(which, 0, -1)))
            share(which, (along, 1))
        if along == 0:
            make_query(blocks - 1)
    for along in (0, -1, 1, 2):
        spot = (along % SIDE) * 4
        for which in (0, 1):
            landing(which, (along, 2), first, stage2, spot + 2).wait_recv()
            landing(which, (along, 2), second, stage2, spot + 3).wait_recv()
            share(which, (along, 2))
    for which in (0, 1):
        for along in range(SIDE):
            for across in range(SIDE):
                if (along, across) != (0, 0):
                    block = 2 * (1 - core) + which
                    spot = along * 4 + across
                    landing(which, (along, across), everything, stage3, spot, block).wait_recv()
    loads[2].wait()
    for store in stores:
        store.wait()
    for transfer in sent:
        transfer.wait_send()


def gather_table(tail_t, head_t, rel_t, head_rows, relations):
    blocks, edges = head_rows.shape
    width = head_t.shape[0]
    sems = pltpu.SemaphoreType.DMA
    anywhere = pl.BlockSpec(memory_space=pl.ANY)
    return pl.pallas_call(
        table_gather,
        out_shape=(
            jax.ShapeDtypeStruct((TAIL,) + tail_t.shape, BF16),
            jax.ShapeDtypeStruct((blocks, width, edges), BF16),
            jax.ShapeDtypeStruct((blocks, width, edges), BF16),
        ),
        in_specs=[pl.BlockSpec(memory_space=pltpu.HBM)] * 5,
        out_specs=(anywhere, anywhere, anywhere),
        scratch_shapes=[
            pltpu.VMEM(head_t.shape, BF16),
            pltpu.VMEM(rel_t.shape, BF16),
            pltpu.VMEM(head_rows.shape, jnp.int32),
            pltpu.VMEM(relations.shape, jnp.int32),
            pltpu.VMEM((blocks, width, edges), BF16),
            pltpu.VMEM((blocks, width, edges), BF16),
            sems((2, 4)),
            sems((2, 4)),
            sems((2, 16)),
            sems((2, 16)),
            sems((2, 16)),
            sems((2, 16)),
            sems((5 + 2 * blocks,)),
        ],
        compiler_params=pltpu.CompilerParams(
            collective_id=0, has_side_effects=True, vmem_limit_bytes=VMEM_BYTES
        ),
    )(tail_t, head_t, rel_t, head_rows, relations)


def pick_blocks(owners, locals_, neg_ids, table, chosen, neg_t, sems):
    owned = table.shape[0] // TAIL
    span = table.shape[2]
    copies = []
    for k in range(neg_ids.shape[0]):
        lanes = pl.ds(k * span, span)
        copies.append(pltpu.make_async_copy(table.at[neg_ids[k]], neg_t.at[:, lanes], sems.at[k]))
    for b in range(chosen.shape[0]):
        block = owners[b] * owned + locals_[b]
        spot = neg_ids.shape[0] + b
        copies.append(pltpu.make_async_copy(table.at[block], chosen.at[b], sems.at[spot]))
    for copy in copies:
        copy.start()
    for copy in copies:
        copy.wait()


def run_pick(owners, locals_, neg_ids, table):
    blocks, negs = owners.shape[0], neg_ids.shape[0]
    width, span = table.shape[1:]
    smem = pl.BlockSpec(memory_space=pltpu.SMEM)
    vmem = pl.BlockSpec(memory_space=pltpu.VMEM)
    anywhere = pl.BlockSpec(memory_space=pl.ANY)
    return pl.pallas_call(
        pick_blocks,
        out_shape=(
            jax.ShapeDtypeStruct((blocks, width, span), BF16),
            jax.ShapeDtypeStruct((width, negs * span), BF16),
        ),
        in_specs=[smem, smem, smem, anywhere],
        out_specs=(vmem, vmem),
        scratch_shapes=[pltpu.SemaphoreType.DMA((blocks + negs,))],
        compiler_params=pltpu.CompilerParams(vmem_limit_bytes=VMEM_BYTES),
    )(owners, locals_, neg_ids, table)


def remote(source, target, send_sem, recv_sem, device):
    return pltpu.make_async_remote_copy(
        src_ref=source,
        dst_ref=target,
        send_sem=send_sem,
        recv_sem=recv_sem,
        device_id=device,
        device_id_type=MESH,
    )


class PlaneSum:
    def __init__(self, spread, in_x, in_y, mid_x, mid_y, end_x, end_y, sems):
        self.refs = (spread, in_x, in_y, mid_x, mid_y, end_x, end_y)
        self.sems = sems
        self.head, tail = lax.axis_index("head"), lax.axis_index("tail")
        self.col, self.row = lax.rem(tail, SIDE), lax.div(tail, SIDE)

    def steps(self):
        for step in range(1, SIDE):
            col = lax.rem(self.col + step, SIDE)
            row = lax.rem(self.row + step, SIDE)
            yield step - 1, col, row, (self.head, self.row * SIDE + col), (
                self.head,
                row * SIDE + self.col,
            )

    def first(self):
        spread, in_x, in_y = self.refs[:3]
        send, recv = self.sems
        copies = []
        for n, col, row, over_x, over_y in self.steps():
            copies.append(
                remote(spread.at[:, col, pl.ds(0, 2)], in_x.at[n], send.at[n], recv.at[n], over_x)
            )
            copies.append(
                remote(
                    spread.at[row, :, pl.ds(2, 2)], in_y.at[n], send.at[3 + n], recv.at[3 + n], over_y
                )
            )
        return copies

    def second(self):
        mid_x, mid_y, end_x, end_y = self.refs[3:]
        send, recv = self.sems
        copies = []
        for n, col, row, over_x, over_y in self.steps():
            copies.append(remote(mid_x.at[row], end_x.at[n], send.at[6 + n], recv.at[6 + n], over_y))
            copies.append(remote(mid_y.at[col], end_y.at[n], send.at[9 + n], recv.at[9 + n], over_x))
        return copies

    def start_first(self):
        for copy in self.first():
            copy.start()

    def start_second(self):
        spread, in_x, in_y, mid_x, mid_y = self.refs[:5]
        for copy in self.first():
            copy.wait_recv()
        for place in range(SIDE):
            for part in range(2):
                total = spread[place, self.col, part]
                other = spread[self.row, place, 2 + part]
                for n in range(SIDE - 1):
                    total = total + in_x[n, place, part]
                    other = other + in_y[n, place, part]
                mid_x[place, part] = total
                mid_y[place, part] = other
        for copy in self.second():
            copy.start()

    def result(self):
        mid_x, mid_y, end_x, end_y = self.refs[3:]
        for copy in self.second():
            copy.wait_recv()
        parts = []
        for part in range(2):
            total = mid_x[self.row, part]
            for n in range(SIDE - 1):
                total = total + end_x[n, part]
            parts.append(total)
        for part in range(2):
            total = mid_y[self.col, part]
            for n in range(SIDE - 1):
                total = total + end_y[n, part]
            parts.append(total)
        return parts

    def finish(self):
        for copy in self.first() + self.second():
            copy.wait_send()


def exchange(
    owners,
    locals_,
    live_count,
    neg_ids,
    chosen_hbm,
    neg_hbm,
    query_hbm,
    rel_hbm,
    head_hbm,
    offsets,
    head_rows,
    head_state,
    own_t,
    own_state,
    out,
    head_new,
    state_new,
    chosen,
    neg_t,
    negs,
    query,
    rel_all,
    prob,
    grad,
    block_part,
    head_emb,
    head_grad,
    hot_head,
    neg_part,
    slots,
    theirs,
    mine,
    neg_in_x,
    neg_in_y,
    neg_mid_x,
    neg_mid_y,
    neg_end_x,
    neg_end_y,
    deep,
    deep_in,
    neg_total,
    slot_rows,
    seats,
    lo,
    lo_in_x,
    lo_in_y,
    lo_mid_x,
    lo_mid_y,
    lo_end_x,
    lo_end_y,
    hi,
    hi_in_x,
    hi_in_y,
    hi_mid_x,
    hi_mid_y,
    hi_end_x,
    hi_end_y,
    update,
    sem_bs,
    sem_br,
    sem_cs,
    sem_cr,
    sem_ps,
    sem_pr,
    sem_zs,
    sem_zr,
    sem_ls,
    sem_lr,
    sem_hs,
    sem_hr,
    sem_ns,
    sem_nr,
    sem_us,
    sem_ur,
    sem_fs,
    sem_fr,
    sem_local,
):
    head, tail = lax.axis_index("head"), lax.axis_index("tail")
    core, depth = lax.rem(head, 2), lax.div(head, 2)
    other = head + 1 - 2 * core
    owned, width, span = own_t.shape
    group = slots.shape[2]
    quarter = DEPTH // 2
    blocks, edges = offsets.shape
    half = width // 2

    def around(index, step, count):
        return lax.rem(index + step, count)

    loads = [
        pltpu.make_async_copy(neg_hbm, neg_t, sem_local.at[0]),
        pltpu.make_async_copy(query_hbm, query, sem_local.at[1]),
        pltpu.make_async_copy(chosen_hbm, chosen, sem_local.at[2]),
        pltpu.make_async_copy(rel_hbm, rel_all, sem_local.at[3]),
        pltpu.make_async_copy(head_hbm, head_emb, sem_local.at[4]),
    ]
    for load in loads:
        load.start()

    barrier = pltpu.get_barrier_semaphore()

    @pl.loop(1, HEAD)
    def _(step):
        pl.semaphore_signal(
            barrier, inc=1, device_id=(around(head, step, HEAD), tail), device_id_type=MESH
        )
        pl.semaphore_signal(
            barrier, inc=1, device_id=(head, around(tail, step, TAIL)), device_id_type=MESH
        )

    loads[0].wait()
    for k in range(negs.shape[0] // span):
        negs[k * span : (k + 1) * span, :] = neg_t[:, k * span : (k + 1) * span].T
    for load in loads[1:]:
        load.wait()

    def edge_block(b):
        live = jnp.where(b < live_count[0], 1.0, 0.0).astype(F32)
        pick = one_hot(span, offsets[pl.ds(b, 1), :])
        tail_vec = mm(chosen[b], pick)
        queries = query[b].astype(F32)
        positive = jnp.sum(queries * tail_vec, axis=0, keepdims=True)
        score = mm(negs[...], query[b])
        largest = jnp.maximum(positive, jnp.max(score, axis=0, keepdims=True))
        pos_exp = jnp.exp(positive - largest)
        neg_exp = jnp.exp(score - largest)
        denominator = pos_exp + jnp.sum(neg_exp, axis=0, keepdims=True)
        pos_grad = (pos_exp / denominator - 1.0) * live
        part = pos_grad * queries
        part_a = part.astype(BF16)
        rest = part - part_a.astype(F32)
        part_b = rest.astype(BF16)
        part_c = (rest - part_b.astype(F32)).astype(BF16)
        block_grad = mm(pick, part_a, NT) + (mm(pick, part_b, NT) + mm(pick, part_c, NT))
        number = (owners[b] * owned + locals_[b]).astype(F32)
        for i in range(HEAD):
            block_part[i, b, :, :width] = block_grad[i * group : (i + 1) * group].astype(BF16)
            block_part[i, b, :, width:] = jnp.full((group, LANES - width), number, BF16)
        prob[b] = (neg_exp * (live / denominator)).astype(BF16)
        query_grad = pos_grad * tail_vec + mm(neg_t[...], prob[b])
        rel = rel_all[b].astype(F32)
        rr, ri = rel[:half], rel[half:]
        qr, qi = query_grad[:half], query_grad[half:]
        for start, change in ((0, qr * rr + qi * ri), (half, qi * rr - qr * ri)):
            change_hi = change.astype(BF16)
            grad[b, 0, start : start + half, :] = change_hi
            grad[b, 1, start : start + half, :] = (change - change_hi.astype(F32)).astype(BF16)

    early = blocks // 2
    pieces = (
        (pl.ds(0, early), pl.ds(0, LANES)),
        (pl.ds(early, blocks - early), pl.ds(CUT, LANES - CUT)),
        (pl.ds(early, blocks - early), pl.ds(0, CUT)),
    )

    def block_copy(piece, step):
        which, lanes = pieces[piece]
        peer = around(head, step, HEAD)
        return remote(
            block_part.at[peer, which, :, lanes],
            slots.at[head, which, :, lanes],
            sem_bs.at[piece, step],
            sem_br.at[piece, step],
            (peer, tail),
        )

    @pl.loop(0, early)
    def _(b):
        edge_block(b)

    pl.semaphore_wait(barrier, HEAD + TAIL - 2)

    @pl.loop(1, HEAD)
    def _(step):
        block_copy(0, step).start()

    @pl.loop(early, blocks)
    def _(b):
        edge_block(b)

    for piece in (1, 2):

        @pl.loop(1, HEAD)
        def _(step):
            block_copy(piece, step).start()

    keep_block = pltpu.make_async_copy(block_part.at[head], slots.at[head], sem_local.at[5])
    keep_block.start()

    def pair_copy(part):
        return remote(
            neg_part.at[part, :, :, 1 - core],
            theirs.at[part],
            sem_cs.at[part],
            sem_cr.at[part],
            (other, tail),
        )

    chunk = prob.shape[1] // SIDE

    @pl.loop(0, SIDE)
    def _(part):
        spots = pl.ds(pl.multiple_of(part * chunk, chunk), chunk)
        total = mm(prob[0, spots, :], query[0], NT)
        for b in range(1, blocks):
            total = total + mm(prob[b, spots, :], query[b], NT)
        neg_part[part] = total.reshape(neg_part.shape[1:])
        pair_copy(part).start()

    for part in range(SIDE):
        pair_copy(part).wait_recv()
        for place in range(SIDE):
            mine[part, place] = neg_part[part, place, :, core] + theirs[part, place]
    plane = PlaneSum(
        mine, neg_in_x, neg_in_y, neg_mid_x, neg_mid_y, neg_end_x, neg_end_y, (sem_ps, sem_pr)
    )
    plane.start_first()

    def spread_rows(piece):
        which, lanes = pieces[piece]

        @pl.loop(0, HEAD)
        def _(source):
            for b in range(which.start, which.start + which.size):
                spot = pl.multiple_of((source * owned + b) * group, group)
                slot_rows[pl.ds(spot, group), lanes] = slots[source, b, :, lanes].astype(F32)

    def arrive(piece):
        @pl.loop(1, HEAD)
        def _(step):
            block_copy(piece, step).wait_recv()

        if piece == 0:
            keep_block.wait()
        spread_rows(piece)

    def fill(dense, sums):
        for block in range(TAIL * owned):
            y, x, part = block // owned // SIDE, block // owned % SIDE, block % owned
            dense[y, x, part] = sums[block * group : (block + 1) * group]

    arrive(0)
    arrive(1)
    count = HEAD * owned * group
    number = slot_rows[:, width : width + 1]
    inner = lax.broadcasted_iota(jnp.int32, (count, 1), 0) % group
    goal = number * group + inner.astype(F32)
    places = lax.broadcasted_iota(jnp.int32, (count, count), 1).astype(F32)
    seats[...] = jnp.where(places == goal, 1.0, 0.0).astype(BF16).T
    fill(hi, mm(seats[...], slot_rows[:, CUT:width].astype(BF16)))
    high = PlaneSum(hi, hi_in_x, hi_in_y, hi_mid_x, hi_mid_y, hi_end_x, hi_end_y, (sem_hs, sem_hr))
    high.start_first()
    plane.start_second()

    rows = hot_head.shape[0]
    piece_rows = 160
    for b in range(blocks):
        hot_head[:, b * edges : (b + 1) * edges] = one_hot(rows, head_rows[b : b + 1, :])

    def head_piece(p, squares):
        spots = pl.ds(pl.multiple_of(p * piece_rows, piece_rows), piece_rows)
        gradient = jnp.zeros((piece_rows, rows), F32)
        for b in range(blocks):
            lanes = slice(b * edges, (b + 1) * edges)
            for n in range(2):
                gradient = gradient + mm(grad[b, n, spots, :], hot_head[:, lanes], NT)
        head_grad[spots, :] = gradient
        return squares + jnp.sum(gradient * gradient, axis=0, keepdims=True)

    squares = lax.fori_loop(0, width // piece_rows, head_piece, jnp.zeros((1, rows), F32))

    for place, total in enumerate(plane.result()):
        deep[place] = total

    zone = lax.rem(tail, 2)
    takes = lax.div(depth, quarter) == zone
    mine_k = lax.div(tail, 2)

    def deep_copy(step):
        level = zone * quarter + step
        return remote(
            deep.at[step],
            deep_in.at[depth],
            sem_zs.at[step],
            sem_zr.at[depth],
            (level * 2 + core, tail),
        )

    def deep_landing(source):
        return remote(
            deep.at[0], deep_in.at[source], sem_zs.at[0], sem_zr.at[source], (other, tail)
        )

    def total_copy(step):
        return remote(
            neg_total.at[mine_k],
            neg_total.at[mine_k],
            sem_ns.at[step],
            sem_nr.at[mine_k],
            (head, around(tail, step, TAIL)),
        )

    def total_landing(k):
        return remote(neg_total.at[k], neg_total.at[k], sem_ns.at[1], sem_nr.at[k], (other, tail))

    @pl.loop(0, quarter)
    def _(step):
        @pl.when(zone * quarter + step != depth)
        def _():
            deep_copy(step).start()

    arrive(2)
    fill(lo, mm(seats[...], slot_rows[:, :CUT].astype(BF16)))
    low = PlaneSum(lo, lo_in_x, lo_in_y, lo_mid_x, lo_mid_y, lo_end_x, lo_end_y, (sem_ls, sem_lr))
    low.start_first()
    @pl.when(takes)
    def _():
        deep_in[depth] = deep[depth - zone * quarter]

        @pl.loop(0, DEPTH)
        def _(source):
            @pl.when(source != depth)
            def _():
                deep_landing(source).wait_recv()

        total = deep_in[0]
        for source in range(1, DEPTH):
            total = total + deep_in[source]
        neg_total[mine_k] = total

        @pl.loop(1, TAIL)
        def _(step):
            total_copy(step).start()

    high.start_second()

    head_next = head_state[...] + squares / width
    state_new[...] = head_next
    rate = LEARN_RATE / jnp.sqrt(head_next)

    @pl.loop(0, width // piece_rows)
    def _(p):
        spots = pl.ds(pl.multiple_of(p * piece_rows, piece_rows), piece_rows)
        head_emb[spots, :] = (head_emb[spots, :].astype(F32) - head_grad[spots, :] * rate).astype(
            BF16
        )

    head_store = pltpu.make_async_copy(head_emb, head_new, sem_local.at[6])
    head_store.start()

    lane = lax.broadcasted_iota(jnp.int32, (group, span), 1)
    mark = lane == head * group + lax.broadcasted_iota(jnp.int32, (group, span), 0)
    rows_now = [mm(jnp.where(mark, 1.0, 0.0).astype(BF16), own_t[b], NT) for b in range(owned)]
    states_now = [
        jnp.sum(jnp.where(mark, own_state[b : b + 1, :], 0.0), axis=1, keepdims=True)
        for b in range(owned)
    ]

    low.start_second()
    high_sums, low_sums = high.result(), low.result()

    @pl.loop(0, neg_total.shape[0])
    def _(k):
        @pl.when(2 * k + lax.div(depth, quarter) != tail)
        def _():
            total_landing(k).wait_recv()

    for b in range(owned):
        low_part, high_part = low_sums[b], high_sums[b]
        for k in range(neg_total.shape[0]):
            weight = jnp.where(neg_ids[k] == tail * owned + b, 1.0, 0.0).astype(F32)
            low_part = low_part + weight * neg_total[k, :, :CUT]
            high_part = high_part + weight * neg_total[k, :, CUT:]
        squares = jnp.sum(low_part * low_part, axis=1, keepdims=True) + jnp.sum(
            high_part * high_part, axis=1, keepdims=True
        )
        fresh = states_now[b] + squares / width
        rate = LEARN_RATE / jnp.sqrt(fresh)
        update[b, :, :CUT] = (rows_now[b][:, :CUT] - low_part * rate).astype(BF16)
        update[b, :, CUT:width] = (rows_now[b][:, CUT:] - high_part * rate).astype(BF16)
        spot = lax.broadcasted_iota(jnp.int32, (group, LANES - width), 1)
        fresh_a = fresh.astype(BF16).astype(F32)
        fresh_b = (fresh - fresh_a).astype(BF16).astype(F32)
        fresh_c = fresh - fresh_a - fresh_b
        parts = jnp.where(spot == 0, fresh_a, jnp.where(spot == 1, fresh_b, fresh_c))
        update[b, :, width:] = parts.astype(BF16)

    def rows_copy(step):
        peer = around(depth, step, DEPTH) * 2 + core
        return remote(update, out.at[:, head], sem_us.at[step], sem_ur.at[step], (peer, tail))

    @pl.loop(1, DEPTH)
    def _(step):
        rows_copy(step).start()

    out_own = pltpu.make_async_copy(update, out.at[:, head], sem_local.at[7])
    out_own.start()
    first_rows = remote(update, out.at[:, head], sem_fs.at[0], sem_fr.at[0], (other, tail))
    first_rows.start()

    def pass_rows(step):
        place = around(depth, DEPTH - step, DEPTH) * 2 + core
        return remote(
            out.at[:, place], out.at[:, place], sem_fs.at[step], sem_fr.at[step], (other, tail)
        )

    plane.finish()
    high.finish()
    low.finish()
    for part in range(SIDE):
        pair_copy(part).wait_send()

    for piece in range(3):

        @pl.loop(1, HEAD)
        def _(step):
            block_copy(piece, step).wait_send()

    @pl.loop(0, quarter)
    def _(step):
        @pl.when(zone * quarter + step != depth)
        def _():
            deep_copy(step).wait_send()

    @pl.when(takes)
    def _():
        @pl.loop(1, TAIL)
        def _(step):
            total_copy(step).wait_send()

    head_store.wait()

    @pl.loop(1, DEPTH)
    def _(step):
        rows_copy(step).wait_recv()
        pass_rows(step).start()

    out_own.wait()
    first_rows.wait()

    @pl.loop(1, DEPTH)
    def _(step):
        pass_rows(step).wait()
        rows_copy(step).wait_send()


def run_exchange(
    owners,
    locals_,
    live_count,
    neg_ids,
    chosen,
    neg_t,
    query,
    rel_vec,
    head_t,
    offsets,
    head_rows,
    head_state,
    own_t,
    own_state,
):
    owned, width, span = own_t.shape
    blocks, edges = offsets.shape
    rows = head_t.shape[1]
    group = span // HEAD
    negs = neg_ids.shape[0]
    quarter = DEPTH // 2
    count = HEAD * owned * group
    sems = pltpu.SemaphoreType.DMA
    smem = pl.BlockSpec(memory_space=pltpu.SMEM)
    anywhere = pl.BlockSpec(memory_space=pl.ANY)
    vmem = pl.BlockSpec(memory_space=pltpu.VMEM)

    def plane_sum(columns):
        return [
            pltpu.VMEM((SIDE, SIDE, 4, group, columns), F32),
            *([pltpu.VMEM((SIDE - 1, SIDE, 2, group, columns), F32)] * 2),
            *([pltpu.VMEM((SIDE, 2, group, columns), F32)] * 2),
            *([pltpu.VMEM((SIDE - 1, 2, group, columns), F32)] * 2),
        ]

    return pl.pallas_call(
        exchange,
        out_shape=(
            jax.ShapeDtypeStruct((owned, HEAD, group, LANES), BF16),
            jax.ShapeDtypeStruct(head_t.shape, BF16),
            jax.ShapeDtypeStruct((1, rows), F32),
        ),
        in_specs=[smem] * 4 + [anywhere] * 5 + [vmem] * 5,
        out_specs=(anywhere, anywhere, vmem),
        scratch_shapes=[
            pltpu.VMEM(chosen.shape, BF16),
            pltpu.VMEM(neg_t.shape, BF16),
            pltpu.VMEM((negs * span, width), BF16),
            pltpu.VMEM(query.shape, BF16),
            pltpu.VMEM(rel_vec.shape, BF16),
            pltpu.VMEM((blocks, negs * span, edges), BF16),
            pltpu.VMEM((blocks, 2, width, edges), BF16),
            pltpu.VMEM((HEAD, blocks, group, LANES), BF16),
            pltpu.VMEM(head_t.shape, BF16),
            pltpu.VMEM(head_t.shape, F32),
            pltpu.VMEM((rows, blocks * edges), BF16),
            pltpu.VMEM((SIDE, SIDE, 4, 2, group, width), F32),
            pltpu.VMEM((HEAD, owned, group, LANES), BF16),
            pltpu.VMEM((SIDE, SIDE, 4, group, width), F32),
            *plane_sum(width),
            pltpu.VMEM((quarter, group, width), F32),
            pltpu.VMEM((DEPTH, group, width), F32),
            pltpu.VMEM((negs, group, width), F32),
            pltpu.VMEM((count, LANES), F32),
            pltpu.VMEM((count, count), BF16),
            *plane_sum(CUT),
            *plane_sum(width - CUT),
            pltpu.VMEM((owned, group, LANES), BF16),
            sems((3, HEAD)),
            sems((3, HEAD)),
            sems((SIDE,)),
            sems((SIDE,)),
            sems((12,)),
            sems((12,)),
            sems((quarter,)),
            sems((DEPTH,)),
            sems((12,)),
            sems((12,)),
            sems((12,)),
            sems((12,)),
            sems((TAIL,)),
            sems((negs,)),
            sems((DEPTH,)),
            sems((DEPTH,)),
            sems((DEPTH,)),
            sems((DEPTH,)),
            sems((8,)),
        ],
        compiler_params=pltpu.CompilerParams(
            collective_id=1, has_side_effects=True, vmem_limit_bytes=VMEM_BYTES
        ),
    )(
        owners,
        locals_,
        live_count,
        neg_ids,
        chosen,
        neg_t,
        query,
        rel_vec,
        head_t,
        offsets,
        head_rows,
        head_state,
        own_t,
        own_state,
    )


def per_device(
    head_emb,
    head_state,
    tail_emb,
    tail_state,
    relation_emb,
    head_rows,
    relations,
    tail_offsets,
    tail_owner,
    tail_local,
    block_count,
    neg_blocks,
):
    owned, span, width = tail_emb.shape
    head_t, tail_t = head_emb.T, tail_emb.transpose(0, 2, 1)
    table, query, rel_vec = gather_table(tail_t, head_t, relation_emb.T, head_rows, relations)
    owners = tail_owner.reshape(-1)
    chosen, neg_t = run_pick(
        owners, tail_local, neg_blocks, table.reshape(TAIL * owned, width, span)
    )
    fresh, head_new, head_state_new = run_exchange(
        owners,
        tail_local,
        block_count,
        neg_blocks,
        chosen,
        neg_t,
        query,
        rel_vec,
        head_t,
        tail_offsets,
        head_rows,
        head_state[None, :],
        tail_t,
        tail_state,
    )
    fresh = fresh.reshape(owned, span, LANES)
    pieces = fresh[:, :, width : width + 3].astype(F32)
    tail_state_new = (pieces[..., 0] + pieces[..., 1]) + pieces[..., 2]
    return (head_new.T, head_state_new[0], fresh[:, :, :width], tail_state_new)


def solution(mesh):
    placed = (
        P(("head", "tail"), None),
        P(("head", "tail")),
        P("tail", None, None),
        P("tail", None),
        P(),
        P(("head", "tail"), None),
        P(("head", "tail"), None),
        P(("head", "tail"), None),
        P(("head", "tail"), None),
        P(("head", "tail")),
        P(("head", "tail")),
        P(),
    )
    return jax.shard_map(
        per_device,
        mesh=mesh,
        in_specs=placed,
        out_specs=(
            P(("head", "tail"), None),
            P(("head", "tail")),
            P("tail", None, None),
            P("tail", None),
        ),
        check_vma=False,
    )
```

```python
import jax
import jax.numpy as jnp
from jax import lax
from jax.experimental import pallas as pl
from jax.experimental.pallas import tpu as pltpu
from jax.sharding import PartitionSpec as P

LEARN_RATE = 0.3
MESH = pl.DeviceIdType.MESH
F32 = jnp.float32
BF16 = jnp.bfloat16
SIDE = 4
DEPTH = 8
HEAD = 16
TAIL = 16
CUT = 512
LANES = 896
VMEM_BYTES = 64 << 20


def greet(targets):
    barrier = pltpu.get_barrier_semaphore()
    for target in targets:
        pl.semaphore_signal(barrier, inc=1, device_id=target, device_id_type=MESH)
    pl.semaphore_wait(barrier, len(targets))


TN = (((0,), (0,)), ((), ()))
NT = (((1,), (1,)), ((), ()))


def mm(left, right, dims=(((1,), (0,)), ((), ()))):
    return lax.dot_general(left, right, dims, preferred_element_type=F32)


def one_hot(count, index_row):
    spots = lax.broadcasted_iota(jnp.int32, (count, index_row.shape[1]), 0)
    return jnp.where(spots == index_row, 1.0, 0.0).astype(BF16)


def table_gather(
    owners,
    locals_,
    neg_ids,
    own,
    head_hbm,
    rel_hbm,
    head_rows_hbm,
    relations_hbm,
    query_out,
    rel_out,
    chosen_out,
    neg_out,
    table,
    chosen,
    neg_t,
    head_t,
    rel_t,
    head_rows,
    relations,
    query,
    rel_vec,
    send1,
    recv1,
    send2,
    recv2,
    send3,
    recv3,
    local,
):
    head, tail = lax.axis_index("head"), lax.axis_index("tail")
    core, col, row = lax.rem(head, 2), lax.rem(tail, SIDE), lax.div(tail, SIDE)
    sibling = (head + 1 - 2 * core, tail)
    size = own.shape[1]
    owned, span = own.shape[0], own.shape[2]
    everything = (0, size)
    first, second = (0, size // 2), (size // 2, size // 2)
    blocks = query.shape[0]

    loads = [
        pltpu.make_async_copy(head_hbm, head_t, local.at[0]),
        pltpu.make_async_copy(rel_hbm, rel_t, local.at[1]),
        pltpu.make_async_copy(own, table.at[pl.ds(tail * owned, owned)], local.at[2]),
        pltpu.make_async_copy(head_rows_hbm, head_rows, local.at[3 + 2 * blocks]),
        pltpu.make_async_copy(relations_hbm, relations, local.at[4 + 2 * blocks]),
    ]
    for load in loads:
        load.start()

    def place(which, along, across):
        dx, dy = (along, across) if which == 0 else (across, along)
        return lax.rem(row + dy + SIDE, SIDE) * SIDE + lax.rem(col + dx + SIDE, SIDE)

    greet(
        [sibling]
        + [(head, place(0, 1, 0)), (head, place(0, -1, 0))]
        + [(head, place(1, 1, 0)), (head, place(1, -1, 0))]
    )

    def copy(which, origin, part, sems, spot, target):
        block = 2 * core + which
        start, count = part
        here = table.at[place(which, *origin) * owned + block, pl.ds(start, count)]
        source = own.at[block, pl.ds(start, count)] if origin == (0, 0) else here
        return pltpu.make_async_remote_copy(
            src_ref=source,
            dst_ref=here,
            send_sem=sems[0].at[which, spot],
            recv_sem=sems[1].at[which, spot],
            device_id=target,
            device_id_type=MESH,
        )

    def landing(which, origin, part, sems, spot, block=None):
        block = 2 * core + which if block is None else block
        start, count = part
        here = table.at[place(which, *origin) * owned + block, pl.ds(start, count)]
        return pltpu.make_async_remote_copy(
            src_ref=here,
            dst_ref=here,
            send_sem=sems[0].at[which, spot],
            recv_sem=sems[1].at[which, spot],
            device_id=sibling,
            device_id_type=MESH,
        )

    stage1, stage2, stage3 = (send1, recv1), (send2, recv2), (send3, recv3)
    sent = []

    def send(*description):
        transfer = copy(*description)
        transfer.start()
        sent.append(transfer)

    def spread(which, origin):
        spot = (origin[0] % SIDE) * 4
        send(which, origin, everything, stage2, spot, (head, place(which, 0, 1)))
        send(which, origin, everything, stage2, spot + 1, (head, place(which, 0, -1)))

    def share(which, origin):
        spot = (origin[0] % SIDE) * 4 + origin[1] % SIDE
        send(which, origin, everything, stage3, spot, sibling)

    stores = []

    def make_query(b):
        half = size // 2
        vec = mm(head_t[...], one_hot(head_t.shape[1], head_rows[b : b + 1, :]))
        rel = mm(rel_t[...], one_hot(rel_t.shape[1], relations[b : b + 1, :]))
        rel_vec[b] = rel.astype(BF16)
        query[b, :half] = (vec[:half] * rel[:half] - vec[half:] * rel[half:]).astype(BF16)
        query[b, half:] = (vec[:half] * rel[half:] + vec[half:] * rel[:half]).astype(BF16)
        for value, target, spot in ((query, query_out, 3), (rel_vec, rel_out, 3 + blocks)):
            store = pltpu.make_async_copy(value.at[b], target.at[b], local.at[spot + b])
            store.start()
            stores.append(store)

    for which in (0, 1):
        send(which, (0, 0), everything, stage1, 0, (head, place(which, 1, 0)))
        send(which, (0, 0), everything, stage1, 1, (head, place(which, -1, 0)))
    for which in (0, 1):
        spread(which, (0, 0))
    for n in (0, 1, 3, 4):
        loads[n].wait()
    make_query(0)
    for which in (0, 1):
        landing(which, (-1, 0), everything, stage1, 0).wait_recv()
        send(which, (-1, 0), first, stage1, 2, (head, place(which, 1, 0)))
        spread(which, (-1, 0))
        share(which, (-1, 0))
        landing(which, (1, 0), everything, stage1, 1).wait_recv()
        send(which, (1, 0), second, stage1, 3, (head, place(which, -1, 0)))
        spread(which, (1, 0))
        share(which, (1, 0))
    for b in range(1, blocks - 1):
        make_query(b)
    for which in (0, 1):
        landing(which, (2, 0), first, stage1, 2).wait_recv()
        landing(which, (2, 0), second, stage1, 3).wait_recv()
        spread(which, (2, 0))
        share(which, (2, 0))
    for along in (0, -1, 1, 2):
        spot = (along % SIDE) * 4
        for which in (0, 1):
            landing(which, (along, -1), everything, stage2, spot).wait_recv()
            send(which, (along, -1), first, stage2, spot + 2, (head, place(which, 0, 1)))
            share(which, (along, -1))
            landing(which, (along, 1), everything, stage2, spot + 1).wait_recv()
            send(which, (along, 1), second, stage2, spot + 3, (head, place(which, 0, -1)))
            share(which, (along, 1))
        if along == 0:
            make_query(blocks - 1)
    for along in (0, -1, 1, 2):
        spot = (along % SIDE) * 4
        for which in (0, 1):
            landing(which, (along, 2), first, stage2, spot + 2).wait_recv()
            landing(which, (along, 2), second, stage2, spot + 3).wait_recv()
            share(which, (along, 2))
    for which in (0, 1):
        for along in range(SIDE):
            for across in range(SIDE):
                if (along, across) != (0, 0):
                    block = 2 * (1 - core) + which
                    spot = along * 4 + across
                    landing(which, (along, across), everything, stage3, spot, block).wait_recv()
    loads[2].wait()
    for k in range(neg_ids.shape[0]):
        neg_t[:, k * span : (k + 1) * span] = table[neg_ids[k]]
    for b in range(blocks):
        chosen[b] = table[owners[b] * owned + locals_[b]]
    for n, (value, target) in enumerate(((neg_t, neg_out), (chosen, chosen_out))):
        store = pltpu.make_async_copy(value, target, local.at[5 + 2 * blocks + n])
        store.start()
        stores.append(store)
    for store in stores:
        store.wait()
    for transfer in sent:
        transfer.wait_send()


def gather_table(owners, locals_, neg_ids, tail_t, head_t, rel_t, head_rows, relations):
    owned, _, span = tail_t.shape
    negs = neg_ids.shape[0]
    blocks, edges = head_rows.shape
    width = head_t.shape[0]
    sems = pltpu.SemaphoreType.DMA
    anywhere = pl.BlockSpec(memory_space=pl.ANY)
    return pl.pallas_call(
        table_gather,
        out_shape=(
            jax.ShapeDtypeStruct((blocks, width, edges), BF16),
            jax.ShapeDtypeStruct((blocks, width, edges), BF16),
            jax.ShapeDtypeStruct((blocks, width, span), BF16),
            jax.ShapeDtypeStruct((width, negs * span), BF16),
        ),
        in_specs=[pl.BlockSpec(memory_space=pltpu.SMEM)] * 3
        + [pl.BlockSpec(memory_space=pltpu.HBM)] * 5,
        out_specs=(anywhere, anywhere, anywhere, anywhere),
        scratch_shapes=[
            pltpu.VMEM((TAIL * owned, width, span), BF16),
            pltpu.VMEM((blocks, width, span), BF16),
            pltpu.VMEM((width, negs * span), BF16),
            pltpu.VMEM(head_t.shape, BF16),
            pltpu.VMEM(rel_t.shape, BF16),
            pltpu.VMEM(head_rows.shape, jnp.int32),
            pltpu.VMEM(relations.shape, jnp.int32),
            pltpu.VMEM((blocks, width, edges), BF16),
            pltpu.VMEM((blocks, width, edges), BF16),
            sems((2, 4)),
            sems((2, 4)),
            sems((2, 16)),
            sems((2, 16)),
            sems((2, 16)),
            sems((2, 16)),
            sems((7 + 2 * blocks,)),
        ],
        compiler_params=pltpu.CompilerParams(
            collective_id=0, has_side_effects=True, vmem_limit_bytes=VMEM_BYTES
        ),
    )(owners, locals_, neg_ids, tail_t, head_t, rel_t, head_rows, relations)


def remote(source, target, send_sem, recv_sem, device):
    return pltpu.make_async_remote_copy(
        src_ref=source,
        dst_ref=target,
        send_sem=send_sem,
        recv_sem=recv_sem,
        device_id=device,
        device_id_type=MESH,
    )


class PlaneSum:
    def __init__(self, spread, in_x, in_y, mid_x, mid_y, end_x, end_y, sems):
        self.refs = (spread, in_x, in_y, mid_x, mid_y, end_x, end_y)
        self.sems = sems
        self.head, tail = lax.axis_index("head"), lax.axis_index("tail")
        self.col, self.row = lax.rem(tail, SIDE), lax.div(tail, SIDE)

    def steps(self):
        for step in range(1, SIDE):
            col = lax.rem(self.col + step, SIDE)
            row = lax.rem(self.row + step, SIDE)
            yield step - 1, col, row, (self.head, self.row * SIDE + col), (
                self.head,
                row * SIDE + self.col,
            )

    def first(self):
        spread, in_x, in_y = self.refs[:3]
        send, recv = self.sems
        copies = []
        for n, col, row, over_x, over_y in self.steps():
            copies.append(
                remote(spread.at[:, col, pl.ds(0, 2)], in_x.at[n], send.at[n], recv.at[n], over_x)
            )
            copies.append(
                remote(
                    spread.at[row, :, pl.ds(2, 2)], in_y.at[n], send.at[3 + n], recv.at[3 + n], over_y
                )
            )
        return copies

    def second(self):
        mid_x, mid_y, end_x, end_y = self.refs[3:]
        send, recv = self.sems
        copies = []
        for n, col, row, over_x, over_y in self.steps():
            copies.append(remote(mid_x.at[row], end_x.at[n], send.at[6 + n], recv.at[6 + n], over_y))
            copies.append(remote(mid_y.at[col], end_y.at[n], send.at[9 + n], recv.at[9 + n], over_x))
        return copies

    def start_first(self):
        for copy in self.first():
            copy.start()

    def start_second(self):
        spread, in_x, in_y, mid_x, mid_y = self.refs[:5]
        for copy in self.first():
            copy.wait_recv()
        for place in range(SIDE):
            for part in range(2):
                total = spread[place, self.col, part]
                other = spread[self.row, place, 2 + part]
                for n in range(SIDE - 1):
                    total = total + in_x[n, place, part]
                    other = other + in_y[n, place, part]
                mid_x[place, part] = total
                mid_y[place, part] = other
        for copy in self.second():
            copy.start()

    def result(self):
        mid_x, mid_y, end_x, end_y = self.refs[3:]
        for copy in self.second():
            copy.wait_recv()
        parts = []
        for part in range(2):
            total = mid_x[self.row, part]
            for n in range(SIDE - 1):
                total = total + end_x[n, part]
            parts.append(total)
        for part in range(2):
            total = mid_y[self.col, part]
            for n in range(SIDE - 1):
                total = total + end_y[n, part]
            parts.append(total)
        return parts

    def finish(self):
        for copy in self.first() + self.second():
            copy.wait_send()


def exchange(
    owners,
    locals_,
    live_count,
    neg_ids,
    chosen_hbm,
    neg_hbm,
    query_hbm,
    rel_hbm,
    head_hbm,
    offsets,
    head_rows,
    head_state,
    own_t,
    own_state,
    out,
    head_new,
    state_new,
    chosen,
    neg_t,
    negs,
    query,
    rel_all,
    prob,
    grad,
    block_part,
    head_emb,
    head_grad,
    hot_head,
    neg_part,
    slots,
    theirs,
    mine,
    neg_in_x,
    neg_in_y,
    neg_mid_x,
    neg_mid_y,
    neg_end_x,
    neg_end_y,
    deep,
    deep_in,
    neg_total,
    slot_rows,
    seats,
    lo,
    lo_in_x,
    lo_in_y,
    lo_mid_x,
    lo_mid_y,
    lo_end_x,
    lo_end_y,
    hi,
    hi_in_x,
    hi_in_y,
    hi_mid_x,
    hi_mid_y,
    hi_end_x,
    hi_end_y,
    update,
    sem_bs,
    sem_br,
    sem_cs,
    sem_cr,
    sem_ps,
    sem_pr,
    sem_zs,
    sem_zr,
    sem_ls,
    sem_lr,
    sem_hs,
    sem_hr,
    sem_ns,
    sem_nr,
    sem_us,
    sem_ur,
    sem_fs,
    sem_fr,
    sem_local,
):
    head, tail = lax.axis_index("head"), lax.axis_index("tail")
    core, depth = lax.rem(head, 2), lax.div(head, 2)
    other = head + 1 - 2 * core
    owned, width, span = own_t.shape
    group = slots.shape[2]
    quarter = DEPTH // 2
    blocks, edges = offsets.shape
    half = width // 2

    def around(index, step, count):
        return lax.rem(index + step, count)

    loads = [
        pltpu.make_async_copy(neg_hbm, neg_t, sem_local.at[0]),
        pltpu.make_async_copy(query_hbm, query, sem_local.at[1]),
        pltpu.make_async_copy(chosen_hbm, chosen, sem_local.at[2]),
        pltpu.make_async_copy(rel_hbm, rel_all, sem_local.at[3]),
        pltpu.make_async_copy(head_hbm, head_emb, sem_local.at[4]),
    ]
    for load in loads:
        load.start()

    barrier = pltpu.get_barrier_semaphore()

    @pl.loop(1, HEAD)
    def _(step):
        pl.semaphore_signal(
            barrier, inc=1, device_id=(around(head, step, HEAD), tail), device_id_type=MESH
        )
        pl.semaphore_signal(
            barrier, inc=1, device_id=(head, around(tail, step, TAIL)), device_id_type=MESH
        )

    loads[0].wait()
    for k in range(negs.shape[0] // span):
        negs[k * span : (k + 1) * span, :] = neg_t[:, k * span : (k + 1) * span].T
    for load in loads[1:]:
        load.wait()

    def edge_block(b):
        live = jnp.where(b < live_count[0], 1.0, 0.0).astype(F32)
        pick = one_hot(span, offsets[pl.ds(b, 1), :])
        tail_vec = mm(chosen[b], pick)
        queries = query[b].astype(F32)
        positive = jnp.sum(queries * tail_vec, axis=0, keepdims=True)
        score = mm(negs[...], query[b])
        largest = jnp.maximum(positive, jnp.max(score, axis=0, keepdims=True))
        pos_exp = jnp.exp(positive - largest)
        neg_exp = jnp.exp(score - largest)
        denominator = pos_exp + jnp.sum(neg_exp, axis=0, keepdims=True)
        pos_grad = (pos_exp / denominator - 1.0) * live
        part = pos_grad * queries
        part_a = part.astype(BF16)
        rest = part - part_a.astype(F32)
        part_b = rest.astype(BF16)
        part_c = (rest - part_b.astype(F32)).astype(BF16)
        block_grad = mm(pick, part_a, NT) + (mm(pick, part_b, NT) + mm(pick, part_c, NT))
        number = (owners[b] * owned + locals_[b]).astype(F32)
        for i in range(HEAD):
            block_part[i, b, :, :width] = block_grad[i * group : (i + 1) * group].astype(BF16)
            block_part[i, b, :, width:] = jnp.full((group, LANES - width), number, BF16)
        prob[b] = (neg_exp * (live / denominator)).astype(BF16)
        query_grad = pos_grad * tail_vec + mm(neg_t[...], prob[b])
        rel = rel_all[b].astype(F32)
        rr, ri = rel[:half], rel[half:]
        qr, qi = query_grad[:half], query_grad[half:]
        for start, change in ((0, qr * rr + qi * ri), (half, qi * rr - qr * ri)):
            change_hi = change.astype(BF16)
            grad[b, 0, start : start + half, :] = change_hi
            grad[b, 1, start : start + half, :] = (change - change_hi.astype(F32)).astype(BF16)

    early = blocks // 2
    pieces = (
        (pl.ds(0, early), pl.ds(0, LANES)),
        (pl.ds(early, blocks - early), pl.ds(CUT, LANES - CUT)),
        (pl.ds(early, blocks - early), pl.ds(0, CUT)),
    )

    def block_copy(piece, step):
        which, lanes = pieces[piece]
        peer = around(head, step, HEAD)
        return remote(
            block_part.at[peer, which, :, lanes],
            slots.at[head, which, :, lanes],
            sem_bs.at[piece, step],
            sem_br.at[piece, step],
            (peer, tail),
        )

    @pl.loop(0, early)
    def _(b):
        edge_block(b)

    pl.semaphore_wait(barrier, HEAD + TAIL - 2)

    @pl.loop(1, HEAD)
    def _(step):
        block_copy(0, step).start()

    @pl.loop(early, blocks)
    def _(b):
        edge_block(b)

    for piece in (1, 2):

        @pl.loop(1, HEAD)
        def _(step):
            block_copy(piece, step).start()

    keep_block = pltpu.make_async_copy(block_part.at[head], slots.at[head], sem_local.at[5])
    keep_block.start()

    def pair_copy(part):
        return remote(
            neg_part.at[part, :, :, 1 - core],
            theirs.at[part],
            sem_cs.at[part],
            sem_cr.at[part],
            (other, tail),
        )

    chunk = prob.shape[1] // SIDE

    @pl.loop(0, SIDE)
    def _(part):
        spots = pl.ds(pl.multiple_of(part * chunk, chunk), chunk)
        total = mm(prob[0, spots, :], query[0], NT)
        for b in range(1, blocks):
            total = total + mm(prob[b, spots, :], query[b], NT)
        neg_part[part] = total.reshape(neg_part.shape[1:])
        pair_copy(part).start()

    for part in range(SIDE):
        pair_copy(part).wait_recv()
        for place in range(SIDE):
            mine[part, place] = neg_part[part, place, :, core] + theirs[part, place]
    plane = PlaneSum(
        mine, neg_in_x, neg_in_y, neg_mid_x, neg_mid_y, neg_end_x, neg_end_y, (sem_ps, sem_pr)
    )
    plane.start_first()

    rows = hot_head.shape[0]
    piece_rows = 160
    for b in range(blocks):
        hot_head[:, b * edges : (b + 1) * edges] = one_hot(rows, head_rows[b : b + 1, :])

    def head_piece(p, squares):
        spots = pl.ds(pl.multiple_of(p * piece_rows, piece_rows), piece_rows)
        gradient = jnp.zeros((piece_rows, rows), F32)
        for b in range(blocks):
            lanes = slice(b * edges, (b + 1) * edges)
            for n in range(2):
                gradient = gradient + mm(grad[b, n, spots, :], hot_head[:, lanes], NT)
        head_grad[spots, :] = gradient
        return squares + jnp.sum(gradient * gradient, axis=0, keepdims=True)

    squares = lax.fori_loop(0, width // piece_rows, head_piece, jnp.zeros((1, rows), F32))

    def spread_rows(piece):
        which, lanes = pieces[piece]

        @pl.loop(0, HEAD)
        def _(source):
            for b in range(which.start, which.start + which.size):
                spot = pl.multiple_of((source * owned + b) * group, group)
                slot_rows[pl.ds(spot, group), lanes] = slots[source, b, :, lanes].astype(F32)

    def arrive(piece):
        @pl.loop(1, HEAD)
        def _(step):
            block_copy(piece, step).wait_recv()

        if piece == 0:
            keep_block.wait()
        spread_rows(piece)

    def fill(dense, sums):
        for block in range(TAIL * owned):
            y, x, part = block // owned // SIDE, block // owned % SIDE, block % owned
            dense[y, x, part] = sums[block * group : (block + 1) * group]

    arrive(0)
    arrive(1)
    count = HEAD * owned * group
    number = slot_rows[:, width : width + 1]
    inner = lax.broadcasted_iota(jnp.int32, (count, 1), 0) % group
    goal = number * group + inner.astype(F32)
    places = lax.broadcasted_iota(jnp.int32, (count, count), 1).astype(F32)
    seats[...] = jnp.where(places == goal, 1.0, 0.0).astype(BF16).T
    fill(hi, mm(seats[...], slot_rows[:, CUT:width].astype(BF16)))
    high = PlaneSum(hi, hi_in_x, hi_in_y, hi_mid_x, hi_mid_y, hi_end_x, hi_end_y, (sem_hs, sem_hr))
    high.start_first()
    plane.start_second()
    arrive(2)
    fill(lo, mm(seats[...], slot_rows[:, :CUT].astype(BF16)))
    low = PlaneSum(lo, lo_in_x, lo_in_y, lo_mid_x, lo_mid_y, lo_end_x, lo_end_y, (sem_ls, sem_lr))
    low.start_first()

    for place, total in enumerate(plane.result()):
        deep[place] = total

    zone = lax.rem(tail, 2)
    takes = lax.div(depth, quarter) == zone
    mine_k = lax.div(tail, 2)

    def deep_copy(step):
        level = zone * quarter + step
        return remote(
            deep.at[step],
            deep_in.at[depth],
            sem_zs.at[step],
            sem_zr.at[depth],
            (level * 2 + core, tail),
        )

    def deep_landing(source):
        return remote(
            deep.at[0], deep_in.at[source], sem_zs.at[0], sem_zr.at[source], (other, tail)
        )

    def total_copy(step):
        return remote(
            neg_total.at[mine_k],
            neg_total.at[mine_k],
            sem_ns.at[step],
            sem_nr.at[mine_k],
            (head, around(tail, step, TAIL)),
        )

    def total_landing(k):
        return remote(neg_total.at[k], neg_total.at[k], sem_ns.at[1], sem_nr.at[k], (other, tail))

    @pl.loop(0, quarter)
    def _(step):
        @pl.when(zone * quarter + step != depth)
        def _():
            deep_copy(step).start()

    high.start_second()

    head_next = head_state[...] + squares / width
    state_new[...] = head_next
    rate = LEARN_RATE / jnp.sqrt(head_next)

    @pl.loop(0, width // piece_rows)
    def _(p):
        spots = pl.ds(pl.multiple_of(p * piece_rows, piece_rows), piece_rows)
        head_emb[spots, :] = (head_emb[spots, :].astype(F32) - head_grad[spots, :] * rate).astype(
            BF16
        )

    head_store = pltpu.make_async_copy(head_emb, head_new, sem_local.at[6])
    head_store.start()

    @pl.when(takes)
    def _():
        deep_in[depth] = deep[depth - zone * quarter]

        @pl.loop(0, DEPTH)
        def _(source):
            @pl.when(source != depth)
            def _():
                deep_landing(source).wait_recv()

        total = deep_in[0]
        for source in range(1, DEPTH):
            total = total + deep_in[source]
        neg_total[mine_k] = total

        @pl.loop(1, TAIL)
        def _(step):
            total_copy(step).start()

    lane = lax.broadcasted_iota(jnp.int32, (group, span), 1)
    mark = lane == head * group + lax.broadcasted_iota(jnp.int32, (group, span), 0)
    rows_now = [mm(jnp.where(mark, 1.0, 0.0).astype(BF16), own_t[b], NT) for b in range(owned)]
    states_now = [
        jnp.sum(jnp.where(mark, own_state[b : b + 1, :], 0.0), axis=1, keepdims=True)
        for b in range(owned)
    ]

    low.start_second()
    high_sums, low_sums = high.result(), low.result()

    @pl.loop(0, neg_total.shape[0])
    def _(k):
        @pl.when(2 * k + lax.div(depth, quarter) != tail)
        def _():
            total_landing(k).wait_recv()

    for b in range(owned):
        low_part, high_part = low_sums[b], high_sums[b]
        for k in range(neg_total.shape[0]):
            weight = jnp.where(neg_ids[k] == tail * owned + b, 1.0, 0.0).astype(F32)
            low_part = low_part + weight * neg_total[k, :, :CUT]
            high_part = high_part + weight * neg_total[k, :, CUT:]
        squares = jnp.sum(low_part * low_part, axis=1, keepdims=True) + jnp.sum(
            high_part * high_part, axis=1, keepdims=True
        )
        fresh = states_now[b] + squares / width
        rate = LEARN_RATE / jnp.sqrt(fresh)
        update[b, :, :CUT] = (rows_now[b][:, :CUT] - low_part * rate).astype(BF16)
        update[b, :, CUT:width] = (rows_now[b][:, CUT:] - high_part * rate).astype(BF16)
        spot = lax.broadcasted_iota(jnp.int32, (group, LANES - width), 1)
        fresh_a = fresh.astype(BF16).astype(F32)
        fresh_b = (fresh - fresh_a).astype(BF16).astype(F32)
        fresh_c = fresh - fresh_a - fresh_b
        parts = jnp.where(spot == 0, fresh_a, jnp.where(spot == 1, fresh_b, fresh_c))
        update[b, :, width:] = parts.astype(BF16)

    def rows_copy(step):
        peer = around(depth, step, DEPTH) * 2 + core
        return remote(update, out.at[:, head], sem_us.at[step], sem_ur.at[step], (peer, tail))

    @pl.loop(1, DEPTH)
    def _(step):
        rows_copy(step).start()

    out_own = pltpu.make_async_copy(update, out.at[:, head], sem_local.at[7])
    out_own.start()
    first_rows = remote(update, out.at[:, head], sem_fs.at[0], sem_fr.at[0], (other, tail))
    first_rows.start()

    def pass_rows(step):
        place = around(depth, DEPTH - step, DEPTH) * 2 + core
        return remote(
            out.at[:, place], out.at[:, place], sem_fs.at[step], sem_fr.at[step], (other, tail)
        )

    plane.finish()
    high.finish()
    low.finish()
    for part in range(SIDE):
        pair_copy(part).wait_send()

    for piece in range(3):

        @pl.loop(1, HEAD)
        def _(step):
            block_copy(piece, step).wait_send()

    @pl.loop(0, quarter)
    def _(step):
        @pl.when(zone * quarter + step != depth)
        def _():
            deep_copy(step).wait_send()

    @pl.when(takes)
    def _():
        @pl.loop(1, TAIL)
        def _(step):
            total_copy(step).wait_send()

    head_store.wait()

    @pl.loop(1, DEPTH)
    def _(step):
        rows_copy(step).wait_recv()
        pass_rows(step).start()

    out_own.wait()
    first_rows.wait()

    @pl.loop(1, DEPTH)
    def _(step):
        pass_rows(step).wait()
        rows_copy(step).wait_send()


def run_exchange(
    owners,
    locals_,
    live_count,
    neg_ids,
    chosen,
    neg_t,
    query,
    rel_vec,
    head_t,
    offsets,
    head_rows,
    head_state,
    own_t,
    own_state,
):
    owned, width, span = own_t.shape
    blocks, edges = offsets.shape
    rows = head_t.shape[1]
    group = span // HEAD
    negs = neg_ids.shape[0]
    quarter = DEPTH // 2
    count = HEAD * owned * group
    sems = pltpu.SemaphoreType.DMA
    smem = pl.BlockSpec(memory_space=pltpu.SMEM)
    anywhere = pl.BlockSpec(memory_space=pl.ANY)
    vmem = pl.BlockSpec(memory_space=pltpu.VMEM)

    def plane_sum(columns):
        return [
            pltpu.VMEM((SIDE, SIDE, 4, group, columns), F32),
            *([pltpu.VMEM((SIDE - 1, SIDE, 2, group, columns), F32)] * 2),
            *([pltpu.VMEM((SIDE, 2, group, columns), F32)] * 2),
            *([pltpu.VMEM((SIDE - 1, 2, group, columns), F32)] * 2),
        ]

    return pl.pallas_call(
        exchange,
        out_shape=(
            jax.ShapeDtypeStruct((owned, HEAD, group, LANES), BF16),
            jax.ShapeDtypeStruct(head_t.shape, BF16),
            jax.ShapeDtypeStruct((1, rows), F32),
        ),
        in_specs=[smem] * 4 + [anywhere] * 5 + [vmem] * 5,
        out_specs=(anywhere, anywhere, vmem),
        scratch_shapes=[
            pltpu.VMEM(chosen.shape, BF16),
            pltpu.VMEM(neg_t.shape, BF16),
            pltpu.VMEM((negs * span, width), BF16),
            pltpu.VMEM(query.shape, BF16),
            pltpu.VMEM(rel_vec.shape, BF16),
            pltpu.VMEM((blocks, negs * span, edges), BF16),
            pltpu.VMEM((blocks, 2, width, edges), BF16),
            pltpu.VMEM((HEAD, blocks, group, LANES), BF16),
            pltpu.VMEM(head_t.shape, BF16),
            pltpu.VMEM(head_t.shape, F32),
            pltpu.VMEM((rows, blocks * edges), BF16),
            pltpu.VMEM((SIDE, SIDE, 4, 2, group, width), F32),
            pltpu.VMEM((HEAD, owned, group, LANES), BF16),
            pltpu.VMEM((SIDE, SIDE, 4, group, width), F32),
            *plane_sum(width),
            pltpu.VMEM((quarter, group, width), F32),
            pltpu.VMEM((DEPTH, group, width), F32),
            pltpu.VMEM((negs, group, width), F32),
            pltpu.VMEM((count, LANES), F32),
            pltpu.VMEM((count, count), BF16),
            *plane_sum(CUT),
            *plane_sum(width - CUT),
            pltpu.VMEM((owned, group, LANES), BF16),
            sems((3, HEAD)),
            sems((3, HEAD)),
            sems((SIDE,)),
            sems((SIDE,)),
            sems((12,)),
            sems((12,)),
            sems((quarter,)),
            sems((DEPTH,)),
            sems((12,)),
            sems((12,)),
            sems((12,)),
            sems((12,)),
            sems((TAIL,)),
            sems((negs,)),
            sems((DEPTH,)),
            sems((DEPTH,)),
            sems((DEPTH,)),
            sems((DEPTH,)),
            sems((8,)),
        ],
        compiler_params=pltpu.CompilerParams(
            collective_id=1, has_side_effects=True, vmem_limit_bytes=VMEM_BYTES
        ),
    )(
        owners,
        locals_,
        live_count,
        neg_ids,
        chosen,
        neg_t,
        query,
        rel_vec,
        head_t,
        offsets,
        head_rows,
        head_state,
        own_t,
        own_state,
    )


def per_device(
    head_emb,
    head_state,
    tail_emb,
    tail_state,
    relation_emb,
    head_rows,
    relations,
    tail_offsets,
    tail_owner,
    tail_local,
    block_count,
    neg_blocks,
):
    owned, span, width = tail_emb.shape
    head_t, tail_t = head_emb.T, tail_emb.transpose(0, 2, 1)
    owners = tail_owner.reshape(-1)
    query, rel_vec, chosen, neg_t = gather_table(
        owners, tail_local, neg_blocks, tail_t, head_t, relation_emb.T, head_rows, relations
    )
    fresh, head_new, head_state_new = run_exchange(
        owners,
        tail_local,
        block_count,
        neg_blocks,
        chosen,
        neg_t,
        query,
        rel_vec,
        head_t,
        tail_offsets,
        head_rows,
        head_state[None, :],
        tail_t,
        tail_state,
    )
    fresh = fresh.reshape(owned, span, LANES)
    pieces = fresh[:, :, width : width + 3].astype(F32)
    tail_state_new = (pieces[..., 0] + pieces[..., 1]) + pieces[..., 2]
    return (head_new.T, head_state_new[0], fresh[:, :, :width], tail_state_new)


def solution(mesh):
    placed = (
        P(("head", "tail"), None),
        P(("head", "tail")),
        P("tail", None, None),
        P("tail", None),
        P(),
        P(("head", "tail"), None),
        P(("head", "tail"), None),
        P(("head", "tail"), None),
        P(("head", "tail"), None),
        P(("head", "tail")),
        P(("head", "tail")),
        P(),
    )
    return jax.shard_map(
        per_device,
        mesh=mesh,
        in_specs=placed,
        out_specs=(
            P(("head", "tail"), None),
            P(("head", "tail")),
            P("tail", None, None),
            P("tail", None),
        ),
        check_vma=False,
    )
```

```python
import jax
import jax.numpy as jnp
from jax import lax
from jax.experimental import pallas as pl
from jax.experimental.pallas import tpu as pltpu
from jax.sharding import PartitionSpec as P

LEARN_RATE = 0.3
MESH = pl.DeviceIdType.MESH
F32 = jnp.float32
BF16 = jnp.bfloat16
SIDE = 4
DEPTH = 8
HEAD = 16
TAIL = 16
CUT = 512
LANES = 896
VMEM_BYTES = 64 << 20


def greet(targets):
    barrier = pltpu.get_barrier_semaphore()
    for target in targets:
        pl.semaphore_signal(barrier, inc=1, device_id=target, device_id_type=MESH)
    pl.semaphore_wait(barrier, len(targets))


TN = (((0,), (0,)), ((), ()))
NT = (((1,), (1,)), ((), ()))


def mm(left, right, dims=(((1,), (0,)), ((), ()))):
    return lax.dot_general(left, right, dims, preferred_element_type=F32)


def one_hot(count, index_row):
    spots = lax.broadcasted_iota(jnp.int32, (count, index_row.shape[1]), 0)
    return jnp.where(spots == index_row, 1.0, 0.0).astype(BF16)


def table_gather(
    owners,
    locals_,
    neg_ids,
    own,
    head_hbm,
    rel_hbm,
    head_rows_hbm,
    relations_hbm,
    query_out,
    rel_out,
    chosen_out,
    neg_out,
    table,
    chosen,
    neg_t,
    head_t,
    rel_t,
    head_rows,
    relations,
    query,
    rel_vec,
    send1,
    recv1,
    send2,
    recv2,
    send3,
    recv3,
    local,
):
    head, tail = lax.axis_index("head"), lax.axis_index("tail")
    core, col, row = lax.rem(head, 2), lax.rem(tail, SIDE), lax.div(tail, SIDE)
    sibling = (head + 1 - 2 * core, tail)
    size = own.shape[1]
    owned, span = own.shape[0], own.shape[2]
    everything = (0, size)
    first, second = (0, size // 2), (size // 2, size // 2)
    blocks = query.shape[0]

    loads = [
        pltpu.make_async_copy(head_hbm, head_t, local.at[0]),
        pltpu.make_async_copy(rel_hbm, rel_t, local.at[1]),
        pltpu.make_async_copy(own, table.at[pl.ds(tail * owned, owned)], local.at[2]),
        pltpu.make_async_copy(head_rows_hbm, head_rows, local.at[3 + 2 * blocks]),
        pltpu.make_async_copy(relations_hbm, relations, local.at[4 + 2 * blocks]),
    ]
    for load in loads:
        load.start()

    def place(which, along, across):
        dx, dy = (along, across) if which == 0 else (across, along)
        return lax.rem(row + dy + SIDE, SIDE) * SIDE + lax.rem(col + dx + SIDE, SIDE)

    greet(
        [sibling]
        + [(head, place(0, 1, 0)), (head, place(0, -1, 0))]
        + [(head, place(1, 1, 0)), (head, place(1, -1, 0))]
    )

    def copy(which, origin, part, sems, spot, target):
        block = 2 * core + which
        start, count = part
        here = table.at[place(which, *origin) * owned + block, pl.ds(start, count)]
        source = own.at[block, pl.ds(start, count)] if origin == (0, 0) else here
        return pltpu.make_async_remote_copy(
            src_ref=source,
            dst_ref=here,
            send_sem=sems[0].at[which, spot],
            recv_sem=sems[1].at[which, spot],
            device_id=target,
            device_id_type=MESH,
        )

    def landing(which, origin, part, sems, spot, block=None):
        block = 2 * core + which if block is None else block
        start, count = part
        here = table.at[place(which, *origin) * owned + block, pl.ds(start, count)]
        return pltpu.make_async_remote_copy(
            src_ref=here,
            dst_ref=here,
            send_sem=sems[0].at[which, spot],
            recv_sem=sems[1].at[which, spot],
            device_id=sibling,
            device_id_type=MESH,
        )

    stage1, stage2, stage3 = (send1, recv1), (send2, recv2), (send3, recv3)
    sent = []

    def send(*description):
        transfer = copy(*description)
        transfer.start()
        sent.append(transfer)

    def spread(which, origin):
        spot = (origin[0] % SIDE) * 4
        send(which, origin, everything, stage2, spot, (head, place(which, 0, 1)))
        send(which, origin, everything, stage2, spot + 1, (head, place(which, 0, -1)))

    def share(which, origin):
        spot = (origin[0] % SIDE) * 4 + origin[1] % SIDE
        send(which, origin, everything, stage3, spot, sibling)

    stores = []

    def make_query(b):
        half = size // 2
        vec = mm(head_t[...], one_hot(head_t.shape[1], head_rows[b : b + 1, :]))
        rel = mm(rel_t[...], one_hot(rel_t.shape[1], relations[b : b + 1, :]))
        rel_vec[b] = rel.astype(BF16)
        query[b, :half] = (vec[:half] * rel[:half] - vec[half:] * rel[half:]).astype(BF16)
        query[b, half:] = (vec[:half] * rel[half:] + vec[half:] * rel[:half]).astype(BF16)
        for value, target, spot in ((query, query_out, 3), (rel_vec, rel_out, 3 + blocks)):
            store = pltpu.make_async_copy(value.at[b], target.at[b], local.at[spot + b])
            store.start()
            stores.append(store)

    for which in (0, 1):
        send(which, (0, 0), everything, stage1, 0, (head, place(which, 1, 0)))
        send(which, (0, 0), everything, stage1, 1, (head, place(which, -1, 0)))
    for which in (0, 1):
        spread(which, (0, 0))
    for n in (0, 1, 3, 4):
        loads[n].wait()
    make_query(0)
    for which in (0, 1):
        landing(which, (-1, 0), everything, stage1, 0).wait_recv()
        send(which, (-1, 0), first, stage1, 2, (head, place(which, 1, 0)))
        spread(which, (-1, 0))
        share(which, (-1, 0))
        landing(which, (1, 0), everything, stage1, 1).wait_recv()
        send(which, (1, 0), second, stage1, 3, (head, place(which, -1, 0)))
        spread(which, (1, 0))
        share(which, (1, 0))
    for b in range(1, blocks - 1):
        make_query(b)
    for which in (0, 1):
        landing(which, (2, 0), first, stage1, 2).wait_recv()
        landing(which, (2, 0), second, stage1, 3).wait_recv()
        spread(which, (2, 0))
        share(which, (2, 0))
    for along in (0, -1, 1, 2):
        spot = (along % SIDE) * 4
        for which in (0, 1):
            landing(which, (along, -1), everything, stage2, spot).wait_recv()
            send(which, (along, -1), first, stage2, spot + 2, (head, place(which, 0, 1)))
            share(which, (along, -1))
            landing(which, (along, 1), everything, stage2, spot + 1).wait_recv()
            send(which, (along, 1), second, stage2, spot + 3, (head, place(which, 0, -1)))
            share(which, (along, 1))
        if along == 0:
            make_query(blocks - 1)
    for along in (0, -1, 1, 2):
        spot = (along % SIDE) * 4
        for which in (0, 1):
            landing(which, (along, 2), first, stage2, spot + 2).wait_recv()
            landing(which, (along, 2), second, stage2, spot + 3).wait_recv()
            share(which, (along, 2))
    for which in (0, 1):
        for along in range(SIDE):
            for across in range(SIDE):
                if (along, across) != (0, 0):
                    block = 2 * (1 - core) + which
                    spot = along * 4 + across
                    landing(which, (along, across), everything, stage3, spot, block).wait_recv()
    loads[2].wait()
    for k in range(neg_ids.shape[0]):
        neg_t[:, k * span : (k + 1) * span] = table[neg_ids[k]]
    for b in range(blocks):
        chosen[b] = table[owners[b] * owned + locals_[b]]
    for n, (value, target) in enumerate(((neg_t, neg_out), (chosen, chosen_out))):
        store = pltpu.make_async_copy(value, target, local.at[5 + 2 * blocks + n])
        store.start()
        stores.append(store)
    for store in stores:
        store.wait()
    for transfer in sent:
        transfer.wait_send()


def gather_table(owners, locals_, neg_ids, tail_t, head_t, rel_t, head_rows, relations):
    owned, _, span = tail_t.shape
    negs = neg_ids.shape[0]
    blocks, edges = head_rows.shape
    width = head_t.shape[0]
    sems = pltpu.SemaphoreType.DMA
    anywhere = pl.BlockSpec(memory_space=pl.ANY)
    return pl.pallas_call(
        table_gather,
        out_shape=(
            jax.ShapeDtypeStruct((blocks, width, edges), BF16),
            jax.ShapeDtypeStruct((blocks, width, edges), BF16),
            jax.ShapeDtypeStruct((blocks, width, span), BF16),
            jax.ShapeDtypeStruct((width, negs * span), BF16),
        ),
        in_specs=[pl.BlockSpec(memory_space=pltpu.SMEM)] * 3
        + [pl.BlockSpec(memory_space=pltpu.HBM)] * 5,
        out_specs=(anywhere, anywhere, anywhere, anywhere),
        scratch_shapes=[
            pltpu.VMEM((TAIL * owned, width, span), BF16),
            pltpu.VMEM((blocks, width, span), BF16),
            pltpu.VMEM((width, negs * span), BF16),
            pltpu.VMEM(head_t.shape, BF16),
            pltpu.VMEM(rel_t.shape, BF16),
            pltpu.VMEM(head_rows.shape, jnp.int32),
            pltpu.VMEM(relations.shape, jnp.int32),
            pltpu.VMEM((blocks, width, edges), BF16),
            pltpu.VMEM((blocks, width, edges), BF16),
            sems((2, 4)),
            sems((2, 4)),
            sems((2, 16)),
            sems((2, 16)),
            sems((2, 16)),
            sems((2, 16)),
            sems((7 + 2 * blocks,)),
        ],
        compiler_params=pltpu.CompilerParams(
            collective_id=0, has_side_effects=True, vmem_limit_bytes=VMEM_BYTES
        ),
    )(owners, locals_, neg_ids, tail_t, head_t, rel_t, head_rows, relations)


def remote(source, target, send_sem, recv_sem, device):
    return pltpu.make_async_remote_copy(
        src_ref=source,
        dst_ref=target,
        send_sem=send_sem,
        recv_sem=recv_sem,
        device_id=device,
        device_id_type=MESH,
    )


class PlaneSum:
    def __init__(self, spread, in_x, in_y, mid_x, mid_y, end_x, end_y, sems):
        self.refs = (spread, in_x, in_y, mid_x, mid_y, end_x, end_y)
        self.sems = sems
        self.head, tail = lax.axis_index("head"), lax.axis_index("tail")
        self.col, self.row = lax.rem(tail, SIDE), lax.div(tail, SIDE)

    def steps(self):
        for step in range(1, SIDE):
            col = lax.rem(self.col + step, SIDE)
            row = lax.rem(self.row + step, SIDE)
            yield step - 1, col, row, (self.head, self.row * SIDE + col), (
                self.head,
                row * SIDE + self.col,
            )

    def first(self):
        spread, in_x, in_y = self.refs[:3]
        send, recv = self.sems
        copies = []
        for n, col, row, over_x, over_y in self.steps():
            copies.append(
                remote(spread.at[:, col, pl.ds(0, 2)], in_x.at[n], send.at[n], recv.at[n], over_x)
            )
            copies.append(
                remote(
                    spread.at[row, :, pl.ds(2, 2)], in_y.at[n], send.at[3 + n], recv.at[3 + n], over_y
                )
            )
        return copies

    def second(self):
        mid_x, mid_y, end_x, end_y = self.refs[3:]
        send, recv = self.sems
        copies = []
        for n, col, row, over_x, over_y in self.steps():
            copies.append(remote(mid_x.at[row], end_x.at[n], send.at[6 + n], recv.at[6 + n], over_y))
            copies.append(remote(mid_y.at[col], end_y.at[n], send.at[9 + n], recv.at[9 + n], over_x))
        return copies

    def start_first(self):
        for copy in self.first():
            copy.start()

    def start_second(self):
        spread, in_x, in_y, mid_x, mid_y = self.refs[:5]
        for copy in self.first():
            copy.wait_recv()
        for place in range(SIDE):
            for part in range(2):
                total = spread[place, self.col, part].astype(F32)
                other = spread[self.row, place, 2 + part].astype(F32)
                for n in range(SIDE - 1):
                    total = total + in_x[n, place, part].astype(F32)
                    other = other + in_y[n, place, part].astype(F32)
                mid_x[place, part] = total
                mid_y[place, part] = other
        for copy in self.second():
            copy.start()

    def result(self):
        mid_x, mid_y, end_x, end_y = self.refs[3:]
        for copy in self.second():
            copy.wait_recv()
        parts = []
        for part in range(2):
            total = mid_x[self.row, part]
            for n in range(SIDE - 1):
                total = total + end_x[n, part]
            parts.append(total)
        for part in range(2):
            total = mid_y[self.col, part]
            for n in range(SIDE - 1):
                total = total + end_y[n, part]
            parts.append(total)
        return parts

    def finish(self):
        for copy in self.first() + self.second():
            copy.wait_send()


def exchange(
    owners,
    locals_,
    live_count,
    neg_ids,
    chosen_hbm,
    neg_hbm,
    query_hbm,
    rel_hbm,
    head_hbm,
    offsets,
    head_rows,
    head_state,
    own_t,
    own_state,
    out,
    head_new,
    state_new,
    chosen,
    neg_t,
    negs,
    query,
    rel_all,
    prob,
    grad,
    block_part,
    head_emb,
    head_grad,
    hot_head,
    neg_part,
    slots,
    theirs,
    mine,
    neg_in_x,
    neg_in_y,
    neg_mid_x,
    neg_mid_y,
    neg_end_x,
    neg_end_y,
    deep,
    deep_in,
    neg_total,
    slot_rows,
    seats,
    lo,
    lo_in_x,
    lo_in_y,
    lo_mid_x,
    lo_mid_y,
    lo_end_x,
    lo_end_y,
    hi,
    hi_in_x,
    hi_in_y,
    hi_mid_x,
    hi_mid_y,
    hi_end_x,
    hi_end_y,
    update,
    sem_bs,
    sem_br,
    sem_cs,
    sem_cr,
    sem_ps,
    sem_pr,
    sem_zs,
    sem_zr,
    sem_ls,
    sem_lr,
    sem_hs,
    sem_hr,
    sem_ns,
    sem_nr,
    sem_us,
    sem_ur,
    sem_fs,
    sem_fr,
    sem_local,
):
    head, tail = lax.axis_index("head"), lax.axis_index("tail")
    core, depth = lax.rem(head, 2), lax.div(head, 2)
    other = head + 1 - 2 * core
    owned, width, span = own_t.shape
    group = slots.shape[2]
    quarter = DEPTH // 2
    blocks, edges = offsets.shape
    half = width // 2

    def around(index, step, count):
        return lax.rem(index + step, count)

    loads = [
        pltpu.make_async_copy(neg_hbm, neg_t, sem_local.at[0]),
        pltpu.make_async_copy(query_hbm, query, sem_local.at[1]),
        pltpu.make_async_copy(chosen_hbm, chosen, sem_local.at[2]),
        pltpu.make_async_copy(rel_hbm, rel_all, sem_local.at[3]),
        pltpu.make_async_copy(head_hbm, head_emb, sem_local.at[4]),
    ]
    for load in loads:
        load.start()

    barrier = pltpu.get_barrier_semaphore()

    @pl.loop(1, HEAD)
    def _(step):
        pl.semaphore_signal(
            barrier, inc=1, device_id=(around(head, step, HEAD), tail), device_id_type=MESH
        )
        pl.semaphore_signal(
            barrier, inc=1, device_id=(head, around(tail, step, TAIL)), device_id_type=MESH
        )

    loads[0].wait()
    for k in range(negs.shape[0] // span):
        negs[k * span : (k + 1) * span, :] = neg_t[:, k * span : (k + 1) * span].T
    for load in loads[1:]:
        load.wait()

    def edge_block(b):
        live = jnp.where(b < live_count[0], 1.0, 0.0).astype(F32)
        pick = one_hot(span, offsets[pl.ds(b, 1), :])
        tail_vec = mm(chosen[b], pick)
        queries = query[b].astype(F32)
        positive = jnp.sum(queries * tail_vec, axis=0, keepdims=True)
        score = mm(negs[...], query[b])
        largest = jnp.maximum(positive, jnp.max(score, axis=0, keepdims=True))
        pos_exp = jnp.exp(positive - largest)
        neg_exp = jnp.exp(score - largest)
        denominator = pos_exp + jnp.sum(neg_exp, axis=0, keepdims=True)
        pos_grad = (pos_exp / denominator - 1.0) * live
        part = pos_grad * queries
        part_a = part.astype(BF16)
        rest = part - part_a.astype(F32)
        part_b = rest.astype(BF16)
        part_c = (rest - part_b.astype(F32)).astype(BF16)
        block_grad = mm(pick, part_a, NT) + (mm(pick, part_b, NT) + mm(pick, part_c, NT))
        number = (owners[b] * owned + locals_[b]).astype(F32)
        for i in range(HEAD):
            block_part[i, b, :, :width] = block_grad[i * group : (i + 1) * group].astype(BF16)
            block_part[i, b, :, width:] = jnp.full((group, LANES - width), number, BF16)
        prob[b] = (neg_exp * (live / denominator)).astype(BF16)
        query_grad = pos_grad * tail_vec + mm(neg_t[...], prob[b])
        rel = rel_all[b].astype(F32)
        rr, ri = rel[:half], rel[half:]
        qr, qi = query_grad[:half], query_grad[half:]
        for start, change in ((0, qr * rr + qi * ri), (half, qi * rr - qr * ri)):
            change_hi = change.astype(BF16)
            grad[b, 0, start : start + half, :] = change_hi
            grad[b, 1, start : start + half, :] = (change - change_hi.astype(F32)).astype(BF16)

    early = blocks // 2
    pieces = (
        *((pl.ds(b, 1), pl.ds(0, LANES)) for b in range(early)),
        (pl.ds(early, blocks - early), pl.ds(CUT, LANES - CUT)),
        (pl.ds(early, blocks - early), pl.ds(0, CUT)),
    )

    def block_copy(piece, step):
        which, lanes = pieces[piece]
        peer = around(head, step, HEAD)
        return remote(
            block_part.at[peer, which, :, lanes],
            slots.at[head, which, :, lanes],
            sem_bs.at[piece, step],
            sem_br.at[piece, step],
            (peer, tail),
        )

    for b in range(early):
        edge_block(b)
        if b == 0:
            pl.semaphore_wait(barrier, HEAD + TAIL - 2)

        @pl.loop(1, HEAD)
        def _(step):
            block_copy(b, step).start()

    @pl.loop(early, blocks)
    def _(b):
        edge_block(b)

    for piece in range(early, len(pieces)):

        @pl.loop(1, HEAD)
        def _(step):
            block_copy(piece, step).start()

    keep_block = pltpu.make_async_copy(block_part.at[head], slots.at[head], sem_local.at[5])
    keep_block.start()

    def pair_copy(part):
        return remote(
            neg_part.at[part, :, :, 1 - core],
            theirs.at[part],
            sem_cs.at[part],
            sem_cr.at[part],
            (other, tail),
        )

    chunk = prob.shape[1] // SIDE

    @pl.loop(0, SIDE)
    def _(part):
        spots = pl.ds(pl.multiple_of(part * chunk, chunk), chunk)
        total = mm(prob[0, spots, :], query[0], NT)
        for b in range(1, blocks):
            total = total + mm(prob[b, spots, :], query[b], NT)
        neg_part[part] = total.reshape(neg_part.shape[1:])
        pair_copy(part).start()

    for part in range(SIDE):
        pair_copy(part).wait_recv()
        for place in range(SIDE):
            total = neg_part[part, place, :, core] + theirs[part, place]
            mine[part, place] = total.astype(BF16)
    plane = PlaneSum(
        mine, neg_in_x, neg_in_y, neg_mid_x, neg_mid_y, neg_end_x, neg_end_y, (sem_ps, sem_pr)
    )
    plane.start_first()

    rows = hot_head.shape[0]
    piece_rows = 160
    for b in range(blocks):
        hot_head[:, b * edges : (b + 1) * edges] = one_hot(rows, head_rows[b : b + 1, :])

    def head_piece(p, squares):
        spots = pl.ds(pl.multiple_of(p * piece_rows, piece_rows), piece_rows)
        gradient = jnp.zeros((piece_rows, rows), F32)
        for b in range(blocks):
            lanes = slice(b * edges, (b + 1) * edges)
            for n in range(2):
                gradient = gradient + mm(grad[b, n, spots, :], hot_head[:, lanes], NT)
        head_grad[spots, :] = gradient
        return squares + jnp.sum(gradient * gradient, axis=0, keepdims=True)

    squares = lax.fori_loop(0, width // piece_rows, head_piece, jnp.zeros((1, rows), F32))

    def spread_rows(piece):
        which, lanes = pieces[piece]

        @pl.loop(0, HEAD)
        def _(source):
            for b in range(which.start, which.start + which.size):
                spot = pl.multiple_of((source * owned + b) * group, group)
                slot_rows[pl.ds(spot, group), lanes] = slots[source, b, :, lanes].astype(F32)

    def arrive(piece):
        @pl.loop(1, HEAD)
        def _(step):
            block_copy(piece, step).wait_recv()

        if piece == 0:
            keep_block.wait()
        spread_rows(piece)

    def fill(dense, sums):
        for block in range(TAIL * owned):
            y, x, part = block // owned // SIDE, block // owned % SIDE, block % owned
            dense[y, x, part] = sums[block * group : (block + 1) * group]

    for piece in range(len(pieces) - 1):
        arrive(piece)
    count = HEAD * owned * group
    number = slot_rows[:, width : width + 1]
    inner = lax.broadcasted_iota(jnp.int32, (count, 1), 0) % group
    goal = number * group + inner.astype(F32)
    places = lax.broadcasted_iota(jnp.int32, (count, count), 1).astype(F32)
    seats[...] = jnp.where(places == goal, 1.0, 0.0).astype(BF16).T
    fill(hi, mm(seats[...], slot_rows[:, CUT:width].astype(BF16)))
    high = PlaneSum(hi, hi_in_x, hi_in_y, hi_mid_x, hi_mid_y, hi_end_x, hi_end_y, (sem_hs, sem_hr))
    high.start_first()
    plane.start_second()
    arrive(len(pieces) - 1)
    fill(lo, mm(seats[...], slot_rows[:, :CUT].astype(BF16)))
    low = PlaneSum(lo, lo_in_x, lo_in_y, lo_mid_x, lo_mid_y, lo_end_x, lo_end_y, (sem_ls, sem_lr))
    low.start_first()

    for place, total in enumerate(plane.result()):
        deep[place] = total

    zone = lax.rem(tail, 2)
    takes = lax.div(depth, quarter) == zone
    mine_k = lax.div(tail, 2)

    def deep_copy(step):
        level = zone * quarter + step
        return remote(
            deep.at[step],
            deep_in.at[depth],
            sem_zs.at[step],
            sem_zr.at[depth],
            (level * 2 + core, tail),
        )

    def deep_landing(source):
        return remote(
            deep.at[0], deep_in.at[source], sem_zs.at[0], sem_zr.at[source], (other, tail)
        )

    def total_copy(step):
        return remote(
            neg_total.at[mine_k],
            neg_total.at[mine_k],
            sem_ns.at[step],
            sem_nr.at[mine_k],
            (head, around(tail, step, TAIL)),
        )

    def total_landing(k):
        return remote(neg_total.at[k], neg_total.at[k], sem_ns.at[1], sem_nr.at[k], (other, tail))

    @pl.loop(0, quarter)
    def _(step):
        @pl.when(zone * quarter + step != depth)
        def _():
            deep_copy(step).start()

    high.start_second()

    head_next = head_state[...] + squares / width
    state_new[...] = head_next
    rate = LEARN_RATE / jnp.sqrt(head_next)

    @pl.loop(0, width // piece_rows)
    def _(p):
        spots = pl.ds(pl.multiple_of(p * piece_rows, piece_rows), piece_rows)
        head_emb[spots, :] = (head_emb[spots, :].astype(F32) - head_grad[spots, :] * rate).astype(
            BF16
        )

    head_store = pltpu.make_async_copy(head_emb, head_new, sem_local.at[6])
    head_store.start()

    @pl.when(takes)
    def _():
        deep_in[depth] = deep[depth - zone * quarter]

        @pl.loop(0, DEPTH)
        def _(source):
            @pl.when(source != depth)
            def _():
                deep_landing(source).wait_recv()

        total = deep_in[0]
        for source in range(1, DEPTH):
            total = total + deep_in[source]
        neg_total[mine_k] = total

        @pl.loop(1, TAIL)
        def _(step):
            total_copy(step).start()

    lane = lax.broadcasted_iota(jnp.int32, (group, span), 1)
    mark = lane == head * group + lax.broadcasted_iota(jnp.int32, (group, span), 0)
    rows_now = [mm(jnp.where(mark, 1.0, 0.0).astype(BF16), own_t[b], NT) for b in range(owned)]
    states_now = [
        jnp.sum(jnp.where(mark, own_state[b : b + 1, :], 0.0), axis=1, keepdims=True)
        for b in range(owned)
    ]

    low.start_second()
    high_sums, low_sums = high.result(), low.result()

    @pl.loop(0, neg_total.shape[0])
    def _(k):
        @pl.when(2 * k + lax.div(depth, quarter) != tail)
        def _():
            total_landing(k).wait_recv()

    for b in range(owned):
        low_part, high_part = low_sums[b], high_sums[b]
        for k in range(neg_total.shape[0]):
            weight = jnp.where(neg_ids[k] == tail * owned + b, 1.0, 0.0).astype(F32)
            low_part = low_part + weight * neg_total[k, :, :CUT]
            high_part = high_part + weight * neg_total[k, :, CUT:]
        squares = jnp.sum(low_part * low_part, axis=1, keepdims=True) + jnp.sum(
            high_part * high_part, axis=1, keepdims=True
        )
        fresh = states_now[b] + squares / width
        rate = LEARN_RATE / jnp.sqrt(fresh)
        update[b, :, :CUT] = (rows_now[b][:, :CUT] - low_part * rate).astype(BF16)
        update[b, :, CUT:width] = (rows_now[b][:, CUT:] - high_part * rate).astype(BF16)
        spot = lax.broadcasted_iota(jnp.int32, (group, LANES - width), 1)
        fresh_a = fresh.astype(BF16).astype(F32)
        fresh_b = (fresh - fresh_a).astype(BF16).astype(F32)
        fresh_c = fresh - fresh_a - fresh_b
        parts = jnp.where(spot == 0, fresh_a, jnp.where(spot == 1, fresh_b, fresh_c))
        update[b, :, width:] = parts.astype(BF16)

    def rows_copy(step):
        peer = around(depth, step, DEPTH) * 2 + core
        return remote(update, out.at[:, head], sem_us.at[step], sem_ur.at[step], (peer, tail))

    @pl.loop(1, DEPTH)
    def _(step):
        rows_copy(step).start()

    out_own = pltpu.make_async_copy(update, out.at[:, head], sem_local.at[7])
    out_own.start()
    first_rows = remote(update, out.at[:, head], sem_fs.at[0], sem_fr.at[0], (other, tail))
    first_rows.start()

    def pass_rows(step):
        place = around(depth, DEPTH - step, DEPTH) * 2 + core
        return remote(
            out.at[:, place], out.at[:, place], sem_fs.at[step], sem_fr.at[step], (other, tail)
        )

    plane.finish()
    high.finish()
    low.finish()
    for part in range(SIDE):
        pair_copy(part).wait_send()

    for piece in range(len(pieces)):

        @pl.loop(1, HEAD)
        def _(step):
            block_copy(piece, step).wait_send()

    @pl.loop(0, quarter)
    def _(step):
        @pl.when(zone * quarter + step != depth)
        def _():
            deep_copy(step).wait_send()

    @pl.when(takes)
    def _():
        @pl.loop(1, TAIL)
        def _(step):
            total_copy(step).wait_send()

    head_store.wait()

    @pl.loop(1, DEPTH)
    def _(step):
        rows_copy(step).wait_recv()
        pass_rows(step).start()

    out_own.wait()
    first_rows.wait()

    @pl.loop(1, DEPTH)
    def _(step):
        pass_rows(step).wait()
        rows_copy(step).wait_send()


def run_exchange(
    owners,
    locals_,
    live_count,
    neg_ids,
    chosen,
    neg_t,
    query,
    rel_vec,
    head_t,
    offsets,
    head_rows,
    head_state,
    own_t,
    own_state,
):
    owned, width, span = own_t.shape
    blocks, edges = offsets.shape
    rows = head_t.shape[1]
    group = span // HEAD
    negs = neg_ids.shape[0]
    quarter = DEPTH // 2
    count = HEAD * owned * group
    sems = pltpu.SemaphoreType.DMA
    smem = pl.BlockSpec(memory_space=pltpu.SMEM)
    anywhere = pl.BlockSpec(memory_space=pl.ANY)
    vmem = pl.BlockSpec(memory_space=pltpu.VMEM)

    def plane_sum(columns, sent=F32):
        return [
            pltpu.VMEM((SIDE, SIDE, 4, group, columns), sent),
            *([pltpu.VMEM((SIDE - 1, SIDE, 2, group, columns), sent)] * 2),
            *([pltpu.VMEM((SIDE, 2, group, columns), F32)] * 2),
            *([pltpu.VMEM((SIDE - 1, 2, group, columns), F32)] * 2),
        ]

    return pl.pallas_call(
        exchange,
        out_shape=(
            jax.ShapeDtypeStruct((owned, HEAD, group, LANES), BF16),
            jax.ShapeDtypeStruct(head_t.shape, BF16),
            jax.ShapeDtypeStruct((1, rows), F32),
        ),
        in_specs=[smem] * 4 + [anywhere] * 5 + [vmem] * 5,
        out_specs=(anywhere, anywhere, vmem),
        scratch_shapes=[
            pltpu.VMEM(chosen.shape, BF16),
            pltpu.VMEM(neg_t.shape, BF16),
            pltpu.VMEM((negs * span, width), BF16),
            pltpu.VMEM(query.shape, BF16),
            pltpu.VMEM(rel_vec.shape, BF16),
            pltpu.VMEM((blocks, negs * span, edges), BF16),
            pltpu.VMEM((blocks, 2, width, edges), BF16),
            pltpu.VMEM((HEAD, blocks, group, LANES), BF16),
            pltpu.VMEM(head_t.shape, BF16),
            pltpu.VMEM(head_t.shape, F32),
            pltpu.VMEM((rows, blocks * edges), BF16),
            pltpu.VMEM((SIDE, SIDE, 4, 2, group, width), F32),
            pltpu.VMEM((HEAD, owned, group, LANES), BF16),
            pltpu.VMEM((SIDE, SIDE, 4, group, width), F32),
            *plane_sum(width, BF16),
            pltpu.VMEM((quarter, group, width), F32),
            pltpu.VMEM((DEPTH, group, width), F32),
            pltpu.VMEM((negs, group, width), F32),
            pltpu.VMEM((count, LANES), F32),
            pltpu.VMEM((count, count), BF16),
            *plane_sum(CUT),
            *plane_sum(width - CUT),
            pltpu.VMEM((owned, group, LANES), BF16),
            sems((blocks // 2 + 2, HEAD)),
            sems((blocks // 2 + 2, HEAD)),
            sems((SIDE,)),
            sems((SIDE,)),
            sems((12,)),
            sems((12,)),
            sems((quarter,)),
            sems((DEPTH,)),
            sems((12,)),
            sems((12,)),
            sems((12,)),
            sems((12,)),
            sems((TAIL,)),
            sems((negs,)),
            sems((DEPTH,)),
            sems((DEPTH,)),
            sems((DEPTH,)),
            sems((DEPTH,)),
            sems((8,)),
        ],
        compiler_params=pltpu.CompilerParams(
            collective_id=1, has_side_effects=True, vmem_limit_bytes=VMEM_BYTES
        ),
    )(
        owners,
        locals_,
        live_count,
        neg_ids,
        chosen,
        neg_t,
        query,
        rel_vec,
        head_t,
        offsets,
        head_rows,
        head_state,
        own_t,
        own_state,
    )


def per_device(
    head_emb,
    head_state,
    tail_emb,
    tail_state,
    relation_emb,
    head_rows,
    relations,
    tail_offsets,
    tail_owner,
    tail_local,
    block_count,
    neg_blocks,
):
    owned, span, width = tail_emb.shape
    head_t, tail_t = head_emb.T, tail_emb.transpose(0, 2, 1)
    owners = tail_owner.reshape(-1)
    query, rel_vec, chosen, neg_t = gather_table(
        owners, tail_local, neg_blocks, tail_t, head_t, relation_emb.T, head_rows, relations
    )
    fresh, head_new, head_state_new = run_exchange(
        owners,
        tail_local,
        block_count,
        neg_blocks,
        chosen,
        neg_t,
        query,
        rel_vec,
        head_t,
        tail_offsets,
        head_rows,
        head_state[None, :],
        tail_t,
        tail_state,
    )
    fresh = fresh.reshape(owned, span, LANES)
    pieces = fresh[:, :, width : width + 3].astype(F32)
    tail_state_new = (pieces[..., 0] + pieces[..., 1]) + pieces[..., 2]
    return (head_new.T, head_state_new[0], fresh[:, :, :width], tail_state_new)


def solution(mesh):
    placed = (
        P(("head", "tail"), None),
        P(("head", "tail")),
        P("tail", None, None),
        P("tail", None),
        P(),
        P(("head", "tail"), None),
        P(("head", "tail"), None),
        P(("head", "tail"), None),
        P(("head", "tail"), None),
        P(("head", "tail")),
        P(("head", "tail")),
        P(),
    )
    return jax.shard_map(
        per_device,
        mesh=mesh,
        in_specs=placed,
        out_specs=(
            P(("head", "tail"), None),
            P(("head", "tail")),
            P("tail", None, None),
            P("tail", None),
        ),
        check_vma=False,
    )
```

```python
import jax
import jax.numpy as jnp
from jax import lax
from jax.experimental import pallas as pl
from jax.experimental.pallas import tpu as pltpu
from jax.sharding import PartitionSpec as P

LEARN_RATE = 0.3
MESH = pl.DeviceIdType.MESH
F32 = jnp.float32
BF16 = jnp.bfloat16
SIDE = 4
DEPTH = 8
HEAD = 16
TAIL = 16
CUT = 512
LANES = 896
VMEM_BYTES = 64 << 20


def greet(targets):
    barrier = pltpu.get_barrier_semaphore()
    for target in targets:
        pl.semaphore_signal(barrier, inc=1, device_id=target, device_id_type=MESH)
    pl.semaphore_wait(barrier, len(targets))


TN = (((0,), (0,)), ((), ()))
NT = (((1,), (1,)), ((), ()))


def mm(left, right, dims=(((1,), (0,)), ((), ()))):
    return lax.dot_general(left, right, dims, preferred_element_type=F32)


def one_hot(count, index_row):
    spots = lax.broadcasted_iota(jnp.int32, (count, index_row.shape[1]), 0)
    return jnp.where(spots == index_row, 1.0, 0.0).astype(BF16)


def table_gather(
    owners,
    locals_,
    neg_ids,
    own,
    head_hbm,
    rel_hbm,
    head_rows_hbm,
    relations_hbm,
    query_out,
    rel_out,
    chosen_out,
    neg_out,
    table,
    chosen,
    neg_t,
    head_t,
    rel_t,
    head_rows,
    relations,
    query,
    rel_vec,
    send1,
    recv1,
    send2,
    recv2,
    send3,
    recv3,
    local,
):
    head, tail = lax.axis_index("head"), lax.axis_index("tail")
    core, col, row = lax.rem(head, 2), lax.rem(tail, SIDE), lax.div(tail, SIDE)
    sibling = (head + 1 - 2 * core, tail)
    size = own.shape[1]
    owned, span = own.shape[0], own.shape[2]
    everything = (0, size)
    first, second = (0, size // 2), (size // 2, size // 2)
    blocks = query.shape[0]

    loads = [
        pltpu.make_async_copy(head_hbm, head_t, local.at[0]),
        pltpu.make_async_copy(rel_hbm, rel_t, local.at[1]),
        pltpu.make_async_copy(own, table.at[pl.ds(tail * owned, owned)], local.at[2]),
        pltpu.make_async_copy(head_rows_hbm, head_rows, local.at[3 + 2 * blocks]),
        pltpu.make_async_copy(relations_hbm, relations, local.at[4 + 2 * blocks]),
    ]
    for load in loads:
        load.start()

    def place(which, along, across):
        dx, dy = (along, across) if which == 0 else (across, along)
        return lax.rem(row + dy + SIDE, SIDE) * SIDE + lax.rem(col + dx + SIDE, SIDE)

    greet(
        [sibling]
        + [(head, place(0, 1, 0)), (head, place(0, -1, 0))]
        + [(head, place(1, 1, 0)), (head, place(1, -1, 0))]
    )

    def copy(which, origin, part, sems, spot, target):
        block = 2 * core + which
        start, count = part
        here = table.at[place(which, *origin) * owned + block, pl.ds(start, count)]
        source = own.at[block, pl.ds(start, count)] if origin == (0, 0) else here
        return pltpu.make_async_remote_copy(
            src_ref=source,
            dst_ref=here,
            send_sem=sems[0].at[which, spot],
            recv_sem=sems[1].at[which, spot],
            device_id=target,
            device_id_type=MESH,
        )

    def landing(which, origin, part, sems, spot, block=None):
        block = 2 * core + which if block is None else block
        start, count = part
        here = table.at[place(which, *origin) * owned + block, pl.ds(start, count)]
        return pltpu.make_async_remote_copy(
            src_ref=here,
            dst_ref=here,
            send_sem=sems[0].at[which, spot],
            recv_sem=sems[1].at[which, spot],
            device_id=sibling,
            device_id_type=MESH,
        )

    stage1, stage2, stage3 = (send1, recv1), (send2, recv2), (send3, recv3)
    sent = []

    def send(*description):
        transfer = copy(*description)
        transfer.start()
        sent.append(transfer)

    def spread(which, origin):
        spot = (origin[0] % SIDE) * 4
        send(which, origin, everything, stage2, spot, (head, place(which, 0, 1)))
        send(which, origin, everything, stage2, spot + 1, (head, place(which, 0, -1)))

    def share(which, origin):
        spot = (origin[0] % SIDE) * 4 + origin[1] % SIDE
        send(which, origin, everything, stage3, spot, sibling)

    stores = []

    def make_query(b):
        half = size // 2
        vec = mm(head_t[...], one_hot(head_t.shape[1], head_rows[b : b + 1, :]))
        rel = mm(rel_t[...], one_hot(rel_t.shape[1], relations[b : b + 1, :]))
        rel_vec[b] = rel.astype(BF16)
        query[b, :half] = (vec[:half] * rel[:half] - vec[half:] * rel[half:]).astype(BF16)
        query[b, half:] = (vec[:half] * rel[half:] + vec[half:] * rel[:half]).astype(BF16)
        for value, target, spot in ((query, query_out, 3), (rel_vec, rel_out, 3 + blocks)):
            store = pltpu.make_async_copy(value.at[b], target.at[b], local.at[spot + b])
            store.start()
            stores.append(store)

    for which in (0, 1):
        send(which, (0, 0), everything, stage1, 0, (head, place(which, 1, 0)))
        send(which, (0, 0), everything, stage1, 1, (head, place(which, -1, 0)))
    for which in (0, 1):
        spread(which, (0, 0))
    for n in (0, 1, 3, 4):
        loads[n].wait()
    make_query(0)
    for which in (0, 1):
        landing(which, (-1, 0), everything, stage1, 0).wait_recv()
        send(which, (-1, 0), first, stage1, 2, (head, place(which, 1, 0)))
        spread(which, (-1, 0))
        share(which, (-1, 0))
        landing(which, (1, 0), everything, stage1, 1).wait_recv()
        send(which, (1, 0), second, stage1, 3, (head, place(which, -1, 0)))
        spread(which, (1, 0))
        share(which, (1, 0))
    for b in range(1, blocks - 1):
        make_query(b)
    for which in (0, 1):
        landing(which, (2, 0), first, stage1, 2).wait_recv()
        landing(which, (2, 0), second, stage1, 3).wait_recv()
        spread(which, (2, 0))
        share(which, (2, 0))
    for along in (0, -1, 1, 2):
        spot = (along % SIDE) * 4
        for which in (0, 1):
            landing(which, (along, -1), everything, stage2, spot).wait_recv()
            send(which, (along, -1), first, stage2, spot + 2, (head, place(which, 0, 1)))
            share(which, (along, -1))
            landing(which, (along, 1), everything, stage2, spot + 1).wait_recv()
            send(which, (along, 1), second, stage2, spot + 3, (head, place(which, 0, -1)))
            share(which, (along, 1))
        if along == 0:
            make_query(blocks - 1)
    for along in (0, -1, 1, 2):
        spot = (along % SIDE) * 4
        for which in (0, 1):
            landing(which, (along, 2), first, stage2, spot + 2).wait_recv()
            landing(which, (along, 2), second, stage2, spot + 3).wait_recv()
            share(which, (along, 2))
    for which in (0, 1):
        for along in range(SIDE):
            for across in range(SIDE):
                if (along, across) != (0, 0):
                    block = 2 * (1 - core) + which
                    spot = along * 4 + across
                    landing(which, (along, across), everything, stage3, spot, block).wait_recv()
    loads[2].wait()
    for k in range(neg_ids.shape[0]):
        neg_t[:, k * span : (k + 1) * span] = table[neg_ids[k]]
    for b in range(blocks):
        chosen[b] = table[owners[b] * owned + locals_[b]]
    for n, (value, target) in enumerate(((neg_t, neg_out), (chosen, chosen_out))):
        store = pltpu.make_async_copy(value, target, local.at[5 + 2 * blocks + n])
        store.start()
        stores.append(store)
    for store in stores:
        store.wait()
    for transfer in sent:
        transfer.wait_send()


def gather_table(owners, locals_, neg_ids, tail_t, head_t, rel_t, head_rows, relations):
    owned, _, span = tail_t.shape
    negs = neg_ids.shape[0]
    blocks, edges = head_rows.shape
    width = head_t.shape[0]
    sems = pltpu.SemaphoreType.DMA
    anywhere = pl.BlockSpec(memory_space=pl.ANY)
    return pl.pallas_call(
        table_gather,
        out_shape=(
            jax.ShapeDtypeStruct((blocks, width, edges), BF16),
            jax.ShapeDtypeStruct((blocks, width, edges), BF16),
            jax.ShapeDtypeStruct((blocks, width, span), BF16),
            jax.ShapeDtypeStruct((width, negs * span), BF16),
        ),
        in_specs=[pl.BlockSpec(memory_space=pltpu.SMEM)] * 3
        + [pl.BlockSpec(memory_space=pltpu.HBM)] * 5,
        out_specs=(anywhere, anywhere, anywhere, anywhere),
        scratch_shapes=[
            pltpu.VMEM((TAIL * owned, width, span), BF16),
            pltpu.VMEM((blocks, width, span), BF16),
            pltpu.VMEM((width, negs * span), BF16),
            pltpu.VMEM(head_t.shape, BF16),
            pltpu.VMEM(rel_t.shape, BF16),
            pltpu.VMEM(head_rows.shape, jnp.int32),
            pltpu.VMEM(relations.shape, jnp.int32),
            pltpu.VMEM((blocks, width, edges), BF16),
            pltpu.VMEM((blocks, width, edges), BF16),
            sems((2, 4)),
            sems((2, 4)),
            sems((2, 16)),
            sems((2, 16)),
            sems((2, 16)),
            sems((2, 16)),
            sems((7 + 2 * blocks,)),
        ],
        compiler_params=pltpu.CompilerParams(
            collective_id=0, has_side_effects=True, vmem_limit_bytes=VMEM_BYTES
        ),
    )(owners, locals_, neg_ids, tail_t, head_t, rel_t, head_rows, relations)


def remote(source, target, send_sem, recv_sem, device):
    return pltpu.make_async_remote_copy(
        src_ref=source,
        dst_ref=target,
        send_sem=send_sem,
        recv_sem=recv_sem,
        device_id=device,
        device_id_type=MESH,
    )


class PlaneSum:
    def __init__(self, spread, in_x, in_y, mid_x, mid_y, end_x, end_y, sems):
        self.refs = (spread, in_x, in_y, mid_x, mid_y, end_x, end_y)
        self.sems = sems
        self.head, tail = lax.axis_index("head"), lax.axis_index("tail")
        self.col, self.row = lax.rem(tail, SIDE), lax.div(tail, SIDE)

    def steps(self):
        for step in range(1, SIDE):
            col = lax.rem(self.col + step, SIDE)
            row = lax.rem(self.row + step, SIDE)
            yield step - 1, col, row, (self.head, self.row * SIDE + col), (
                self.head,
                row * SIDE + self.col,
            )

    def first(self):
        spread, in_x, in_y = self.refs[:3]
        send, recv = self.sems
        copies = []
        for n, col, row, over_x, over_y in self.steps():
            copies.append(
                remote(spread.at[:, col, pl.ds(0, 2)], in_x.at[n], send.at[n], recv.at[n], over_x)
            )
            copies.append(
                remote(
                    spread.at[row, :, pl.ds(2, 2)], in_y.at[n], send.at[3 + n], recv.at[3 + n], over_y
                )
            )
        return copies

    def second(self):
        mid_x, mid_y, end_x, end_y = self.refs[3:]
        send, recv = self.sems
        copies = []
        for n, col, row, over_x, over_y in self.steps():
            copies.append(remote(mid_x.at[row], end_x.at[n], send.at[6 + n], recv.at[6 + n], over_y))
            copies.append(remote(mid_y.at[col], end_y.at[n], send.at[9 + n], recv.at[9 + n], over_x))
        return copies

    def start_first(self):
        for copy in self.first():
            copy.start()

    def start_second(self):
        spread, in_x, in_y, mid_x, mid_y = self.refs[:5]
        for copy in self.first():
            copy.wait_recv()
        for place in range(SIDE):
            for part in range(2):
                total = spread[place, self.col, part]
                other = spread[self.row, place, 2 + part]
                for n in range(SIDE - 1):
                    total = total + in_x[n, place, part]
                    other = other + in_y[n, place, part]
                mid_x[place, part] = total
                mid_y[place, part] = other
        for copy in self.second():
            copy.start()

    def result(self):
        mid_x, mid_y, end_x, end_y = self.refs[3:]
        for copy in self.second():
            copy.wait_recv()
        parts = []
        for part in range(2):
            total = mid_x[self.row, part]
            for n in range(SIDE - 1):
                total = total + end_x[n, part]
            parts.append(total)
        for part in range(2):
            total = mid_y[self.col, part]
            for n in range(SIDE - 1):
                total = total + end_y[n, part]
            parts.append(total)
        return parts

    def finish(self):
        for copy in self.first() + self.second():
            copy.wait_send()


def exchange(
    owners,
    locals_,
    live_count,
    neg_ids,
    chosen_hbm,
    neg_hbm,
    query_hbm,
    rel_hbm,
    head_hbm,
    offsets,
    head_rows,
    head_state,
    own_t,
    own_state,
    out,
    head_new,
    state_new,
    chosen,
    neg_t,
    negs,
    query,
    rel_all,
    prob,
    grad,
    block_part,
    head_emb,
    head_grad,
    hot_head,
    neg_part,
    slots,
    theirs,
    mine,
    neg_in_x,
    neg_in_y,
    neg_mid_x,
    neg_mid_y,
    neg_end_x,
    neg_end_y,
    deep,
    deep_in,
    neg_total,
    slot_rows,
    seats,
    lo,
    lo_in_x,
    lo_in_y,
    lo_mid_x,
    lo_mid_y,
    lo_end_x,
    lo_end_y,
    hi,
    hi_in_x,
    hi_in_y,
    hi_mid_x,
    hi_mid_y,
    hi_end_x,
    hi_end_y,
    update,
    sem_bs,
    sem_br,
    sem_cs,
    sem_cr,
    sem_ps,
    sem_pr,
    sem_zs,
    sem_zr,
    sem_ls,
    sem_lr,
    sem_hs,
    sem_hr,
    sem_ns,
    sem_nr,
    sem_us,
    sem_ur,
    sem_fs,
    sem_fr,
    sem_local,
):
    head, tail = lax.axis_index("head"), lax.axis_index("tail")
    core, depth = lax.rem(head, 2), lax.div(head, 2)
    other = head + 1 - 2 * core
    owned, width, span = own_t.shape
    group = slots.shape[2]
    quarter = DEPTH // 2
    blocks, edges = offsets.shape
    half = width // 2

    def around(index, step, count):
        return lax.rem(index + step, count)

    loads = [
        pltpu.make_async_copy(neg_hbm, neg_t, sem_local.at[0]),
        pltpu.make_async_copy(query_hbm, query, sem_local.at[1]),
        pltpu.make_async_copy(chosen_hbm, chosen, sem_local.at[2]),
        pltpu.make_async_copy(rel_hbm, rel_all, sem_local.at[3]),
        pltpu.make_async_copy(head_hbm, head_emb, sem_local.at[4]),
    ]
    for load in loads:
        load.start()

    barrier = pltpu.get_barrier_semaphore()

    @pl.loop(1, HEAD)
    def _(step):
        pl.semaphore_signal(
            barrier, inc=1, device_id=(around(head, step, HEAD), tail), device_id_type=MESH
        )
        pl.semaphore_signal(
            barrier, inc=1, device_id=(head, around(tail, step, TAIL)), device_id_type=MESH
        )

    loads[0].wait()
    for k in range(negs.shape[0] // span):
        negs[k * span : (k + 1) * span, :] = neg_t[:, k * span : (k + 1) * span].T
    for load in loads[1:]:
        load.wait()

    def edge_block(b):
        live = jnp.where(b < live_count[0], 1.0, 0.0).astype(F32)
        pick = one_hot(span, offsets[pl.ds(b, 1), :])
        tail_vec = mm(chosen[b], pick)
        queries = query[b].astype(F32)
        positive = jnp.sum(queries * tail_vec, axis=0, keepdims=True)
        score = mm(negs[...], query[b])
        largest = jnp.maximum(positive, jnp.max(score, axis=0, keepdims=True))
        pos_exp = jnp.exp(positive - largest)
        neg_exp = jnp.exp(score - largest)
        denominator = pos_exp + jnp.sum(neg_exp, axis=0, keepdims=True)
        pos_grad = (pos_exp / denominator - 1.0) * live
        part = pos_grad * queries
        part_a = part.astype(BF16)
        rest = part - part_a.astype(F32)
        part_b = rest.astype(BF16)
        part_c = (rest - part_b.astype(F32)).astype(BF16)
        block_grad = mm(pick, part_a, NT) + (mm(pick, part_b, NT) + mm(pick, part_c, NT))
        number = (owners[b] * owned + locals_[b]).astype(F32)
        for i in range(HEAD):
            block_part[i, b, :, :width] = block_grad[i * group : (i + 1) * group].astype(BF16)
            block_part[i, b, :, width:] = jnp.full((group, LANES - width), number, BF16)
        prob[b] = (neg_exp * (live / denominator)).astype(BF16)
        query_grad = pos_grad * tail_vec + mm(neg_t[...], prob[b])
        rel = rel_all[b].astype(F32)
        rr, ri = rel[:half], rel[half:]
        qr, qi = query_grad[:half], query_grad[half:]
        for start, change in ((0, qr * rr + qi * ri), (half, qi * rr - qr * ri)):
            change_hi = change.astype(BF16)
            grad[b, 0, start : start + half, :] = change_hi
            grad[b, 1, start : start + half, :] = (change - change_hi.astype(F32)).astype(BF16)

    early = blocks // 2
    pieces = (
        *((pl.ds(b, 1), pl.ds(0, LANES)) for b in range(early)),
        (pl.ds(early, blocks - early), pl.ds(CUT, LANES - CUT)),
        (pl.ds(early, blocks - early), pl.ds(0, CUT)),
    )

    def block_copy(piece, step):
        which, lanes = pieces[piece]
        peer = around(head, step, HEAD)
        return remote(
            block_part.at[peer, which, :, lanes],
            slots.at[head, which, :, lanes],
            sem_bs.at[piece, step],
            sem_br.at[piece, step],
            (peer, tail),
        )

    for b in range(early):
        edge_block(b)
        if b == 0:
            pl.semaphore_wait(barrier, HEAD + TAIL - 2)

        @pl.loop(1, HEAD)
        def _(step):
            block_copy(b, step).start()

    @pl.loop(early, blocks)
    def _(b):
        edge_block(b)

    for piece in range(early, len(pieces)):

        @pl.loop(1, HEAD)
        def _(step):
            block_copy(piece, step).start()

    keep_block = pltpu.make_async_copy(block_part.at[head], slots.at[head], sem_local.at[5])
    keep_block.start()

    def pair_copy(part):
        return remote(
            neg_part.at[part, :, :, 1 - core],
            theirs.at[part],
            sem_cs.at[part],
            sem_cr.at[part],
            (other, tail),
        )

    chunk = prob.shape[1] // SIDE

    @pl.loop(0, SIDE)
    def _(part):
        spots = pl.ds(pl.multiple_of(part * chunk, chunk), chunk)
        total = mm(prob[0, spots, :], query[0], NT)
        for b in range(1, blocks):
            total = total + mm(prob[b, spots, :], query[b], NT)
        neg_part[part] = total.reshape(neg_part.shape[1:])
        pair_copy(part).start()

    for part in range(SIDE):
        pair_copy(part).wait_recv()
        for place in range(SIDE):
            total = neg_part[part, place, :, core] + theirs[part, place]
            mine[part, place] = total
    plane = PlaneSum(
        mine, neg_in_x, neg_in_y, neg_mid_x, neg_mid_y, neg_end_x, neg_end_y, (sem_ps, sem_pr)
    )
    plane.start_first()

    rows = hot_head.shape[0]
    piece_rows = 160
    for b in range(blocks):
        hot_head[:, b * edges : (b + 1) * edges] = one_hot(rows, head_rows[b : b + 1, :])

    def head_piece(p, squares):
        spots = pl.ds(pl.multiple_of(p * piece_rows, piece_rows), piece_rows)
        gradient = jnp.zeros((piece_rows, rows), F32)
        for b in range(blocks):
            lanes = slice(b * edges, (b + 1) * edges)
            for n in range(2):
                gradient = gradient + mm(grad[b, n, spots, :], hot_head[:, lanes], NT)
        head_grad[spots, :] = gradient
        return squares + jnp.sum(gradient * gradient, axis=0, keepdims=True)

    squares = lax.fori_loop(0, width // piece_rows, head_piece, jnp.zeros((1, rows), F32))

    def spread_rows(piece):
        which, lanes = pieces[piece]

        @pl.loop(0, HEAD)
        def _(source):
            for b in range(which.start, which.start + which.size):
                spot = pl.multiple_of((source * owned + b) * group, group)
                slot_rows[pl.ds(spot, group), lanes] = slots[source, b, :, lanes].astype(F32)

    def arrive(piece):
        @pl.loop(1, HEAD)
        def _(step):
            block_copy(piece, step).wait_recv()

        if piece == 0:
            keep_block.wait()
        spread_rows(piece)

    def fill(dense, sums):
        for block in range(TAIL * owned):
            y, x, part = block // owned // SIDE, block // owned % SIDE, block % owned
            dense[y, x, part] = sums[block * group : (block + 1) * group]

    for piece in range(len(pieces) - 1):
        arrive(piece)
    count = HEAD * owned * group
    number = slot_rows[:, width : width + 1]
    inner = lax.broadcasted_iota(jnp.int32, (count, 1), 0) % group
    goal = number * group + inner.astype(F32)
    places = lax.broadcasted_iota(jnp.int32, (count, count), 1).astype(F32)
    seats[...] = jnp.where(places == goal, 1.0, 0.0).astype(BF16).T
    fill(hi, mm(seats[...], slot_rows[:, CUT:width].astype(BF16)))
    high = PlaneSum(hi, hi_in_x, hi_in_y, hi_mid_x, hi_mid_y, hi_end_x, hi_end_y, (sem_hs, sem_hr))
    high.start_first()
    plane.start_second()
    arrive(len(pieces) - 1)
    fill(lo, mm(seats[...], slot_rows[:, :CUT].astype(BF16)))
    low = PlaneSum(lo, lo_in_x, lo_in_y, lo_mid_x, lo_mid_y, lo_end_x, lo_end_y, (sem_ls, sem_lr))
    low.start_first()

    for place, total in enumerate(plane.result()):
        deep[place] = total

    zone = lax.rem(tail, 2)
    takes = lax.div(depth, quarter) == zone
    mine_k = lax.div(tail, 2)

    def deep_copy(step):
        level = zone * quarter + step
        return remote(
            deep.at[step],
            deep_in.at[depth],
            sem_zs.at[step],
            sem_zr.at[depth],
            (level * 2 + core, tail),
        )

    def deep_landing(source):
        return remote(
            deep.at[0], deep_in.at[source], sem_zs.at[0], sem_zr.at[source], (other, tail)
        )

    def total_copy(step):
        return remote(
            neg_total.at[mine_k],
            neg_total.at[mine_k],
            sem_ns.at[step],
            sem_nr.at[mine_k],
            (head, around(tail, step, TAIL)),
        )

    def total_landing(k):
        return remote(neg_total.at[k], neg_total.at[k], sem_ns.at[1], sem_nr.at[k], (other, tail))

    @pl.loop(0, quarter)
    def _(step):
        @pl.when(zone * quarter + step != depth)
        def _():
            deep_copy(step).start()

    high.start_second()

    head_next = head_state[...] + squares / width
    state_new[...] = head_next
    rate = LEARN_RATE / jnp.sqrt(head_next)

    @pl.loop(0, width // piece_rows)
    def _(p):
        spots = pl.ds(pl.multiple_of(p * piece_rows, piece_rows), piece_rows)
        head_emb[spots, :] = (head_emb[spots, :].astype(F32) - head_grad[spots, :] * rate).astype(
            BF16
        )

    head_store = pltpu.make_async_copy(head_emb, head_new, sem_local.at[6])
    head_store.start()

    @pl.when(takes)
    def _():
        deep_in[depth] = deep[depth - zone * quarter]

        @pl.loop(0, DEPTH)
        def _(source):
            @pl.when(source != depth)
            def _():
                deep_landing(source).wait_recv()

        total = deep_in[0]
        for source in range(1, DEPTH):
            total = total + deep_in[source]
        neg_total[mine_k] = total

        @pl.loop(1, TAIL)
        def _(step):
            total_copy(step).start()

    lane = lax.broadcasted_iota(jnp.int32, (group, span), 1)
    mark = lane == head * group + lax.broadcasted_iota(jnp.int32, (group, span), 0)
    rows_now = [mm(jnp.where(mark, 1.0, 0.0).astype(BF16), own_t[b], NT) for b in range(owned)]
    states_now = [
        jnp.sum(jnp.where(mark, own_state[b : b + 1, :], 0.0), axis=1, keepdims=True)
        for b in range(owned)
    ]

    low.start_second()
    high_sums, low_sums = high.result(), low.result()

    @pl.loop(0, neg_total.shape[0])
    def _(k):
        @pl.when(2 * k + lax.div(depth, quarter) != tail)
        def _():
            total_landing(k).wait_recv()

    for b in range(owned):
        low_part, high_part = low_sums[b], high_sums[b]
        for k in range(neg_total.shape[0]):
            weight = jnp.where(neg_ids[k] == tail * owned + b, 1.0, 0.0).astype(F32)
            low_part = low_part + weight * neg_total[k, :, :CUT]
            high_part = high_part + weight * neg_total[k, :, CUT:]
        squares = jnp.sum(low_part * low_part, axis=1, keepdims=True) + jnp.sum(
            high_part * high_part, axis=1, keepdims=True
        )
        fresh = states_now[b] + squares / width
        rate = LEARN_RATE / jnp.sqrt(fresh)
        update[b, :, :CUT] = (rows_now[b][:, :CUT] - low_part * rate).astype(BF16)
        update[b, :, CUT:width] = (rows_now[b][:, CUT:] - high_part * rate).astype(BF16)
        spot = lax.broadcasted_iota(jnp.int32, (group, LANES - width), 1)
        fresh_a = fresh.astype(BF16).astype(F32)
        fresh_b = (fresh - fresh_a).astype(BF16).astype(F32)
        fresh_c = fresh - fresh_a - fresh_b
        parts = jnp.where(spot == 0, fresh_a, jnp.where(spot == 1, fresh_b, fresh_c))
        update[b, :, width:] = parts.astype(BF16)

    def rows_copy(step):
        peer = around(depth, step, DEPTH) * 2 + core
        return remote(update, out.at[:, head], sem_us.at[step], sem_ur.at[step], (peer, tail))

    @pl.loop(1, DEPTH)
    def _(step):
        rows_copy(step).start()

    out_own = pltpu.make_async_copy(update, out.at[:, head], sem_local.at[7])
    out_own.start()
    first_rows = remote(update, out.at[:, head], sem_fs.at[0], sem_fr.at[0], (other, tail))
    first_rows.start()

    def pass_rows(step):
        place = around(depth, DEPTH - step, DEPTH) * 2 + core
        return remote(
            out.at[:, place], out.at[:, place], sem_fs.at[step], sem_fr.at[step], (other, tail)
        )

    plane.finish()
    high.finish()
    low.finish()
    for part in range(SIDE):
        pair_copy(part).wait_send()

    for piece in range(len(pieces)):

        @pl.loop(1, HEAD)
        def _(step):
            block_copy(piece, step).wait_send()

    @pl.loop(0, quarter)
    def _(step):
        @pl.when(zone * quarter + step != depth)
        def _():
            deep_copy(step).wait_send()

    @pl.when(takes)
    def _():
        @pl.loop(1, TAIL)
        def _(step):
            total_copy(step).wait_send()

    head_store.wait()

    @pl.loop(1, DEPTH)
    def _(step):
        rows_copy(step).wait_recv()
        pass_rows(step).start()

    out_own.wait()
    first_rows.wait()

    @pl.loop(1, DEPTH)
    def _(step):
        pass_rows(step).wait()
        rows_copy(step).wait_send()


def run_exchange(
    owners,
    locals_,
    live_count,
    neg_ids,
    chosen,
    neg_t,
    query,
    rel_vec,
    head_t,
    offsets,
    head_rows,
    head_state,
    own_t,
    own_state,
):
    owned, width, span = own_t.shape
    blocks, edges = offsets.shape
    rows = head_t.shape[1]
    group = span // HEAD
    negs = neg_ids.shape[0]
    quarter = DEPTH // 2
    count = HEAD * owned * group
    sems = pltpu.SemaphoreType.DMA
    smem = pl.BlockSpec(memory_space=pltpu.SMEM)
    anywhere = pl.BlockSpec(memory_space=pl.ANY)
    vmem = pl.BlockSpec(memory_space=pltpu.VMEM)

    def plane_sum(columns):
        return [
            pltpu.VMEM((SIDE, SIDE, 4, group, columns), F32),
            *([pltpu.VMEM((SIDE - 1, SIDE, 2, group, columns), F32)] * 2),
            *([pltpu.VMEM((SIDE, 2, group, columns), F32)] * 2),
            *([pltpu.VMEM((SIDE - 1, 2, group, columns), F32)] * 2),
        ]

    return pl.pallas_call(
        exchange,
        out_shape=(
            jax.ShapeDtypeStruct((owned, HEAD, group, LANES), BF16),
            jax.ShapeDtypeStruct(head_t.shape, BF16),
            jax.ShapeDtypeStruct((1, rows), F32),
        ),
        in_specs=[smem] * 4 + [anywhere] * 5 + [vmem] * 5,
        out_specs=(anywhere, anywhere, vmem),
        scratch_shapes=[
            pltpu.VMEM(chosen.shape, BF16),
            pltpu.VMEM(neg_t.shape, BF16),
            pltpu.VMEM((negs * span, width), BF16),
            pltpu.VMEM(query.shape, BF16),
            pltpu.VMEM(rel_vec.shape, BF16),
            pltpu.VMEM((blocks, negs * span, edges), BF16),
            pltpu.VMEM((blocks, 2, width, edges), BF16),
            pltpu.VMEM((HEAD, blocks, group, LANES), BF16),
            pltpu.VMEM(head_t.shape, BF16),
            pltpu.VMEM(head_t.shape, F32),
            pltpu.VMEM((rows, blocks * edges), BF16),
            pltpu.VMEM((SIDE, SIDE, 4, 2, group, width), F32),
            pltpu.VMEM((HEAD, owned, group, LANES), BF16),
            pltpu.VMEM((SIDE, SIDE, 4, group, width), F32),
            *plane_sum(width),
            pltpu.VMEM((quarter, group, width), F32),
            pltpu.VMEM((DEPTH, group, width), F32),
            pltpu.VMEM((negs, group, width), F32),
            pltpu.VMEM((count, LANES), F32),
            pltpu.VMEM((count, count), BF16),
            *plane_sum(CUT),
            *plane_sum(width - CUT),
            pltpu.VMEM((owned, group, LANES), BF16),
            sems((blocks // 2 + 2, HEAD)),
            sems((blocks // 2 + 2, HEAD)),
            sems((SIDE,)),
            sems((SIDE,)),
            sems((12,)),
            sems((12,)),
            sems((quarter,)),
            sems((DEPTH,)),
            sems((12,)),
            sems((12,)),
            sems((12,)),
            sems((12,)),
            sems((TAIL,)),
            sems((negs,)),
            sems((DEPTH,)),
            sems((DEPTH,)),
            sems((DEPTH,)),
            sems((DEPTH,)),
            sems((8,)),
        ],
        compiler_params=pltpu.CompilerParams(
            collective_id=1, has_side_effects=True, vmem_limit_bytes=VMEM_BYTES
        ),
    )(
        owners,
        locals_,
        live_count,
        neg_ids,
        chosen,
        neg_t,
        query,
        rel_vec,
        head_t,
        offsets,
        head_rows,
        head_state,
        own_t,
        own_state,
    )


def per_device(
    head_emb,
    head_state,
    tail_emb,
    tail_state,
    relation_emb,
    head_rows,
    relations,
    tail_offsets,
    tail_owner,
    tail_local,
    block_count,
    neg_blocks,
):
    owned, span, width = tail_emb.shape
    head_t, tail_t = head_emb.T, tail_emb.transpose(0, 2, 1)
    owners = tail_owner.reshape(-1)
    query, rel_vec, chosen, neg_t = gather_table(
        owners, tail_local, neg_blocks, tail_t, head_t, relation_emb.T, head_rows, relations
    )
    fresh, head_new, head_state_new = run_exchange(
        owners,
        tail_local,
        block_count,
        neg_blocks,
        chosen,
        neg_t,
        query,
        rel_vec,
        head_t,
        tail_offsets,
        head_rows,
        head_state[None, :],
        tail_t,
        tail_state,
    )
    fresh = fresh.reshape(owned, span, LANES)
    pieces = fresh[:, :, width : width + 3].astype(F32)
    tail_state_new = (pieces[..., 0] + pieces[..., 1]) + pieces[..., 2]
    return (head_new.T, head_state_new[0], fresh[:, :, :width], tail_state_new)


def solution(mesh):
    placed = (
        P(("head", "tail"), None),
        P(("head", "tail")),
        P("tail", None, None),
        P("tail", None),
        P(),
        P(("head", "tail"), None),
        P(("head", "tail"), None),
        P(("head", "tail"), None),
        P(("head", "tail"), None),
        P(("head", "tail")),
        P(("head", "tail")),
        P(),
    )
    return jax.shard_map(
        per_device,
        mesh=mesh,
        in_specs=placed,
        out_specs=(
            P(("head", "tail"), None),
            P(("head", "tail")),
            P("tail", None, None),
            P("tail", None),
        ),
        check_vma=False,
    )
```
